128 devices in a mesh: dp: 4 (over z), expert: 32 (over x, y, core).
Axes of the slice: x: 4, y: 4, z: 4, core: 2. Of those that a mesh axis runs over, the one named last changes fastest.
Arguments:
- tokens: bfloat16 [16384, 2048], P(('dp', 'expert')), may hold values from -6 to 6
- routes: int32 [16384, 8], P(('dp', 'expert')), may hold values from 0 to 63, all different within a row; in each aligned block of 128 rows (0 to 127, 128 to 255, ...) at most 24 rows name the same one
- route_weights: float32 [16384, 8], P(('dp', 'expert')), may hold values from 0.05 to 0.3
- cotangent: bfloat16 [16384, 2048], P(('dp', 'expert')), may hold values from -6 to 6
- gate_proj: bfloat16 [64, 2048, 640], P('expert'), may hold values from -0.125 to 0.125
- up_proj: bfloat16 [64, 2048, 640], P('expert'), may hold values from -0.125 to 0.125
- down_proj: bfloat16 [64, 640, 2048], P('expert'), may hold values from -0.25 to 0.25
Outputs:
- layer_output: bfloat16 [16384, 2048], P(('dp', 'expert'))
- input_grad: bfloat16 [16384, 2048], P(('dp', 'expert'))
- route_weight_grad: float32 [16384, 8], P(('dp', 'expert'))
- gate_grad: float32 [2048, 64, 640], P('dp', 'expert')
- up_grad: float32 [2048, 64, 640], P('dp', 'expert')
- down_grad: float32 [2048, 64, 640], P('dp', 'expert')
The draws below stay inside these ranges and needn't reach their ends.
Inputs may be any that keep to these rules, and one draw needn't show every extreme that they name: `routes`: each row names 8 different experts. Among the 128 rows of one device, no expert is named by more than 24 rows, a bound that some block reaches.
All inputs are finite; a program needn't handle non-finite values.
Results may differ from the reference program's by a relative error of at most 0.0095.
Values may be sent and summed in bfloat16 or wider, within the bound.
A program may use at most 192 MiB of HBM per device.

```python
import math
import jax
import jax.numpy as jnp
import numpy as np
from jax import lax

D = 2048
HID = 640
TOP = 8
TOK_DEV = 128
EXPERTS = 64
CAP = 24
TOKENS = 16384
N_DP = 4
N_EXPERT = 32


def block_levels(key, dims, pieces, low, high):
    loudness, own = 1.0, jax.random.fold_in(key, 6)
    for dim, shards_of in pieces:
        steps = jnp.exp(jax.random.uniform(jax.random.fold_in(own, dim), (shards_of,), jnp.float32, low / len(pieces), high / len(pieces)))
        loudness = loudness * jnp.repeat(steps, dims[dim] // shards_of).reshape([-1 if axis == dim else 1 for axis in range(len(dims))])
    return loudness


def shared_out(own_key, own, number, rows, count, top, bound, lean):
    ranking = jax.random.permutation(own_key, count)
    crowded, common = load_shares(count, rows * top, bound, lean, True), load_shares(count, rows * top, bound, lean, False)
    places = jnp.arange(count)

    def named(sizes, rotation):
        used = int((sizes > 0).sum())
        fixed = max(1, used // 4)
        passed = fixed + (places - fixed + rotation * (used - fixed)) % max(1, count - fixed)
        return jnp.zeros((count,), jnp.int32).at[ranking[jnp.where(places < fixed, places, passed)]].set(jnp.asarray(sizes, jnp.int32))

    sizes = jnp.where(number % 4 == 0, named(crowded, number // 4), named(common, number - number // 4 - 1))
    mixed = jax.random.permutation(jax.random.fold_in(own, 3), count)
    giver, sink = mixed[0:count // 2 * 2:2], mixed[1:count // 2 * 2:2]
    room = jnp.minimum(sizes[giver] - 1, bound - sizes[sink]) // 2
    room = jnp.where((giver == ranking[0]) | (sink == ranking[0]) | (sizes[sink] == 0), 0, jnp.maximum(room, 0))
    passed = jax.random.randint(jax.random.fold_in(own, 4), (count // 2,), 0, 1 << 20) % (room + 1)
    sizes = sizes.at[giver].add(-passed).at[sink].add(passed)
    labels = jnp.searchsorted(jnp.cumsum(sizes), jnp.arange(rows * top), side="right").astype(jnp.int32)
    grid = labels.reshape(top, rows).T
    grid = grid[jax.random.permutation(jax.random.fold_in(own, 1), rows)]
    rotation = jax.random.randint(jax.random.fold_in(own, 2), (rows, 1), 0, top)
    return jnp.take_along_axis(grid, (jnp.arange(top)[None, :] + rotation) % top, axis=1)


def load_shares(count, total, limit, lean, full):
    loads = [(1 << 20) // math.isqrt(grade ** lean) + 1 for grade in range(1, count + 1)]
    largest = limit if full else min(limit, max(-(-total // count), total * loads[0] // sum(loads)))
    least = 1 if total - largest >= count - 1 else 0
    given, surplus = [largest] + [least] * (count - 1), total - largest - least * (count - 1)
    while surplus > 0:
        free = [i for i in range(1, count) if given[i] < largest] or [i for i in range(1, count) if given[i] < limit]
        pool, budget = sum([loads[i] for i in free]), surplus
        for i in free:
            extra = min(limit - given[i], max(1, budget * loads[i] // pool), surplus)
            given[i] = given[i] + extra
            surplus = surplus - extra
    return np.array(given)


def gaussian(own_key, shape, scale, bound, split=(), kind=jnp.bfloat16):
    values = scale * jax.random.normal(own_key, shape, jnp.float32)
    if split:
        values = values * block_levels(own_key, shape, split, -0.22, 0.18)
    return jnp.clip(values, -bound, bound).astype(kind)


def setup_inputs(seed: int = 0) -> dict:
    splits = jax.random.split(jax.random.key(seed), 8)
    tokens = gaussian(splits[0], (TOKENS, D), 1.0, 6.0, ((0, 128),))
    routes_keys = jax.random.split(jax.random.fold_in(splits[1], 1), TOKENS // TOK_DEV)
    routes_turns = jax.random.permutation(jax.random.fold_in(splits[1], 3), TOKENS // TOK_DEV)
    routes = jax.vmap(lambda own, number: shared_out(jax.random.fold_in(splits[1], 2), own, number, TOK_DEV, EXPERTS, TOP, CAP, 2))(routes_keys, routes_turns).reshape((TOKENS, TOP))
    route_weights = jnp.clip(0.05 + 0.25 * jax.random.uniform(splits[2], (TOKENS, TOP), jnp.float32) ** block_levels(splits[2], (TOKENS, TOP), ((0, 128),), -0.2, 0.2), 0.05, 0.3)
    cotangent = gaussian(splits[3], (TOKENS, D), 1.0, 6.0, ((0, 128),))
    gate_proj = gaussian(splits[4], (EXPERTS, D, HID), D ** -0.5, 0.125, ((0, 32),))
    up_proj = gaussian(splits[5], (EXPERTS, D, HID), D ** -0.5, 0.125, ((0, 32),))
    down_proj = gaussian(splits[6], (EXPERTS, HID, D), HID ** -0.5, 0.25, ((0, 32),))
    return dict(tokens=tokens, routes=routes, route_weights=route_weights, cotangent=cotangent, gate_proj=gate_proj, up_proj=up_proj, down_proj=down_proj)


def swish_parts(gate_pre):
    sig_value = jax.nn.sigmoid(gate_pre)
    return gate_pre * sig_value, sig_value * (1.0 + gate_pre * (1.0 - sig_value))


def reference(tokens, routes, route_weights, cotangent, gate_proj, up_proj, down_proj):
    n_tokens = tokens.shape[0]
    n_routes = n_tokens * TOP
    row_count = N_DP * N_EXPERT * CAP
    flat_expert = routes.reshape(-1).astype(jnp.int32)
    sort_order = jnp.argsort(flat_expert, stable=True).astype(jnp.int32)
    sorted_expert = flat_expert[sort_order]
    counts = jnp.zeros((EXPERTS,), jnp.int32).at[flat_expert].add(1)
    starts = (jnp.cumsum(counts) - counts).astype(jnp.int32)
    position = (jnp.arange(n_routes, dtype=jnp.int32) - starts[sorted_expert]).astype(jnp.int32)
    row_table = jnp.full((EXPERTS, row_count), n_routes, jnp.int32).at[sorted_expert, position].set(sort_order)
    tok_pad = jnp.concatenate([tokens, jnp.zeros((1, D), tokens.dtype)], 0)
    cot_pad = jnp.concatenate([cotangent, jnp.zeros((1, D), cotangent.dtype)], 0)
    weight_pad = jnp.concatenate([route_weights.reshape(-1), jnp.zeros((1,), jnp.float32)], 0)

    def one_expert(state_now, per_expert):
        out_acc, grad_acc, weight_acc = state_now
        row_index, gate_mat, up_mat, down_mat = per_expert
        token_row = (row_index // TOP).astype(jnp.int32)
        rows_in = tok_pad[token_row]
        rows_cot = cot_pad[token_row]
        row_weight = weight_pad[row_index]
        gate_pre = jnp.dot(rows_in, gate_mat, preferred_element_type=jnp.float32)
        up_pre = jnp.dot(rows_in, up_mat, preferred_element_type=jnp.float32)
        swish, d_swish = swish_parts(gate_pre)
        hidden = (swish * up_pre).astype(jnp.bfloat16)
        route_out = jnp.dot(hidden, down_mat, preferred_element_type=jnp.float32).astype(jnp.bfloat16)
        out_acc = out_acc.at[token_row].add(row_weight[:, None] * route_out.astype(jnp.float32))
        weight_grad = jnp.sum(route_out.astype(jnp.float32) * rows_cot.astype(jnp.float32), axis=1)
        weight_acc = weight_acc.at[row_index].set(weight_grad)
        route_cot = (row_weight[:, None] * rows_cot.astype(jnp.float32)).astype(jnp.bfloat16)
        d_hidden = jnp.dot(route_cot, down_mat.T, preferred_element_type=jnp.float32)
        d_gate = (d_hidden * up_pre * d_swish).astype(jnp.bfloat16)
        d_up = (d_hidden * swish).astype(jnp.bfloat16)
        route_dx = (jnp.dot(d_gate, gate_mat.T, preferred_element_type=jnp.float32)
                    + jnp.dot(d_up, up_mat.T, preferred_element_type=jnp.float32)).astype(jnp.bfloat16)
        grad_acc = grad_acc.at[token_row].add(route_dx.astype(jnp.float32))
        gate_g = jnp.dot(rows_in.T, d_gate, preferred_element_type=jnp.float32)
        up_g = jnp.dot(rows_in.T, d_up, preferred_element_type=jnp.float32)
        down_g = jnp.dot(route_cot.T, hidden, preferred_element_type=jnp.float32)
        return (out_acc, grad_acc, weight_acc), (gate_g, up_g, down_g)

    start_state = (jnp.zeros((n_tokens + 1, D), jnp.float32), jnp.zeros((n_tokens + 1, D), jnp.float32),
                   jnp.zeros((n_routes + 1,), jnp.float32))
    final_state, grads = lax.scan(one_expert, start_state, (row_table, gate_proj, up_proj, down_proj))
    out_acc, grad_acc, weight_acc = final_state
    layer_output = out_acc[:n_tokens].astype(jnp.bfloat16)
    input_grad = grad_acc[:n_tokens].astype(jnp.bfloat16)
    route_weight_grad = weight_acc[:n_routes].reshape(n_tokens, TOP)
    gate_grad = jnp.transpose(grads[0], (1, 0, 2))
    up_grad = jnp.transpose(grads[1], (1, 0, 2))
    down_grad = jnp.transpose(grads[2], (1, 0, 2))
    return (layer_output, input_grad, route_weight_grad, gate_grad, up_grad, down_grad)
```

```python
import jax
import jax.numpy as jnp
from jax import lax
from jax.experimental import pallas as pl
from jax.experimental.pallas import tpu as pltpu
from jax.sharding import PartitionSpec as P

MESH = pl.DeviceIdType.MESH
BF = jnp.bfloat16
F32 = jnp.float32
SIDE = 4
TOK = 128
HALF = 64
SUB = 32
CAP = 24
META = 128


def _place():
    me = lax.axis_index("expert")
    return lax.axis_index("dp"), me // 8, (me // 2) % 4, me % 2


def _at(x, y, c):
    return ((x + 8) % 4) * 8 + ((y + 8) % 4) * 2 + c


def _greet(peers):
    barrier = pltpu.get_barrier_semaphore()
    for peer in peers:
        pl.semaphore_signal(barrier, inc=1, device_id=peer, device_id_type=MESH)
    pl.semaphore_wait(barrier, len(peers))


def _shift(h, x, y, o1, o2, c):
    return _at(x + o1, y + o2, c) if h == 0 else _at(x + o2, y + o1, c)


def _gather_kernel(blk, out, ssem, rsem, lsem):
    z, x, y, c = _place()
    sib = _at(x, y, 1 - c)
    _greet(
        [(z, _at(x + 1, y, c)), (z, _at(x - 1, y, c)), (z, _at(x, y + 1, c)), (z, _at(x, y - 1, c)), (z, sib)]
    )
    mine = _at(x, y, c)
    own = pltpu.make_async_copy(blk, out.at[mine], lsem)
    own.start()
    sends, keys = [], {}

    def key(*k):
        return keys.setdefault(k, len(keys))

    def send(slot, row, n, to, k):
        src = blk.at[pl.ds(row, n)] if slot is None else out.at[slot, pl.ds(row, n)]
        cp = pltpu.make_async_remote_copy(
            src_ref=src,
            dst_ref=out.at[mine if slot is None else slot, pl.ds(row, n)],
            send_sem=ssem.at[len(sends)],
            recv_sem=rsem.at[k],
            device_id=(z, to),
            device_id_type=MESH,
        )
        cp.start()
        sends.append(cp)

    def landed(slot, row, n, k):
        view = out.at[slot, pl.ds(row, n)]
        pltpu.make_async_remote_copy(
            src_ref=view,
            dst_ref=view,
            send_sem=ssem.at[0],
            recv_sem=rsem.at[k],
            device_id=(z, sib),
            device_id_type=MESH,
        ).wait_recv()

    def line(h, o1, slot):
        send(slot, h * HALF, HALF, _shift(h, x, y, 0, 1, c), key(h, "G+", o1))
        send(slot, h * HALF, HALF, _shift(h, x, y, 0, -1, c), key(h, "G-", o1))

    def aside(h, o1, o2, slot):
        send(slot, h * HALF, HALF, sib, key(h, "S", o1, o2))

    def start(h):
        send(None, h * HALF, HALF, _shift(h, x, y, 1, 0, c), key(h, "F+"))
        send(None, h * HALF, HALF, _shift(h, x, y, -1, 0, c), key(h, "F-"))
        line(h, 0, None)
        aside(h, 0, 0, None)

    def first(h, up):
        o = -1 if up else 1
        slot = _shift(h, x, y, o, 0, c)
        landed(slot, h * HALF, HALF, key(h, "F+" if up else "F-"))
        row = h * HALF + (0 if up else SUB)
        send(slot, row, SUB, _shift(h, x, y, 1 if up else -1, 0, c), key(h, "FF+" if up else "FF-"))
        line(h, o, slot)
        aside(h, o, 0, slot)

    def far(h):
        slot = _shift(h, x, y, 2, 0, c)
        landed(slot, h * HALF, SUB, key(h, "FF+"))
        landed(slot, h * HALF + SUB, SUB, key(h, "FF-"))
        line(h, 2, slot)
        aside(h, 2, 0, slot)

    def second(h, o1, up):
        o = -1 if up else 1
        slot = _shift(h, x, y, o1, o, c)
        landed(slot, h * HALF, HALF, key(h, "G+" if up else "G-", o1))
        row = h * HALF + (0 if up else SUB)
        send(slot, row, SUB, _shift(h, x, y, 0, 1 if up else -1, c), key(h, "GF+" if up else "GF-", o1))
        aside(h, o1, o, slot)

    def corner(h, o1):
        slot = _shift(h, x, y, o1, 2, c)
        landed(slot, h * HALF, SUB, key(h, "GF+", o1))
        landed(slot, h * HALF + SUB, SUB, key(h, "GF-", o1))
        aside(h, o1, 2, slot)

    both = (0, 1)
    for h in both:
        start(h)
    for up in (True, False):
        for h in both:
            first(h, up)
    for up in (True, False):
        for h in both:
            second(h, 0, up)
    for h in both:
        far(h)
    for o1 in (-1, 1):
        for up in (True, False):
            for h in both:
                second(h, o1, up)
    for h in both:
        corner(h, 0)
    for up in (True, False):
        for h in both:
            second(h, 2, up)
    for o1 in (-1, 1, 2):
        for h in both:
            corner(h, o1)
    for o2 in (0, -1, 1, 2):
        for o1 in (0, -1, 1, 2):
            for h in both:
                landed(_shift(h, x, y, o1, o2, 1 - c), h * HALF, HALF, key(h, "S", o1, o2))
    for cp in sends:
        cp.wait_send()
    own.wait()


def _gather(blk):
    width = blk.shape[1]
    return pl.pallas_call(
        _gather_kernel,
        out_shape=jax.ShapeDtypeStruct((32, TOK, width), BF),
        in_specs=[pl.BlockSpec(memory_space=pltpu.VMEM)],
        out_specs=pl.BlockSpec(memory_space=pl.ANY),
        scratch_shapes=[
            pltpu.SemaphoreType.DMA((72,)),
            pltpu.SemaphoreType.DMA((72,)),
            pltpu.SemaphoreType.DMA,
        ],
        compiler_params=pltpu.CompilerParams(collective_id=0, has_side_effects=True),
        name="plane_gather",
    )(blk)


def _add(dst, src, n):
    @pl.loop(0, n // 16)
    def _(i):
        rows = pl.ds(pl.multiple_of(i * 16, 16), 16)
        dst[rows, :] = (dst[rows, :].astype(F32) + src[rows, :].astype(F32)).astype(BF)


def _add3(dst, own, one, two, n):
    @pl.loop(0, n // 16)
    def _(i):
        rows = pl.ds(pl.multiple_of(i * 16, 16), 16)
        total = own[rows, :].astype(F32) + one[rows, :].astype(F32) + two[rows, :].astype(F32)
        dst[rows, :] = total.astype(dst.dtype)


def _reduce_kernel(
    part, gg, ug, dg, out, go, uo, do, aside,
    T, sb, ra, rb, r2a, r2b, za, zt, zf, zown, zout,
    ssem, rsem, tsem, bsem, zsem, osem, wsem,
):
    z, x, y, c = _place()
    sib = (z, _at(x, y, 1 - c))
    zup, zdn = ((z + 1) % 4, _at(x, y, c)), ((z + 3) % 4, _at(x, y, c))
    _greet(
        [(z, _at(x + 1, y, c)), (z, _at(x - 1, y, c)), (z, _at(x, y + 1, c)), (z, _at(x, y - 1, c)), sib, zup, zdn]
    )
    sends, keys = [], {}

    def remote(src, dst, to, *k):
        cp = pltpu.make_async_remote_copy(
            src_ref=src,
            dst_ref=dst,
            send_sem=ssem.at[len(sends)],
            recv_sem=rsem.at[keys.setdefault(k, len(keys))],
            device_id=to,
            device_id_type=MESH,
        )
        cp.start()
        sends.append(cp)

    def landed(dst, *k):
        pltpu.make_async_remote_copy(
            src_ref=dst,
            dst_ref=dst,
            send_sem=ssem.at[0],
            recv_sem=rsem.at[keys[k]],
            device_id=sib,
            device_id_type=MESH,
        ).wait_recv()

    lo, hi, full = pl.ds(0, SUB), pl.ds(SUB, SUB), pl.ds(0, HALF)
    both = (0, 1)
    obs, oas = (2, 1, 3, 0), (2, 1, 3, 0)
    order = [(h, ob, oa) for ob in obs for oa in oas for h in both]

    def ax(h, o):
        return (z, _shift(1 - h, x, y, o, 0, c))

    def bx(h, o):
        return (z, _shift(h, x, y, o, 0, c))

    def slot(h, ob, oa, core):
        return _shift(h, x, y, ob, oa, core)

    grads, couts = (gg, ug, dg), (go, uo, do)
    quads = [(k, e) for k in range(3) for e in range(2)]
    zl, zh = pl.ds(0, 256), pl.ds(256, 256)
    zp, zm, zq = (z + 1) % 4, (z + 3) % 4, (z + 2) % 4

    for q, (k, e) in enumerate(quads):
        remote(grads[k].at[e, zq, zl], za.at[q, 0], zup, "za", q, 0)
        remote(grads[k].at[e, zq, zh], za.at[q, 1], zdn, "za", q, 1)

    tcopies = {}
    for i, (h, ob, oa) in enumerate(order):
        rows = pl.ds(h * HALF, HALF)
        k = ob * 4 + oa
        remote(part.at[slot(h, ob, oa, 1 - c), rows], aside.at[h, k], sib, "s", h, ob, oa)
        cp = pltpu.make_async_copy(part.at[slot(h, ob, oa, c), rows], T.at[h, k], tsem.at[i])
        cp.start()
        tcopies[h, ob, oa] = cp
    zcopies = []
    for q, (k, e) in enumerate(quads):
        remote(grads[k].at[e, zp, zh], zf.at[q, 0, zh], zup, "zd", q, 0)
        remote(grads[k].at[e, zm, zl], zf.at[q, 1, zl], zdn, "zd", q, 1)
        pair = []
        for d, (where, rows) in enumerate(((zp, zl), (zm, zh))):
            cp = pltpu.make_async_copy(grads[k].at[e, where, rows], zt.at[q, d], zsem.at[q * 2 + d])
            cp.start()
            pair.append(cp)
        zcopies.append(pair)

    loads = {}

    def fetch(i):
        h, ob, oa = order[i]
        landed(aside.at[h, ob * 4 + oa], "s", h, ob, oa)
        cp = pltpu.make_async_copy(aside.at[h, ob * 4 + oa], sb.at[i % 3], bsem.at[i % 3])
        cp.start()
        loads[i] = cp

    def one(i):
        h, ob, oa = order[i]
        if i + 1 < len(order):
            fetch(i + 1)
        tcopies[h, ob, oa].wait()
        loads[i].wait()
        t = T.at[h, ob * 4 + oa]
        _add(t, sb.at[i % 3], HALF)
        if oa == 2:
            remote(t.at[lo], ra.at[h, ob, 0], ax(h, 1), "ra", h, ob, 0)
            remote(t.at[hi], ra.at[h, ob, 1], ax(h, -1), "ra", h, ob, 1)
        elif oa == 1:
            remote(t.at[hi], rb.at[h, ob, 0, hi], ax(h, 1), "rd", h, ob, 0)
        elif oa == 3:
            remote(t.at[lo], rb.at[h, ob, 1, lo], ax(h, -1), "rd", h, ob, 1)

    def stage1(j):
        for i in range(j * 8, j * 8 + 8):
            one(i)

    def stage2(j):
        ob = obs[j]
        for h in both:
            landed(ra.at[h, ob, 0], "ra", h, ob, 0)
            t = T.at[h, ob * 4 + 1]
            _add(t.at[lo], ra.at[h, ob, 0], SUB)
            remote(t.at[lo], rb.at[h, ob, 0, lo], ax(h, 1), "rs", h, ob, 0)
            landed(ra.at[h, ob, 1], "ra", h, ob, 1)
            t = T.at[h, ob * 4 + 3]
            _add(t.at[hi], ra.at[h, ob, 1], SUB)
            remote(t.at[hi], rb.at[h, ob, 1, hi], ax(h, -1), "rs", h, ob, 1)

    def stage3(j):
        ob = obs[j]
        for h in both:
            landed(rb.at[h, ob, 0, hi], "rd", h, ob, 0)
            landed(rb.at[h, ob, 1, lo], "rd", h, ob, 1)
            landed(rb.at[h, ob, 0, lo], "rs", h, ob, 0)
            landed(rb.at[h, ob, 1, hi], "rs", h, ob, 1)
            t = T.at[h, ob * 4]
            _add3(t, t, rb.at[h, ob, 0], rb.at[h, ob, 1], HALF)
            if ob == 2:
                remote(t.at[lo], r2a.at[h, 0], bx(h, 1), "2a", h, 0)
                remote(t.at[hi], r2a.at[h, 1], bx(h, -1), "2a", h, 1)
            elif ob == 1:
                remote(t.at[hi], r2b.at[h, 0, hi], bx(h, 1), "2d", h, 0)
            elif ob == 3:
                remote(t.at[lo], r2b.at[h, 1, lo], bx(h, -1), "2d", h, 1)

    def stage4():
        for h in both:
            landed(r2a.at[h, 0], "2a", h, 0)
            t = T.at[h, 4]
            _add(t.at[lo], r2a.at[h, 0], SUB)
            remote(t.at[lo], r2b.at[h, 0, lo], bx(h, 1), "2s", h, 0)
            landed(r2a.at[h, 1], "2a", h, 1)
            t = T.at[h, 12]
            _add(t.at[hi], r2a.at[h, 1], SUB)
            remote(t.at[hi], r2b.at[h, 1, hi], bx(h, -1), "2s", h, 1)

    def stage5():
        for h in both:
            landed(r2b.at[h, 0, hi], "2d", h, 0)
            landed(r2b.at[h, 1, lo], "2d", h, 1)
            landed(r2b.at[h, 0, lo], "2s", h, 0)
            landed(r2b.at[h, 1, hi], "2s", h, 1)
            _add3(out.at[pl.ds(h * HALF, HALF)], T.at[h, 0], r2b.at[h, 0], r2b.at[h, 1], HALF)

    def zmid(q):
        for d, (rows, to) in enumerate(((zl, zup), (zh, zdn))):
            landed(za.at[q, d], "za", q, d)
            zcopies[q][d].wait()
            _add(zt.at[q, d], za.at[q, d], 256)
            remote(zt.at[q, d], zf.at[q, d, rows], to, "zs", q, d)

    owns, writes = {}, {}

    def zload(q):
        k, e = quads[q]
        cp = pltpu.make_async_copy(grads[k].at[e, z], zown.at[q % 2], osem.at[q % 2])
        cp.start()
        owns[q] = cp

    def zend(q):
        k, e = quads[q]
        landed(zf.at[q, 0, zh], "zd", q, 0)
        landed(zf.at[q, 1, zl], "zd", q, 1)
        landed(zf.at[q, 0, zl], "zs", q, 0)
        landed(zf.at[q, 1, zh], "zs", q, 1)
        owns[q].wait()
        if q >= 2:
            writes[q - 2].wait()
        _add3(zout.at[q % 2], zown.at[q % 2], zf.at[q, 0], zf.at[q, 1], 512)
        cp = pltpu.make_async_copy(zout.at[q % 2], couts[k].at[e], wsem.at[q % 2])
        cp.start()
        writes[q] = cp
        if q + 2 < 6:
            zload(q + 2)

    zload(0)
    zload(1)
    fetch(0)
    stage1(0)
    stage1(1)
    stage2(0)
    zmid(0)
    stage1(2)
    stage2(1)
    stage3(0)
    zmid(1)
    stage1(3)
    stage2(2)
    stage3(1)
    zmid(2)
    stage2(3)
    stage3(2)
    stage4()
    zmid(3)
    stage3(3)
    zmid(4)
    stage5()
    zmid(5)
    for q in range(6):
        zend(q)
    writes[4].wait()
    writes[5].wait()
    for cp in sends:
        cp.wait_send()


def _reduce(part, gg, ug, dg):
    width = part.shape[2]
    hid = gg.shape[-1]
    grad = jax.ShapeDtypeStruct((2, 512, hid), F32)
    hbm = pl.BlockSpec(memory_space=pl.ANY)
    return pl.pallas_call(
        _reduce_kernel,
        out_shape=(
            jax.ShapeDtypeStruct((TOK, width), BF),
            grad,
            grad,
            grad,
            jax.ShapeDtypeStruct((2, 16, HALF, width), BF),
        ),
        in_specs=[hbm] * 4,
        out_specs=(pl.BlockSpec(memory_space=pltpu.VMEM), hbm, hbm, hbm, hbm),
        scratch_shapes=[
            pltpu.VMEM((2, 16, HALF, width), BF),
            pltpu.VMEM((3, HALF, width), BF),
            pltpu.VMEM((2, 4, 2, SUB, width), BF),
            pltpu.VMEM((2, 4, 2, HALF, width), BF),
            pltpu.VMEM((2, 2, SUB, width), BF),
            pltpu.VMEM((2, 2, HALF, width), BF),
            pltpu.VMEM((6, 2, 256, hid), BF),
            pltpu.VMEM((6, 2, 256, hid), BF),
            pltpu.VMEM((6, 2, 512, hid), BF),
            pltpu.VMEM((2, 512, hid), BF),
            pltpu.VMEM((2, 512, hid), F32),
            pltpu.SemaphoreType.DMA((128,)),
            pltpu.SemaphoreType.DMA((128,)),
            pltpu.SemaphoreType.DMA((32,)),
            pltpu.SemaphoreType.DMA((3,)),
            pltpu.SemaphoreType.DMA((12,)),
            pltpu.SemaphoreType.DMA((2,)),
            pltpu.SemaphoreType.DMA((2,)),
        ],
        compiler_params=pltpu.CompilerParams(
            collective_id=1, has_side_effects=True, vmem_limit_bytes=63 * 1024 * 1024
        ),
        name="plane_and_z_reduce",
    )(part, gg, ug, dg)


def _pick_kernel(all_ref, s_ref, w_ref, x_ref, c_ref):
    width = x_ref.shape[-1]
    pick = s_ref[0]
    xs = jnp.dot(pick, all_ref[0, :, :width], preferred_element_type=F32).astype(BF)
    cs = jnp.dot(pick, all_ref[0, :, width : 2 * width], preferred_element_type=F32)
    cs = (cs * w_ref[0]).astype(BF)
    for e in range(2):
        x_ref[e, 0] = xs[e * CAP : (e + 1) * CAP]
        c_ref[e, 0] = cs[e * CAP : (e + 1) * CAP]


def _pick(everything, sel, wrow, width):
    rows = jax.ShapeDtypeStruct((2, 32, CAP, width), BF)
    spec = pl.BlockSpec((2, 1, CAP, width), lambda s: (0, s, 0, 0))
    return pl.pallas_call(
        _pick_kernel,
        grid=(32,),
        out_shape=(rows, rows),
        in_specs=[
            pl.BlockSpec((1,) + everything.shape[1:], lambda s: (s, 0, 0)),
            pl.BlockSpec((1, 2 * CAP, TOK), lambda s: (s, 0, 0)),
            pl.BlockSpec((1, 2 * CAP, 1), lambda s: (s, 0, 0)),
        ],
        out_specs=(spec, spec),
        name="pick_rows",
    )(everything, sel, wrow)


def _spread_kernel(s_ref, y_ref, d_ref, r_ref, out_ref):
    width = y_ref.shape[-1]
    sel = s_ref[0]
    dims = (((0,), (0,)), ((), ()))

    def put(rows, at, n):
        out_ref[0, :, at : at + n] = lax.dot_general(sel, rows, dims, preferred_element_type=F32).astype(BF)

    put(jnp.concatenate([y_ref[0, 0], y_ref[1, 0]], 0), 0, width)
    put(jnp.concatenate([d_ref[0, 0], d_ref[1, 0]], 0), width, width)
    put(r_ref[0], 2 * width, META)


def _spread(sel, yrows, dxrows, rrows):
    width = yrows.shape[-1]
    spec = pl.BlockSpec((2, 1, CAP, width), lambda s: (0, s, 0, 0))
    full = 2 * width + META
    return pl.pallas_call(
        _spread_kernel,
        grid=(32,),
        out_shape=jax.ShapeDtypeStruct((32, TOK, full), BF),
        in_specs=[
            pl.BlockSpec((1, 2 * CAP, TOK), lambda s: (s, 0, 0)),
            spec,
            spec,
            pl.BlockSpec((1, 2 * CAP, META), lambda s: (s, 0, 0)),
        ],
        out_specs=pl.BlockSpec((1, TOK, full), lambda s: (s, 0, 0)),
        name="spread_rows",
    )(sel, yrows, dxrows, rrows)


def _bits(v):
    return lax.reduce_precision(v, 8, 7)


def on_device(tokens, routes, route_weights, cotangent, gate_proj, up_proj, down_proj):
    width = tokens.shape[1]
    hid = gate_proj.shape[2]
    me = lax.axis_index("expert")
    w_hi = _bits(route_weights)
    w_mid = _bits(route_weights - w_hi)
    w_lo = route_weights - w_hi - w_mid
    meta = jnp.concatenate(
        [routes.astype(F32), w_hi, w_mid, w_lo, jnp.zeros((TOK, META - 32), F32)], 1
    ).astype(BF)
    everything = _gather(jnp.concatenate([tokens, cotangent, meta], 1))

    meta_all = everything[:, :, 2 * width :].astype(F32)
    named = meta_all[:, :, 0:8].astype(jnp.int32)
    weights = meta_all[:, :, 8:16] + meta_all[:, :, 16:24] + meta_all[:, :, 24:32]
    mine = 2 * me + jnp.arange(2, dtype=jnp.int32)
    match = named[:, None, :, :] == mine[None, :, None, None]
    hit = jnp.any(match, axis=3)
    wtok = jnp.sum(jnp.where(match, weights[:, None], 0.0), axis=3)
    tri = (jnp.arange(TOK)[:, None] < jnp.arange(TOK)[None, :]).astype(BF)
    place = jnp.dot(hit.reshape(64, TOK).astype(BF), tri, preferred_element_type=F32)
    place = place.reshape(32, 2, 1, TOK).astype(jnp.int32)
    chosen = hit[:, :, None, :] & (place == jnp.arange(CAP, dtype=jnp.int32)[None, None, :, None])
    sel = chosen.astype(BF).reshape(32, 2 * CAP, TOK)
    wrow = jnp.sum(jnp.where(chosen, wtok[:, :, None, :], 0.0), axis=3)

    xr, cr = _pick(everything, sel, wrow.reshape(32, 2 * CAP, 1), width)
    xr = xr.reshape(2, 32 * CAP, width)
    cr = cr.reshape(2, 32 * CAP, width)
    we = jnp.transpose(wrow, (1, 0, 2)).reshape(2, 32 * CAP, 1)

    gate_pre = jnp.einsum("erd,edh->erh", xr, gate_proj, preferred_element_type=F32)
    up_pre = jnp.einsum("erd,edh->erh", xr, up_proj, preferred_element_type=F32)
    sig = jax.nn.sigmoid(gate_pre)
    swish = gate_pre * sig
    d_swish = sig * (1.0 + gate_pre * (1.0 - sig))
    hidden = (swish * up_pre).astype(BF)
    d_hidden = jnp.einsum("erd,ehd->erh", cr, down_proj, preferred_element_type=F32)
    d_gate = (d_hidden * up_pre * d_swish).astype(BF)
    d_up = (d_hidden * swish).astype(BF)
    rw = jnp.sum(d_hidden * hidden.astype(F32), axis=2, keepdims=True) / jnp.where(we > 0, we, 1.0)

    def grad(rows, cots):
        g = jnp.einsum("erd,erh->edh", rows, cots, preferred_element_type=F32).astype(BF)
        return g.reshape(2, 4, width // 4, hid)

    gg, ug, dg = grad(xr, d_gate), grad(xr, d_up), grad(cr, hidden)
    yrows = (jnp.einsum("erh,ehd->erd", hidden, down_proj, preferred_element_type=F32) * we).astype(BF)
    dxrows = (
        jnp.einsum("erh,edh->erd", d_gate, gate_proj, preferred_element_type=F32)
        + jnp.einsum("erh,edh->erd", d_up, up_proj, preferred_element_type=F32)
    ).astype(BF)
    lane = jnp.arange(META, dtype=jnp.int32)
    r_hi = _bits(rw)
    r_lo = rw - r_hi
    spot = lane[None, None, :] - mine[:, None, None]
    rrows = jnp.where(spot == 0, r_hi, 0.0) + jnp.where(spot == 64, r_lo, 0.0)
    rrows = rrows.reshape(2, 32, CAP, META).transpose(1, 0, 2, 3).reshape(32, 2 * CAP, META).astype(BF)

    part = _spread(
        sel, yrows.reshape(2, 32, CAP, width), dxrows.reshape(2, 32, CAP, width), rrows
    )
    out, go, uo, do, _ = _reduce(part, gg, ug, dg)
    table = out[:, 2 * width : 2 * width + 64].astype(F32) + out[:, 2 * width + 64 :].astype(F32)
    onehot = routes[:, :, None] == jnp.arange(64, dtype=jnp.int32)[None, None, :]
    weight_grad = jnp.sum(jnp.where(onehot, table[:, None, :], 0.0), axis=2)

    def final(g):
        return jnp.transpose(g, (1, 0, 2))

    return (out[:, :width], out[:, width : 2 * width], weight_grad, final(go), final(uo), final(do))


def solution(mesh):
    rows = P(("dp", "expert"), None)
    experts = P("expert", None, None)
    grads = P("dp", "expert", None)
    return jax.shard_map(
        on_device,
        mesh=mesh,
        in_specs=(rows, rows, rows, rows, experts, experts, experts),
        out_specs=(rows, rows, rows, grads, grads, grads),
        check_vma=False,
    )
```

```python
import jax
import jax.numpy as jnp
from jax import lax
from jax.experimental import pallas as pl
from jax.experimental.pallas import tpu as pltpu
from jax.sharding import PartitionSpec as P

MESH = pl.DeviceIdType.MESH
BF = jnp.bfloat16
F32 = jnp.float32
SIDE = 4
TOK = 128
HALF = 64
SUB = 32
CAP = 24
META = 128


def _place():
    me = lax.axis_index("expert")
    return lax.axis_index("dp"), me // 8, (me // 2) % 4, me % 2


def _at(x, y, c):
    return ((x + 8) % 4) * 8 + ((y + 8) % 4) * 2 + c


def _greet(peers):
    barrier = pltpu.get_barrier_semaphore()
    for peer in peers:
        pl.semaphore_signal(barrier, inc=1, device_id=peer, device_id_type=MESH)
    pl.semaphore_wait(barrier, len(peers))


def _shift(h, x, y, o1, o2, c):
    return _at(x + o1, y + o2, c) if h == 0 else _at(x + o2, y + o1, c)


def _gather_kernel(blk, out, ssem, rsem, lsem):
    z, x, y, c = _place()
    sib = _at(x, y, 1 - c)
    _greet(
        [(z, _at(x + 1, y, c)), (z, _at(x - 1, y, c)), (z, _at(x, y + 1, c)), (z, _at(x, y - 1, c)), (z, sib)]
    )
    mine = _at(x, y, c)
    own = pltpu.make_async_copy(blk, out.at[mine], lsem)
    own.start()
    sends, keys = [], {}

    def key(*k):
        return keys.setdefault(k, len(keys))

    def send(slot, row, n, to, k):
        src = blk.at[pl.ds(row, n)] if slot is None else out.at[slot, pl.ds(row, n)]
        cp = pltpu.make_async_remote_copy(
            src_ref=src,
            dst_ref=out.at[mine if slot is None else slot, pl.ds(row, n)],
            send_sem=ssem.at[len(sends)],
            recv_sem=rsem.at[k],
            device_id=(z, to),
            device_id_type=MESH,
        )
        cp.start()
        sends.append(cp)

    def landed(slot, row, n, k):
        view = out.at[slot, pl.ds(row, n)]
        pltpu.make_async_remote_copy(
            src_ref=view,
            dst_ref=view,
            send_sem=ssem.at[0],
            recv_sem=rsem.at[k],
            device_id=(z, sib),
            device_id_type=MESH,
        ).wait_recv()

    def line(h, o1, slot):
        send(slot, h * HALF, HALF, _shift(h, x, y, 0, 1, c), key(h, "G+", o1))
        send(slot, h * HALF, HALF, _shift(h, x, y, 0, -1, c), key(h, "G-", o1))

    def aside(h, o1, o2, slot):
        send(slot, h * HALF, HALF, sib, key(h, "S", o1, o2))

    def start(h):
        send(None, h * HALF, HALF, _shift(h, x, y, 1, 0, c), key(h, "F+"))
        send(None, h * HALF, HALF, _shift(h, x, y, -1, 0, c), key(h, "F-"))
        line(h, 0, None)
        aside(h, 0, 0, None)

    def first(h, up):
        o = -1 if up else 1
        slot = _shift(h, x, y, o, 0, c)
        landed(slot, h * HALF, HALF, key(h, "F+" if up else "F-"))
        row = h * HALF + (0 if up else SUB)
        send(slot, row, SUB, _shift(h, x, y, 1 if up else -1, 0, c), key(h, "FF+" if up else "FF-"))
        line(h, o, slot)
        aside(h, o, 0, slot)

    def far(h):
        slot = _shift(h, x, y, 2, 0, c)
        landed(slot, h * HALF, SUB, key(h, "FF+"))
        landed(slot, h * HALF + SUB, SUB, key(h, "FF-"))
        line(h, 2, slot)
        aside(h, 2, 0, slot)

    def second(h, o1, up):
        o = -1 if up else 1
        slot = _shift(h, x, y, o1, o, c)
        landed(slot, h * HALF, HALF, key(h, "G+" if up else "G-", o1))
        row = h * HALF + (0 if up else SUB)
        send(slot, row, SUB, _shift(h, x, y, 0, 1 if up else -1, c), key(h, "GF+" if up else "GF-", o1))
        aside(h, o1, o, slot)

    def corner(h, o1):
        slot = _shift(h, x, y, o1, 2, c)
        landed(slot, h * HALF, SUB, key(h, "GF+", o1))
        landed(slot, h * HALF + SUB, SUB, key(h, "GF-", o1))
        aside(h, o1, 2, slot)

    both = (0, 1)
    for h in both:
        start(h)
    for up in (True, False):
        for h in both:
            first(h, up)
    for up in (True, False):
        for h in both:
            second(h, 0, up)
    for h in both:
        far(h)
    for o1 in (-1, 1):
        for up in (True, False):
            for h in both:
                second(h, o1, up)
    for h in both:
        corner(h, 0)
    for up in (True, False):
        for h in both:
            second(h, 2, up)
    for o1 in (-1, 1, 2):
        for h in both:
            corner(h, o1)
    for o2 in (0, -1, 1, 2):
        for o1 in (0, -1, 1, 2):
            for h in both:
                landed(_shift(h, x, y, o1, o2, 1 - c), h * HALF, HALF, key(h, "S", o1, o2))
    for cp in sends:
        cp.wait_send()
    own.wait()


def _gather(blk):
    width = blk.shape[1]
    return pl.pallas_call(
        _gather_kernel,
        out_shape=jax.ShapeDtypeStruct((32, TOK, width), BF),
        in_specs=[pl.BlockSpec(memory_space=pltpu.VMEM)],
        out_specs=pl.BlockSpec(memory_space=pl.ANY),
        scratch_shapes=[
            pltpu.SemaphoreType.DMA((72,)),
            pltpu.SemaphoreType.DMA((72,)),
            pltpu.SemaphoreType.DMA,
        ],
        compiler_params=pltpu.CompilerParams(collective_id=0, has_side_effects=True),
        name="plane_gather",
    )(blk)


def _add(dst, src, n):
    @pl.loop(0, n // 16)
    def _(i):
        rows = pl.ds(pl.multiple_of(i * 16, 16), 16)
        dst[rows, :] = (dst[rows, :].astype(F32) + src[rows, :].astype(F32)).astype(BF)


def _add3(dst, own, one, two, n):
    @pl.loop(0, n // 16)
    def _(i):
        rows = pl.ds(pl.multiple_of(i * 16, 16), 16)
        total = own[rows, :].astype(F32) + one[rows, :].astype(F32) + two[rows, :].astype(F32)
        dst[rows, :] = total.astype(dst.dtype)


def _reduce_kernel(
    part, out, aside, T, sb, ra, rb, r2a, r2b, ssem, rsem, tsem, bsem
):
    z, x, y, c = _place()
    sib = (z, _at(x, y, 1 - c))
    _greet(
        [(z, _at(x + 1, y, c)), (z, _at(x - 1, y, c)), (z, _at(x, y + 1, c)), (z, _at(x, y - 1, c)), sib]
    )
    sends, keys = [], {}

    def remote(src, dst, to, *k):
        cp = pltpu.make_async_remote_copy(
            src_ref=src,
            dst_ref=dst,
            send_sem=ssem.at[len(sends)],
            recv_sem=rsem.at[keys.setdefault(k, len(keys))],
            device_id=to,
            device_id_type=MESH,
        )
        cp.start()
        sends.append(cp)

    def landed(dst, *k):
        pltpu.make_async_remote_copy(
            src_ref=dst,
            dst_ref=dst,
            send_sem=ssem.at[0],
            recv_sem=rsem.at[keys[k]],
            device_id=sib,
            device_id_type=MESH,
        ).wait_recv()

    lo, hi, full = pl.ds(0, SUB), pl.ds(SUB, SUB), pl.ds(0, HALF)
    both = (0, 1)
    obs, oas = (2, 1, 3, 0), (2, 1, 3, 0)
    order = [(h, ob, oa) for ob in obs for oa in oas for h in both]

    def ax(h, o):
        return (z, _shift(1 - h, x, y, o, 0, c))

    def bx(h, o):
        return (z, _shift(h, x, y, o, 0, c))

    def slot(h, ob, oa, core):
        return _shift(h, x, y, ob, oa, core)

    tcopies = {}
    for i, (h, ob, oa) in enumerate(order):
        rows = pl.ds(h * HALF, HALF)
        k = ob * 4 + oa
        remote(part.at[slot(h, ob, oa, 1 - c), rows], aside.at[h, k], sib, "s", h, ob, oa)
        cp = pltpu.make_async_copy(part.at[slot(h, ob, oa, c), rows], T.at[h, k], tsem.at[i])
        cp.start()
        tcopies[h, ob, oa] = cp
    loads = {}

    def fetch(i):
        h, ob, oa = order[i]
        landed(aside.at[h, ob * 4 + oa], "s", h, ob, oa)
        cp = pltpu.make_async_copy(aside.at[h, ob * 4 + oa], sb.at[i % 3], bsem.at[i % 3])
        cp.start()
        loads[i] = cp

    def one(i):
        h, ob, oa = order[i]
        if i + 1 < len(order):
            fetch(i + 1)
        tcopies[h, ob, oa].wait()
        loads[i].wait()
        t = T.at[h, ob * 4 + oa]
        _add(t, sb.at[i % 3], HALF)
        if oa == 2:
            remote(t.at[lo], ra.at[h, ob, 0], ax(h, 1), "ra", h, ob, 0)
            remote(t.at[hi], ra.at[h, ob, 1], ax(h, -1), "ra", h, ob, 1)
        elif oa == 1:
            remote(t.at[hi], rb.at[h, ob, 0, hi], ax(h, 1), "rd", h, ob, 0)
        elif oa == 3:
            remote(t.at[lo], rb.at[h, ob, 1, lo], ax(h, -1), "rd", h, ob, 1)

    def stage1(j):
        for i in range(j * 8, j * 8 + 8):
            one(i)

    def stage2(j):
        ob = obs[j]
        for h in both:
            landed(ra.at[h, ob, 0], "ra", h, ob, 0)
            t = T.at[h, ob * 4 + 1]
            _add(t.at[lo], ra.at[h, ob, 0], SUB)
            remote(t.at[lo], rb.at[h, ob, 0, lo], ax(h, 1), "rs", h, ob, 0)
            landed(ra.at[h, ob, 1], "ra", h, ob, 1)
            t = T.at[h, ob * 4 + 3]
            _add(t.at[hi], ra.at[h, ob, 1], SUB)
            remote(t.at[hi], rb.at[h, ob, 1, hi], ax(h, -1), "rs", h, ob, 1)

    def stage3(j):
        ob = obs[j]
        for h in both:
            landed(rb.at[h, ob, 0, hi], "rd", h, ob, 0)
            landed(rb.at[h, ob, 1, lo], "rd", h, ob, 1)
            landed(rb.at[h, ob, 0, lo], "rs", h, ob, 0)
            landed(rb.at[h, ob, 1, hi], "rs", h, ob, 1)
            t = T.at[h, ob * 4]
            _add3(t, t, rb.at[h, ob, 0], rb.at[h, ob, 1], HALF)
            if ob == 2:
                remote(t.at[lo], r2a.at[h, 0], bx(h, 1), "2a", h, 0)
                remote(t.at[hi], r2a.at[h, 1], bx(h, -1), "2a", h, 1)
            elif ob == 1:
                remote(t.at[hi], r2b.at[h, 0, hi], bx(h, 1), "2d", h, 0)
            elif ob == 3:
                remote(t.at[lo], r2b.at[h, 1, lo], bx(h, -1), "2d", h, 1)

    def stage4():
        for h in both:
            landed(r2a.at[h, 0], "2a", h, 0)
            t = T.at[h, 4]
            _add(t.at[lo], r2a.at[h, 0], SUB)
            remote(t.at[lo], r2b.at[h, 0, lo], bx(h, 1), "2s", h, 0)
            landed(r2a.at[h, 1], "2a", h, 1)
            t = T.at[h, 12]
            _add(t.at[hi], r2a.at[h, 1], SUB)
            remote(t.at[hi], r2b.at[h, 1, hi], bx(h, -1), "2s", h, 1)

    def stage5():
        for h in both:
            landed(r2b.at[h, 0, hi], "2d", h, 0)
            landed(r2b.at[h, 1, lo], "2d", h, 1)
            landed(r2b.at[h, 0, lo], "2s", h, 0)
            landed(r2b.at[h, 1, hi], "2s", h, 1)
            _add3(out.at[pl.ds(h * HALF, HALF)], T.at[h, 0], r2b.at[h, 0], r2b.at[h, 1], HALF)

    fetch(0)
    stage1(0)
    stage1(1)
    stage2(0)
    stage1(2)
    stage2(1)
    stage3(0)
    stage1(3)
    stage2(2)
    stage3(1)
    stage2(3)
    stage3(2)
    stage4()
    stage3(3)
    stage5()
    for cp in sends:
        cp.wait_send()


def _reduce(part):
    width = part.shape[2]
    hbm = pl.BlockSpec(memory_space=pl.ANY)
    return pl.pallas_call(
        _reduce_kernel,
        out_shape=(
            jax.ShapeDtypeStruct((TOK, width), BF),
            jax.ShapeDtypeStruct((2, 16, HALF, width), BF),
        ),
        in_specs=[hbm],
        out_specs=(pl.BlockSpec(memory_space=pltpu.VMEM), hbm),
        scratch_shapes=[
            pltpu.VMEM((2, 16, HALF, width), BF),
            pltpu.VMEM((3, HALF, width), BF),
            pltpu.VMEM((2, 4, 2, SUB, width), BF),
            pltpu.VMEM((2, 4, 2, HALF, width), BF),
            pltpu.VMEM((2, 2, SUB, width), BF),
            pltpu.VMEM((2, 2, HALF, width), BF),
            pltpu.SemaphoreType.DMA((96,)),
            pltpu.SemaphoreType.DMA((96,)),
            pltpu.SemaphoreType.DMA((32,)),
            pltpu.SemaphoreType.DMA((3,)),
        ],
        compiler_params=pltpu.CompilerParams(
            collective_id=1, has_side_effects=True, vmem_limit_bytes=48 * 1024 * 1024
        ),
        cost_estimate=pl.CostEstimate(flops=0, bytes_accessed=300_000_000, transcendentals=0),
        name="plane_reduce",
    )(part)


def _grads_kernel(q_ref, x_ref, c_ref, dg_ref, du_ref, h_ref, lo_ref, hi_ref):
    dims = (((0,), (0,)), ((), ()))
    n = lo_ref.shape[2]
    for k, (rows, cots) in enumerate(((x_ref, dg_ref), (x_ref, du_ref), (c_ref, h_ref))):
        g = lax.dot_general(rows[0], cots[0], dims, preferred_element_type=F32).astype(BF)
        lo_ref[k, 0] = g[:n]
        hi_ref[k, 0] = g[n:]


def _grads(quarter, xr, cr, d_gate, d_up, hidden):
    rows, width = xr.shape[1:]
    hid = hidden.shape[2]
    wide = pl.BlockSpec((1, rows, width // 4), lambda e, q: (e, 0, q[0]))
    thin = pl.BlockSpec((1, rows, hid), lambda e, q: (e, 0, 0))
    half = jax.ShapeDtypeStruct((3, 2, width // 8, hid), BF)
    spec = pl.BlockSpec((3, 1, width // 8, hid), lambda e, q: (0, e, 0, 0))
    return pl.pallas_call(
        _grads_kernel,
        grid_spec=pltpu.PrefetchScalarGridSpec(
            num_scalar_prefetch=1, grid=(2,), in_specs=[wide, wide, thin, thin, thin], out_specs=(spec, spec)
        ),
        out_shape=(half, half),
        cost_estimate=pl.CostEstimate(
            flops=12 * rows * (width // 4) * hid, bytes_accessed=14_000_000, transcendentals=0
        ),
        name="grad_quarter",
    )(quarter, xr, cr, d_gate, d_up, hidden)


GROUP = 4
PAIRS = GROUP // 2


def _pick_kernel(all_ref, s_ref, w_ref, x_ref, c_ref):
    width = x_ref.shape[-1]
    for p in range(PAIRS):
        pick = s_ref[p]
        xs = jnp.dot(pick, all_ref[p, :, :width], preferred_element_type=F32).astype(BF)
        cs = jnp.dot(pick, all_ref[p, :, width : 2 * width], preferred_element_type=F32)
        cs = (cs * w_ref[p]).astype(BF)
        for i in range(2):
            for e in range(2):
                at = (2 * i + e) * CAP
                x_ref[e, 2 * p + i] = xs[at : at + CAP]
                c_ref[e, 2 * p + i] = cs[at : at + CAP]


def _pick(everything, sel, wrow, width):
    rows = jax.ShapeDtypeStruct((2, 32, CAP, width), BF)
    spec = pl.BlockSpec((2, GROUP, CAP, width), lambda s: (0, s, 0, 0))
    return pl.pallas_call(
        _pick_kernel,
        grid=(32 // GROUP,),
        out_shape=(rows, rows),
        in_specs=[
            pl.BlockSpec((PAIRS,) + everything.shape[1:], lambda s: (s, 0, 0)),
            pl.BlockSpec((PAIRS, 4 * CAP, 2 * TOK), lambda s: (s, 0, 0)),
            pl.BlockSpec((PAIRS, 4 * CAP, 1), lambda s: (s, 0, 0)),
        ],
        out_specs=(spec, spec),
        compiler_params=pltpu.CompilerParams(vmem_limit_bytes=40 * 1024 * 1024),
        cost_estimate=pl.CostEstimate(flops=3_000_000_000, bytes_accessed=48_000_000, transcendentals=0),
        name="pick_rows",
    )(everything, sel, wrow)


def _spread_kernel(s_ref, y_ref, d_ref, r_ref, out_ref):
    width = y_ref.shape[-1]
    for p in range(PAIRS):
        sel = s_ref[p]

        def put(rows, at, n):
            spread = jnp.dot(sel, rows, preferred_element_type=F32).astype(BF)
            for i in range(2):
                out_ref[2 * p + i, :, at : at + n] = spread[i * TOK : (i + 1) * TOK]

        for at, ref in ((0, y_ref), (width, d_ref)):
            rows = [ref[e, 2 * p + i] for i in range(2) for e in range(2)]
            put(jnp.concatenate(rows, 0), at, width)
        put(r_ref[p], 2 * width, META)


def _spread(sel, yrows, dxrows, rrows):
    width = yrows.shape[-1]
    spec = pl.BlockSpec((2, GROUP, CAP, width), lambda s: (0, s, 0, 0))
    full = 2 * width + META
    return pl.pallas_call(
        _spread_kernel,
        grid=(32 // GROUP,),
        out_shape=jax.ShapeDtypeStruct((32, TOK, full), BF),
        in_specs=[
            pl.BlockSpec((PAIRS, 2 * TOK, 4 * CAP), lambda s: (s, 0, 0)),
            spec,
            spec,
            pl.BlockSpec((PAIRS, 4 * CAP, META), lambda s: (s, 0, 0)),
        ],
        out_specs=pl.BlockSpec((GROUP, TOK, full), lambda s: (s, 0, 0)),
        compiler_params=pltpu.CompilerParams(vmem_limit_bytes=40 * 1024 * 1024),
        cost_estimate=pl.CostEstimate(flops=3_000_000_000, bytes_accessed=48_000_000, transcendentals=0),
        name="spread_rows",
    )(sel, yrows, dxrows, rrows)


def _bits(v):
    return lax.reduce_precision(v, 8, 7)


def on_device(tokens, routes, route_weights, cotangent, gate_proj, up_proj, down_proj):
    width = tokens.shape[1]
    hid = gate_proj.shape[2]
    me = lax.axis_index("expert")
    w_hi = _bits(route_weights)
    w_mid = _bits(route_weights - w_hi)
    w_lo = route_weights - w_hi - w_mid
    meta = jnp.concatenate(
        [routes.astype(F32), w_hi, w_mid, w_lo, jnp.zeros((TOK, META - 32), F32)], 1
    ).astype(BF)
    everything = _gather(jnp.concatenate([tokens, cotangent, meta], 1))

    meta_all = everything[:, :, 2 * width :].astype(F32)
    named = meta_all[:, :, 0:8].astype(jnp.int32)
    weights = meta_all[:, :, 8:16] + meta_all[:, :, 16:24] + meta_all[:, :, 24:32]
    mine = 2 * me + jnp.arange(2, dtype=jnp.int32)
    match = named[:, None, :, :] == mine[None, :, None, None]
    hit = jnp.any(match, axis=3)
    wtok = jnp.sum(jnp.where(match, weights[:, None], 0.0), axis=3)
    tri = (jnp.arange(TOK)[:, None] < jnp.arange(TOK)[None, :]).astype(BF)
    place = jnp.dot(hit.reshape(64, TOK).astype(BF), tri, preferred_element_type=F32)
    place = place.reshape(32, 2, 1, TOK).astype(jnp.int32)
    chosen = hit[:, :, None, :] & (place == jnp.arange(CAP, dtype=jnp.int32)[None, None, :, None])
    pair = jnp.eye(2, dtype=bool)[None, :, None, :, None]
    sel = (chosen.reshape(16, 2, 2 * CAP, 1, TOK) & pair).astype(BF)
    sel = sel.reshape(16, 4 * CAP, 2 * TOK)
    back = jnp.transpose(sel, (0, 2, 1))
    wrow = jnp.sum(jnp.where(chosen, wtok[:, :, None, :], 0.0), axis=3)

    xr, cr = _pick(
        everything.reshape(16, 2 * TOK, 2 * width + META), sel, wrow.reshape(16, 4 * CAP, 1), width
    )
    xr = xr.reshape(2, 32 * CAP, width)
    cr = cr.reshape(2, 32 * CAP, width)
    we = jnp.transpose(wrow, (1, 0, 2)).reshape(2, 32 * CAP, 1)

    gate_pre = jnp.einsum("erd,edh->erh", xr, gate_proj, preferred_element_type=F32)
    up_pre = jnp.einsum("erd,edh->erh", xr, up_proj, preferred_element_type=F32)
    sig = jax.nn.sigmoid(gate_pre)
    swish = gate_pre * sig
    d_swish = sig * (1.0 + gate_pre * (1.0 - sig))
    hidden = (swish * up_pre).astype(BF)
    d_hidden = jnp.einsum("erd,ehd->erh", cr, down_proj, preferred_element_type=F32)
    d_gate = (d_hidden * up_pre * d_swish).astype(BF)
    d_up = (d_hidden * swish).astype(BF)
    rw = jnp.sum(d_hidden * hidden.astype(F32), axis=2, keepdims=True) / jnp.where(we > 0, we, 1.0)

    z = lax.axis_index("dp")
    up = [(i, (i + 1) % 4) for i in range(4)]
    down = [(i, (i + 3) % 4) for i in range(4)]

    def quarter(o):
        return _grads(((z + o) % 4).reshape(1), xr, cr, d_gate, d_up, hidden)

    def along(v, way):
        return lax.ppermute(v, "dp", way)

    lo2, hi2 = quarter(2)
    far_up, far_down = along(lo2, up), along(hi2, down)
    lo1, hi1 = quarter(1)
    near_up = along(hi1, up)
    lo3, hi3 = quarter(3)
    near_down = along(lo3, down)
    lo0, hi0 = quarter(0)
    yrows = (jnp.einsum("erh,ehd->erd", hidden, down_proj, preferred_element_type=F32) * we).astype(BF)
    dxrows = (
        jnp.einsum("erh,edh->erd", d_gate, gate_proj, preferred_element_type=F32)
        + jnp.einsum("erh,edh->erd", d_up, up_proj, preferred_element_type=F32)
    ).astype(BF)
    lane = jnp.arange(META, dtype=jnp.int32)
    r_hi = _bits(rw)
    r_lo = rw - r_hi
    spot = lane[None, None, :] - mine[:, None, None]
    rrows = jnp.where(spot == 0, r_hi, 0.0) + jnp.where(spot == 64, r_lo, 0.0)
    rrows = rrows.reshape(2, 32, CAP, META).transpose(1, 0, 2, 3).reshape(16, 4 * CAP, META).astype(BF)

    part = _spread(
        back, yrows.reshape(2, 32, CAP, width), dxrows.reshape(2, 32, CAP, width), rrows
    )

    def plus(one, two):
        return (one.astype(F32) + two.astype(F32)).astype(BF)

    sum_up, sum_down = along(plus(lo1, far_up), up), along(plus(hi3, far_down), down)
    out, _ = _reduce(part)

    def total(one, two, three):
        return one.astype(F32) + two.astype(F32) + three.astype(F32)

    shares = jnp.concatenate([total(lo0, sum_up, near_down), total(hi0, near_up, sum_down)], 2)
    table = out[:, 2 * width : 2 * width + 64].astype(F32) + out[:, 2 * width + 64 :].astype(F32)
    onehot = routes[:, :, None] == jnp.arange(64, dtype=jnp.int32)[None, None, :]
    weight_grad = jnp.sum(jnp.where(onehot, table[:, None, :], 0.0), axis=2)

    def final(g):
        return jnp.transpose(g, (1, 0, 2))

    return (out[:, :width], out[:, width : 2 * width], weight_grad, final(shares[0]), final(shares[1]), final(shares[2]))


def solution(mesh):
    rows = P(("dp", "expert"), None)
    experts = P("expert", None, None)
    grads = P("dp", "expert", None)
    return jax.shard_map(
        on_device,
        mesh=mesh,
        in_specs=(rows, rows, rows, rows, experts, experts, experts),
        out_specs=(rows, rows, rows, grads, grads, grads),
        check_vma=False,
    )
```

```python
import jax
import jax.numpy as jnp
from jax import lax
from jax.experimental import pallas as pl
from jax.experimental.pallas import tpu as pltpu
from jax.sharding import PartitionSpec as P

MESH = pl.DeviceIdType.MESH
BF = jnp.bfloat16
F32 = jnp.float32
SIDE = 4
TOK = 128
HALF = 64
SUB = 32
CAP = 24
META = 128


def _place():
    me = lax.axis_index("expert")
    return lax.axis_index("dp"), me // 8, (me // 2) % 4, me % 2


def _at(x, y, c):
    return ((x + 8) % 4) * 8 + ((y + 8) % 4) * 2 + c


def _greet(peers):
    barrier = pltpu.get_barrier_semaphore()
    for peer in peers:
        pl.semaphore_signal(barrier, inc=1, device_id=peer, device_id_type=MESH)
    pl.semaphore_wait(barrier, len(peers))


def _shift(h, x, y, o1, o2, c):
    return _at(x + o1, y + o2, c) if h == 0 else _at(x + o2, y + o1, c)


class _Gather:
    def __init__(self, tag, blk, out, ssem, rsem, sends, keys):
        self.tag, self.blk, self.out, self.ssem, self.rsem = tag, blk, out, ssem, rsem
        self.sends, self.keys = sends, keys
        self.z, self.x, self.y, self.c = _place()
        self.mine = _at(self.x, self.y, self.c)
        self.sib = _at(self.x, self.y, 1 - self.c)

    def shift(self, h, o1, o2):
        return _shift(h, self.x, self.y, o1, o2, self.c)

    def send(self, slot, row, n, to, *k):
        k = self.keys.setdefault((self.tag,) + k, len(self.keys))
        src = self.blk.at[pl.ds(row, n)] if slot is None else self.out.at[slot, pl.ds(row, n)]
        cp = pltpu.make_async_remote_copy(
            src_ref=src,
            dst_ref=self.out.at[self.mine if slot is None else slot, pl.ds(row, n)],
            send_sem=self.ssem.at[len(self.sends)],
            recv_sem=self.rsem.at[k],
            device_id=(self.z, to),
            device_id_type=MESH,
        )
        cp.start()
        self.sends.append(cp)

    def landed(self, slot, row, n, *k):
        k = self.keys[(self.tag,) + k]
        view = self.out.at[slot, pl.ds(row, n)]
        pltpu.make_async_remote_copy(
            src_ref=view,
            dst_ref=view,
            send_sem=self.ssem.at[0],
            recv_sem=self.rsem.at[k],
            device_id=(self.z, self.sib),
            device_id_type=MESH,
        ).wait_recv()

    def line(self, h, o1, slot):
        self.send(slot, h * HALF, HALF, self.shift(h, 0, 1), h, "G+", o1)
        self.send(slot, h * HALF, HALF, self.shift(h, 0, -1), h, "G-", o1)

    def aside(self, h, o1, o2, slot):
        self.send(slot, h * HALF, HALF, self.sib, h, "S", o1, o2)

    def start(self):
        for h in (0, 1):
            self.send(None, h * HALF, HALF, self.shift(h, 1, 0), h, "F+")
            self.send(None, h * HALF, HALF, self.shift(h, -1, 0), h, "F-")
            self.line(h, 0, None)
            self.aside(h, 0, 0, None)

    def first(self, h, o):
        slot, sign = self.shift(h, o, 0), "+" if o < 0 else "-"
        self.landed(slot, h * HALF, HALF, h, "F" + sign)
        self.send(slot, h * HALF + (0 if o < 0 else SUB), SUB, self.shift(h, -o, 0), h, "FF" + sign)
        self.line(h, o, slot)
        self.aside(h, o, 0, slot)

    def far(self, h):
        slot = self.shift(h, 2, 0)
        self.landed(slot, h * HALF, SUB, h, "FF+")
        self.landed(slot, h * HALF + SUB, SUB, h, "FF-")
        self.line(h, 2, slot)
        self.aside(h, 2, 0, slot)

    def second(self, h, o1, o):
        slot, sign = self.shift(h, o1, o), "+" if o < 0 else "-"
        self.landed(slot, h * HALF, HALF, h, "G" + sign, o1)
        self.send(slot, h * HALF + (0 if o < 0 else SUB), SUB, self.shift(h, 0, -o), h, "GF" + sign, o1)
        self.aside(h, o1, o, slot)

    def corner(self, h, o1):
        slot = self.shift(h, o1, 2)
        self.landed(slot, h * HALF, SUB, h, "GF+", o1)
        self.landed(slot, h * HALF + SUB, SUB, h, "GF-", o1)
        self.aside(h, o1, 2, slot)

    def event(self, o1, o2):
        for h in (0, 1):
            if o2 == 0:
                self.far(h) if o1 == 2 else self.first(h, o1)
            elif o2 == 2:
                self.corner(h, o1)
            else:
                self.second(h, o1, o2)

    def chip(self, dx, dy):
        for h, o1, o2 in ((0, dx, dy), (1, dy, dx)):
            slot = _at(self.x + dx, self.y + dy, 1 - self.c)
            self.landed(slot, h * HALF, HALF, h, "S", o1, o2)
        return _at(self.x + dx, self.y + dy, 0) // 2


EVENTS = (
    (-1, 0), (1, 0), (0, -1), (0, 1), (2, 0), (-1, -1), (-1, 1), (1, -1), (1, 1),
    (0, 2), (2, -1), (2, 1), (-1, 2), (1, 2), (2, 2),
)
ROWS = 2 * CAP


def _tokens_of(ref, chip, lanes):
    return ref[pl.ds(2 * chip, 2), :, lanes].reshape(2 * TOK, -1)


def _pick_dot(back, rows):
    dims = (((0,), (0,)), ((), ()))
    return lax.dot_general(back, rows, dims, preferred_element_type=F32)[: 2 * ROWS]


def _front_kernel(
    xm, ct, gw, uw, back_out, xr_out, cr_out, wr_out, gu_out, call,
    xall, cbuf, xr, cr, wgu, gu, back, wr,
    ssem, rsem, lsem, wsem, csem, osem, rowsem,
):
    me = lax.axis_index("expert")
    z, x, y, c = _place()
    width, hid = ct.shape[1], gw.shape[2]
    weights = []
    for e in range(2):
        for k, ref in enumerate((gw, uw)):
            cp = pltpu.make_async_copy(ref.at[e], wgu.at[e, :, pl.ds(k * hid, hid)], wsem.at[2 * e + k])
            cp.start()
            weights.append(cp)
    _greet(
        [
            (z, _at(x + 1, y, c)), (z, _at(x - 1, y, c)), (z, _at(x, y + 1, c)), (z, _at(x, y - 1, c)),
            (z, _at(x, y, 1 - c)),
        ]
    )
    sends, keys = [], {}
    gx = _Gather("x", xm, xall, ssem, rsem, sends, keys)
    gc = _Gather("c", ct, call, ssem, rsem, sends, keys)
    own_x = pltpu.make_async_copy(xm, xall.at[gx.mine], lsem.at[0])
    own_c = pltpu.make_async_copy(ct, call.at[gx.mine], lsem.at[1])
    own_x.start()
    own_c.start()
    gx.start()

    def number(shape, dim):
        return lax.broadcasted_iota(jnp.int32, shape, dim)

    def rows_of(dx, dy):
        chip = gx.chip(dx, dy)
        meta = _tokens_of(xall, chip, pl.ds(width, META)).astype(F32)
        tok, lane = number((2 * TOK, META), 0), number((2 * TOK, META), 1)
        hits = []
        for e in range(2):
            match = (meta == (2 * me + e).astype(F32)) & (lane < 8)
            hits.append(jnp.max(jnp.where(match, 1.0, 0.0), axis=1, keepdims=True))
        both = jnp.where(lane == 0, hits[0], jnp.where(lane == 1, hits[1], 0.0)).astype(BF)
        t0, t1 = number((2 * TOK, 2 * TOK), 0), number((2 * TOK, 2 * TOK), 1)
        earlier = ((t1 < t0) & ((t1 < TOK) == (t0 < TOK))).astype(F32).astype(BF)
        before = jnp.dot(earlier, both, preferred_element_type=F32)
        second = lane >= ROWS
        place = lane - jnp.where(second, ROWS, 0)
        late = place >= CAP
        place = place - jnp.where(late, CAP, 0)
        hit = jnp.where(second, hits[1], hits[0])
        spot = jnp.where(second, before[:, 1:2], before[:, 0:1])
        chosen = (hit > 0.5) & (spot == place.astype(F32)) & (late == (tok >= TOK)) & (lane < 2 * ROWS)
        pick = jnp.where(chosen, 1.0, 0.0).astype(BF)
        back[chip] = pick
        rows = _pick_dot(pick, _tokens_of(xall, chip, pl.ds(0, width))).astype(BF)
        at = pl.ds(pl.multiple_of(chip * ROWS, 16), ROWS)
        xr[0, at, :] = rows[:ROWS]
        xr[1, at, :] = rows[ROWS:]
        info = _pick_dot(pick, meta.astype(BF))
        shape = (2 * ROWS, META)
        expert = (2 * me + jnp.where(number(shape, 0) >= ROWS, 1, 0)).astype(F32)
        match = jnp.where((info == expert) & (number(shape, 1) < 8), 1.0, 0.0).astype(BF)
        k0, k1 = number((META, META), 0), number((META, META), 1)
        copies = ((k1 == k0 + 8) | (k1 == k0 + 16) | (k1 == k0 + 24)) & (k0 < 8)
        spread = jnp.dot(match, jnp.where(copies, 1.0, 0.0).astype(BF), preferred_element_type=F32)
        weight = jnp.sum(spread * info, axis=1, keepdims=True)
        wr[chip] = jnp.broadcast_to(weight, shape)

    def drive(gather, work, before=None):
        done, waiting, ready = {(0, 0)}, [], [(0, 0)]
        for n, (o1, o2) in enumerate(EVENTS):
            if before is not None:
                before(n)
            gather.event(o1, o2)
            for chip in waiting:
                work(*chip)
            waiting, ready = ready, []
            done.add((o1, o2))
            if (o2, o1) in done:
                ready = [(o1, o2)] if o1 == o2 else [(o1, o2), (o2, o1)]
        for chip in waiting + ready:
            work(*chip)

    def middle(n):
        if n == 9:
            gc.start()

    own_x.wait()
    drive(gx, rows_of, middle)
    outs = []

    def put(src, dst, sem):
        cp = pltpu.make_async_copy(src, dst, sem)
        cp.start()
        outs.append(cp)

    put(xr, xr_out, osem.at[0])
    put(back, back_out, osem.at[1])
    put(wr, wr_out, osem.at[2])

    def project(e, first, last):
        @pl.loop(first, last)
        def _(j):
            cols = pl.ds(pl.multiple_of(j * 256, 256), 256)
            gu[e, :, cols] = jnp.dot(xr[e], wgu[e, :, cols], preferred_element_type=F32)

    steps = 2 * hid // 256
    units = {2: (0, 0, 2), 4: (0, 2, steps), 6: (1, 0, 2), 8: (1, 2, steps)}

    def compute(n):
        if n in units:
            e, first, last = units[n]
            if first == 0:
                weights[2 * e].wait()
                weights[2 * e + 1].wait()
            project(e, first, last)
            if last == steps:
                put(gu.at[e], gu_out.at[e], osem.at[3 + e])

    own_c.wait()
    fetched = []

    def finish():
        i, chip, cp = fetched.pop(0)
        cp.wait()
        rows = _pick_dot(back[chip], cbuf[i % 3].reshape(2 * TOK, width))
        rows = (rows * wr[chip][:, 0:1]).astype(BF)
        at = pl.ds(pl.multiple_of(chip * ROWS, 16), ROWS)
        for e in range(2):
            cr[e, at, :] = rows[e * ROWS : (e + 1) * ROWS]
            put(cr.at[e, at], cr_out.at[e, at], rowsem.at[2 * i + e])

    count = [0]

    def cot_of(dx, dy):
        chip = gc.chip(dx, dy)
        i = count[0]
        count[0] += 1
        cp = pltpu.make_async_copy(call.at[pl.ds(2 * chip, 2)], cbuf.at[i % 3], csem.at[i % 3])
        cp.start()
        fetched.append((i, chip, cp))
        if len(fetched) > 2:
            finish()

    drive(gc, cot_of, compute)
    while fetched:
        finish()
    for cp in outs:
        cp.wait()
    for cp in sends:
        cp.wait_send()


def _front(xm, ct, gate_proj, up_proj):
    width, hid = ct.shape[1], gate_proj.shape[2]
    hbm = pl.BlockSpec(memory_space=pl.ANY)
    vmem = pl.BlockSpec(memory_space=pltpu.VMEM)
    rows = 32 * CAP
    return pl.pallas_call(
        _front_kernel,
        out_shape=(
            jax.ShapeDtypeStruct((16, 2 * TOK, META), BF),
            jax.ShapeDtypeStruct((2, rows, width), BF),
            jax.ShapeDtypeStruct((2, rows, width), BF),
            jax.ShapeDtypeStruct((16, 2 * ROWS, META), F32),
            jax.ShapeDtypeStruct((2, rows, 2 * hid), F32),
            jax.ShapeDtypeStruct((32, TOK, width), BF),
        ),
        in_specs=[vmem, vmem, hbm, hbm],
        out_specs=(hbm,) * 6,
        scratch_shapes=[
            pltpu.VMEM((32, TOK, width + META), BF),
            pltpu.VMEM((3, 2, TOK, width), BF),
            pltpu.VMEM((2, rows, width), BF),
            pltpu.VMEM((2, rows, width), BF),
            pltpu.VMEM((2, width, 2 * hid), BF),
            pltpu.VMEM((2, rows, 2 * hid), F32),
            pltpu.VMEM((16, 2 * TOK, META), BF),
            pltpu.VMEM((16, 2 * ROWS, META), F32),
            pltpu.SemaphoreType.DMA((144,)),
            pltpu.SemaphoreType.DMA((144,)),
            pltpu.SemaphoreType.DMA((2,)),
            pltpu.SemaphoreType.DMA((4,)),
            pltpu.SemaphoreType.DMA((3,)),
            pltpu.SemaphoreType.DMA((5,)),
            pltpu.SemaphoreType.DMA((32,)),
        ],
        compiler_params=pltpu.CompilerParams(
            collective_id=0, has_side_effects=True, vmem_limit_bytes=63 * 1024 * 1024
        ),
        cost_estimate=pl.CostEstimate(flops=10_000_000_000, bytes_accessed=300_000_000, transcendentals=0),
        name="plane_gather",
    )(xm, ct, gate_proj, up_proj)


def _add(dst, src, n):
    @pl.loop(0, n // 16)
    def _(i):
        rows = pl.ds(pl.multiple_of(i * 16, 16), 16)
        dst[rows, :] = (dst[rows, :].astype(F32) + src[rows, :].astype(F32)).astype(BF)


def _add3(dst, own, one, two, n):
    @pl.loop(0, n // 16)
    def _(i):
        rows = pl.ds(pl.multiple_of(i * 16, 16), 16)
        total = own[rows, :].astype(F32) + one[rows, :].astype(F32) + two[rows, :].astype(F32)
        dst[rows, :] = total.astype(dst.dtype)


def _reduce_kernel(
    part, out, aside, T, sb, ra, rb, r2a, r2b, ssem, rsem, tsem, bsem
):
    z, x, y, c = _place()
    sib = (z, _at(x, y, 1 - c))
    _greet(
        [(z, _at(x + 1, y, c)), (z, _at(x - 1, y, c)), (z, _at(x, y + 1, c)), (z, _at(x, y - 1, c)), sib]
    )
    sends, keys = [], {}

    def remote(src, dst, to, *k):
        cp = pltpu.make_async_remote_copy(
            src_ref=src,
            dst_ref=dst,
            send_sem=ssem.at[len(sends)],
            recv_sem=rsem.at[keys.setdefault(k, len(keys))],
            device_id=to,
            device_id_type=MESH,
        )
        cp.start()
        sends.append(cp)

    def landed(dst, *k):
        pltpu.make_async_remote_copy(
            src_ref=dst,
            dst_ref=dst,
            send_sem=ssem.at[0],
            recv_sem=rsem.at[keys[k]],
            device_id=sib,
            device_id_type=MESH,
        ).wait_recv()

    lo, hi, full = pl.ds(0, SUB), pl.ds(SUB, SUB), pl.ds(0, HALF)
    both = (0, 1)
    obs, oas = (2, 1, 3, 0), (2, 1, 3, 0)
    order = [(h, ob, oa) for ob in obs for oa in oas for h in both]

    def ax(h, o):
        return (z, _shift(1 - h, x, y, o, 0, c))

    def bx(h, o):
        return (z, _shift(h, x, y, o, 0, c))

    def slot(h, ob, oa, core):
        return _shift(h, x, y, ob, oa, core)

    tcopies = {}
    for i, (h, ob, oa) in enumerate(order):
        rows = pl.ds(h * HALF, HALF)
        k = ob * 4 + oa
        remote(part.at[slot(h, ob, oa, 1 - c), rows], aside.at[h, k], sib, "s", h, ob, oa)
        cp = pltpu.make_async_copy(part.at[slot(h, ob, oa, c), rows], T.at[h, k], tsem.at[i])
        cp.start()
        tcopies[h, ob, oa] = cp
    loads = {}

    def fetch(i):
        h, ob, oa = order[i]
        landed(aside.at[h, ob * 4 + oa], "s", h, ob, oa)
        cp = pltpu.make_async_copy(aside.at[h, ob * 4 + oa], sb.at[i % 3], bsem.at[i % 3])
        cp.start()
        loads[i] = cp

    def one(i):
        h, ob, oa = order[i]
        if i + 1 < len(order):
            fetch(i + 1)
        tcopies[h, ob, oa].wait()
        loads[i].wait()
        t = T.at[h, ob * 4 + oa]
        _add(t, sb.at[i % 3], HALF)
        if oa == 2:
            remote(t.at[lo], ra.at[h, ob, 0], ax(h, 1), "ra", h, ob, 0)
            remote(t.at[hi], ra.at[h, ob, 1], ax(h, -1), "ra", h, ob, 1)
        elif oa == 1:
            remote(t.at[hi], rb.at[h, ob, 0, hi], ax(h, 1), "rd", h, ob, 0)
        elif oa == 3:
            remote(t.at[lo], rb.at[h, ob, 1, lo], ax(h, -1), "rd", h, ob, 1)

    def stage1(j):
        for i in range(j * 8, j * 8 + 8):
            one(i)

    def stage2(j):
        ob = obs[j]
        for h in both:
            landed(ra.at[h, ob, 0], "ra", h, ob, 0)
            t = T.at[h, ob * 4 + 1]
            _add(t.at[lo], ra.at[h, ob, 0], SUB)
            remote(t.at[lo], rb.at[h, ob, 0, lo], ax(h, 1), "rs", h, ob, 0)
            landed(ra.at[h, ob, 1], "ra", h, ob, 1)
            t = T.at[h, ob * 4 + 3]
            _add(t.at[hi], ra.at[h, ob, 1], SUB)
            remote(t.at[hi], rb.at[h, ob, 1, hi], ax(h, -1), "rs", h, ob, 1)

    def stage3(j):
        ob = obs[j]
        for h in both:
            landed(rb.at[h, ob, 0, hi], "rd", h, ob, 0)
            landed(rb.at[h, ob, 1, lo], "rd", h, ob, 1)
            landed(rb.at[h, ob, 0, lo], "rs", h, ob, 0)
            landed(rb.at[h, ob, 1, hi], "rs", h, ob, 1)
            t = T.at[h, ob * 4]
            _add3(t, t, rb.at[h, ob, 0], rb.at[h, ob, 1], HALF)
            if ob == 2:
                remote(t.at[lo], r2a.at[h, 0], bx(h, 1), "2a", h, 0)
                remote(t.at[hi], r2a.at[h, 1], bx(h, -1), "2a", h, 1)
            elif ob == 1:
                remote(t.at[hi], r2b.at[h, 0, hi], bx(h, 1), "2d", h, 0)
            elif ob == 3:
                remote(t.at[lo], r2b.at[h, 1, lo], bx(h, -1), "2d", h, 1)

    def stage4():
        for h in both:
            landed(r2a.at[h, 0], "2a", h, 0)
            t = T.at[h, 4]
            _add(t.at[lo], r2a.at[h, 0], SUB)
            remote(t.at[lo], r2b.at[h, 0, lo], bx(h, 1), "2s", h, 0)
            landed(r2a.at[h, 1], "2a", h, 1)
            t = T.at[h, 12]
            _add(t.at[hi], r2a.at[h, 1], SUB)
            remote(t.at[hi], r2b.at[h, 1, hi], bx(h, -1), "2s", h, 1)

    def stage5():
        for h in both:
            landed(r2b.at[h, 0, hi], "2d", h, 0)
            landed(r2b.at[h, 1, lo], "2d", h, 1)
            landed(r2b.at[h, 0, lo], "2s", h, 0)
            landed(r2b.at[h, 1, hi], "2s", h, 1)
            _add3(out.at[pl.ds(h * HALF, HALF)], T.at[h, 0], r2b.at[h, 0], r2b.at[h, 1], HALF)

    fetch(0)
    stage1(0)
    stage1(1)
    stage2(0)
    stage1(2)
    stage2(1)
    stage3(0)
    stage1(3)
    stage2(2)
    stage3(1)
    stage2(3)
    stage3(2)
    stage4()
    stage3(3)
    stage5()
    for cp in sends:
        cp.wait_send()


def _reduce(part):
    width = part.shape[2]
    hbm = pl.BlockSpec(memory_space=pl.ANY)
    return pl.pallas_call(
        _reduce_kernel,
        out_shape=(
            jax.ShapeDtypeStruct((TOK, width), BF),
            jax.ShapeDtypeStruct((2, 16, HALF, width), BF),
        ),
        in_specs=[hbm],
        out_specs=(pl.BlockSpec(memory_space=pltpu.VMEM), hbm),
        scratch_shapes=[
            pltpu.VMEM((2, 16, HALF, width), BF),
            pltpu.VMEM((3, HALF, width), BF),
            pltpu.VMEM((2, 4, 2, SUB, width), BF),
            pltpu.VMEM((2, 4, 2, HALF, width), BF),
            pltpu.VMEM((2, 2, SUB, width), BF),
            pltpu.VMEM((2, 2, HALF, width), BF),
            pltpu.SemaphoreType.DMA((96,)),
            pltpu.SemaphoreType.DMA((96,)),
            pltpu.SemaphoreType.DMA((32,)),
            pltpu.SemaphoreType.DMA((3,)),
        ],
        compiler_params=pltpu.CompilerParams(
            collective_id=1, has_side_effects=True, vmem_limit_bytes=48 * 1024 * 1024
        ),
        cost_estimate=pl.CostEstimate(flops=0, bytes_accessed=300_000_000, transcendentals=0),
        name="plane_reduce",
    )(part)


def _grads_kernel(q_ref, x_ref, c_ref, dg_ref, du_ref, h_ref, lo_ref, hi_ref):
    dims = (((0,), (0,)), ((), ()))
    n = lo_ref.shape[2]
    for k, (rows, cots) in enumerate(((x_ref, dg_ref), (x_ref, du_ref), (c_ref, h_ref))):
        g = lax.dot_general(rows[0], cots[0], dims, preferred_element_type=F32).astype(BF)
        lo_ref[k, 0] = g[:n]
        hi_ref[k, 0] = g[n:]


def _grads(quarter, xr, cr, d_gate, d_up, hidden):
    rows, width = xr.shape[1:]
    hid = hidden.shape[2]
    wide = pl.BlockSpec((1, rows, width // 4), lambda e, q: (e, 0, q[0]))
    thin = pl.BlockSpec((1, rows, hid), lambda e, q: (e, 0, 0))
    half = jax.ShapeDtypeStruct((3, 2, width // 8, hid), BF)
    spec = pl.BlockSpec((3, 1, width // 8, hid), lambda e, q: (0, e, 0, 0))
    return pl.pallas_call(
        _grads_kernel,
        grid_spec=pltpu.PrefetchScalarGridSpec(
            num_scalar_prefetch=1, grid=(2,), in_specs=[wide, wide, thin, thin, thin], out_specs=(spec, spec)
        ),
        out_shape=(half, half),
        cost_estimate=pl.CostEstimate(
            flops=12 * rows * (width // 4) * hid, bytes_accessed=14_000_000, transcendentals=0
        ),
        name="grad_quarter",
    )(quarter, xr, cr, d_gate, d_up, hidden)


GROUP = 4
PAIRS = GROUP // 2


def _spread_kernel(s_ref, y_ref, d_ref, r_ref, out_ref):
    width = y_ref.shape[-1]
    for p in range(PAIRS):
        sel = s_ref[p, :, : 2 * ROWS]
        at_rows = pl.ds(p * ROWS, ROWS)

        def put(rows, at, n):
            spread = jnp.dot(sel, rows, preferred_element_type=F32).astype(BF)
            for i in range(2):
                out_ref[2 * p + i, :, at : at + n] = spread[i * TOK : (i + 1) * TOK]

        for at, ref in ((0, y_ref), (width, d_ref)):
            put(jnp.concatenate([ref[0, at_rows], ref[1, at_rows]], 0), at, width)
        put(r_ref[p], 2 * width, META)


def _spread(sel, yrows, dxrows, rrows):
    width = yrows.shape[-1]
    spec = pl.BlockSpec((2, PAIRS * ROWS, width), lambda s: (0, s, 0))
    full = 2 * width + META
    return pl.pallas_call(
        _spread_kernel,
        grid=(32 // GROUP,),
        out_shape=jax.ShapeDtypeStruct((32, TOK, full), BF),
        in_specs=[
            pl.BlockSpec((PAIRS, 2 * TOK, META), lambda s: (s, 0, 0)),
            spec,
            spec,
            pl.BlockSpec((PAIRS, 2 * ROWS, META), lambda s: (s, 0, 0)),
        ],
        out_specs=pl.BlockSpec((GROUP, TOK, full), lambda s: (s, 0, 0)),
        compiler_params=pltpu.CompilerParams(vmem_limit_bytes=40 * 1024 * 1024),
        cost_estimate=pl.CostEstimate(flops=3_000_000_000, bytes_accessed=48_000_000, transcendentals=0),
        name="spread_rows",
    )(sel, yrows, dxrows, rrows)


def _bits(v):
    return lax.reduce_precision(v, 8, 7)


def on_device(tokens, routes, route_weights, cotangent, gate_proj, up_proj, down_proj):
    width = tokens.shape[1]
    hid = gate_proj.shape[2]
    me = lax.axis_index("expert")
    w_hi = _bits(route_weights)
    w_mid = _bits(route_weights - w_hi)
    w_lo = route_weights - w_hi - w_mid
    meta = jnp.concatenate(
        [routes.astype(F32), w_hi, w_mid, w_lo, jnp.zeros((TOK, META - 32), F32)], 1
    ).astype(BF)
    mine = 2 * me + jnp.arange(2, dtype=jnp.int32)
    back, xr, cr, wr, gu, _ = _front(jnp.concatenate([tokens, meta], 1), cotangent, gate_proj, up_proj)
    we = wr[:, :, 0].reshape(16, 2, ROWS).transpose(1, 0, 2).reshape(2, 32 * CAP, 1)
    gate_pre, up_pre = gu[:, :, :hid], gu[:, :, hid:]
    sig = jax.nn.sigmoid(gate_pre)
    swish = gate_pre * sig
    d_swish = sig * (1.0 + gate_pre * (1.0 - sig))
    hidden = (swish * up_pre).astype(BF)
    d_hidden = jnp.einsum("erd,ehd->erh", cr, down_proj, preferred_element_type=F32)
    d_gate = (d_hidden * up_pre * d_swish).astype(BF)
    d_up = (d_hidden * swish).astype(BF)
    rw = jnp.sum(d_hidden * hidden.astype(F32), axis=2, keepdims=True) / jnp.where(we > 0, we, 1.0)

    z = lax.axis_index("dp")
    up = [(i, (i + 1) % 4) for i in range(4)]
    down = [(i, (i + 3) % 4) for i in range(4)]

    def quarter(o, after=None):
        which = ((z + o) % 4).reshape(1)
        if after is not None:
            which, _ = lax.optimization_barrier((which, after))
        return _grads(which, xr, cr, d_gate, d_up, hidden)

    def along(v, way):
        return lax.ppermute(v, "dp", way)

    lo2, hi2 = quarter(2)
    far_up, far_down = along(lo2, up), along(hi2, down)
    lo1, hi1 = quarter(1, lo2)
    near_up = along(hi1, up)
    lo3, hi3 = quarter(3, lo2)
    near_down = along(lo3, down)
    lo0, hi0 = quarter(0, lo3)
    yrows = (jnp.einsum("erh,ehd->erd", hidden, down_proj, preferred_element_type=F32) * we).astype(BF)
    dxrows = (
        jnp.einsum("erh,edh->erd", d_gate, gate_proj, preferred_element_type=F32)
        + jnp.einsum("erh,edh->erd", d_up, up_proj, preferred_element_type=F32)
    ).astype(BF)
    lane = jnp.arange(META, dtype=jnp.int32)
    r_hi = _bits(rw)
    r_lo = rw - r_hi
    spot = lane[None, None, :] - mine[:, None, None]
    rrows = jnp.where(spot == 0, r_hi, 0.0) + jnp.where(spot == 64, r_lo, 0.0)
    rrows = rrows.reshape(2, 16, ROWS, META).transpose(1, 0, 2, 3).reshape(16, 2 * ROWS, META).astype(BF)

    part = _spread(
        back, yrows, dxrows, rrows
    )

    def plus(one, two):
        return (one.astype(F32) + two.astype(F32)).astype(BF)

    sum_up, sum_down = along(plus(lo1, far_up), up), along(plus(hi3, far_down), down)
    out, _ = _reduce(part)

    def total(one, two, three):
        return one.astype(F32) + two.astype(F32) + three.astype(F32)

    shares = jnp.concatenate([total(lo0, sum_up, near_down), total(hi0, near_up, sum_down)], 2)
    table = out[:, 2 * width : 2 * width + 64].astype(F32) + out[:, 2 * width + 64 :].astype(F32)
    onehot = routes[:, :, None] == jnp.arange(64, dtype=jnp.int32)[None, None, :]
    weight_grad = jnp.sum(jnp.where(onehot, table[:, None, :], 0.0), axis=2)

    def final(g):
        return jnp.transpose(g, (1, 0, 2))

    return (out[:, :width], out[:, width : 2 * width], weight_grad, final(shares[0]), final(shares[1]), final(shares[2]))


def solution(mesh):
    rows = P(("dp", "expert"), None)
    experts = P("expert", None, None)
    grads = P("dp", "expert", None)
    return jax.shard_map(
        on_device,
        mesh=mesh,
        in_specs=(rows, rows, rows, rows, experts, experts, experts),
        out_specs=(rows, rows, rows, grads, grads, grads),
        check_vma=False,
    )
```

```python
import jax
import jax.numpy as jnp
from jax import lax
from jax.experimental import pallas as pl
from jax.experimental.pallas import tpu as pltpu
from jax.sharding import PartitionSpec as P

MESH = pl.DeviceIdType.MESH
BF = jnp.bfloat16
F32 = jnp.float32
TOK = 128
HALF = 64
SUB = 32
CAP = 24
META = 128


def _place():
    me = lax.axis_index("expert")
    return lax.axis_index("dp"), me // 8, (me // 2) % 4, me % 2


def _at(x, y, c):
    return ((x + 8) % 4) * 8 + ((y + 8) % 4) * 2 + c


def _greet(peers):
    barrier = pltpu.get_barrier_semaphore()
    for peer in peers:
        pl.semaphore_signal(barrier, inc=1, device_id=peer, device_id_type=MESH)
    pl.semaphore_wait(barrier, len(peers))


def _shift(h, x, y, o1, o2, c):
    return _at(x + o1, y + o2, c) if h == 0 else _at(x + o2, y + o1, c)


class _Gather:
    def __init__(self, tag, blk, out, ssem, rsem, sends, keys):
        self.tag, self.blk, self.out, self.ssem, self.rsem = tag, blk, out, ssem, rsem
        self.sends, self.keys = sends, keys
        self.z, self.x, self.y, self.c = _place()
        self.mine = _at(self.x, self.y, self.c)
        self.sib = _at(self.x, self.y, 1 - self.c)

    def shift(self, h, o1, o2):
        return _shift(h, self.x, self.y, o1, o2, self.c)

    def send(self, slot, row, n, to, *k):
        k = self.keys.setdefault((self.tag,) + k, len(self.keys))
        src = self.blk.at[pl.ds(row, n)] if slot is None else self.out.at[slot, pl.ds(row, n)]
        cp = pltpu.make_async_remote_copy(
            src_ref=src,
            dst_ref=self.out.at[self.mine if slot is None else slot, pl.ds(row, n)],
            send_sem=self.ssem.at[len(self.sends)],
            recv_sem=self.rsem.at[k],
            device_id=(self.z, to),
            device_id_type=MESH,
        )
        cp.start()
        self.sends.append(cp)

    def landed(self, slot, row, n, *k):
        k = self.keys[(self.tag,) + k]
        view = self.out.at[slot, pl.ds(row, n)]
        pltpu.make_async_remote_copy(
            src_ref=view,
            dst_ref=view,
            send_sem=self.ssem.at[0],
            recv_sem=self.rsem.at[k],
            device_id=(self.z, self.sib),
            device_id_type=MESH,
        ).wait_recv()

    def line(self, h, o1, slot):
        self.send(slot, h * HALF, HALF, self.shift(h, 0, 1), h, "G+", o1)
        self.send(slot, h * HALF, HALF, self.shift(h, 0, -1), h, "G-", o1)

    def aside(self, h, o1, o2, slot):
        self.send(slot, h * HALF, HALF, self.sib, h, "S", o1, o2)

    def start(self):
        for h in (0, 1):
            self.send(None, h * HALF, HALF, self.shift(h, 1, 0), h, "F+")
            self.send(None, h * HALF, HALF, self.shift(h, -1, 0), h, "F-")
            self.line(h, 0, None)
            self.aside(h, 0, 0, None)

    def first(self, h, o):
        slot, sign = self.shift(h, o, 0), "+" if o < 0 else "-"
        self.landed(slot, h * HALF, HALF, h, "F" + sign)
        self.send(slot, h * HALF + (0 if o < 0 else SUB), SUB, self.shift(h, -o, 0), h, "FF" + sign)
        self.line(h, o, slot)
        self.aside(h, o, 0, slot)

    def far(self, h):
        slot = self.shift(h, 2, 0)
        self.landed(slot, h * HALF, SUB, h, "FF+")
        self.landed(slot, h * HALF + SUB, SUB, h, "FF-")
        self.line(h, 2, slot)
        self.aside(h, 2, 0, slot)

    def second(self, h, o1, o):
        slot, sign = self.shift(h, o1, o), "+" if o < 0 else "-"
        self.landed(slot, h * HALF, HALF, h, "G" + sign, o1)
        self.send(slot, h * HALF + (0 if o < 0 else SUB), SUB, self.shift(h, 0, -o), h, "GF" + sign, o1)
        self.aside(h, o1, o, slot)

    def corner(self, h, o1):
        slot = self.shift(h, o1, 2)
        self.landed(slot, h * HALF, SUB, h, "GF+", o1)
        self.landed(slot, h * HALF + SUB, SUB, h, "GF-", o1)
        self.aside(h, o1, 2, slot)

    def event(self, o1, o2):
        for h in (0, 1):
            if o2 == 0:
                self.far(h) if o1 == 2 else self.first(h, o1)
            elif o2 == 2:
                self.corner(h, o1)
            else:
                self.second(h, o1, o2)

    def chip(self, dx, dy):
        for h, o1, o2 in ((0, dx, dy), (1, dy, dx)):
            slot = _at(self.x + dx, self.y + dy, 1 - self.c)
            self.landed(slot, h * HALF, HALF, h, "S", o1, o2)
        return _at(self.x + dx, self.y + dy, 0) // 2


EVENTS = (
    (-1, 0), (1, 0), (0, -1), (0, 1), (2, 0), (-1, -1), (-1, 1), (1, -1), (1, 1),
    (0, 2), (2, -1), (2, 1), (-1, 2), (1, 2), (2, 2),
)
ROWS = 2 * CAP


def _tokens_of(ref, chip, lanes):
    return ref[pl.ds(2 * chip, 2), :, lanes].reshape(2 * TOK, -1)


def _pick_dot(back, rows):
    dims = (((0,), (0,)), ((), ()))
    return lax.dot_general(back, rows, dims, preferred_element_type=F32)[: 2 * ROWS]


def _front_kernel(
    xm, ct, gw, uw, back_out, xr_out, cr_out, wr_out, gu_out, call,
    xall, cbuf, xr, cr, wgu, gu, back, wr,
    ssem, rsem, lsem, wsem, csem, osem, rowsem,
):
    me = lax.axis_index("expert")
    z, x, y, c = _place()
    width, hid = ct.shape[1], gw.shape[2]
    weights = []
    for e in range(2):
        for k, ref in enumerate((gw, uw)):
            cp = pltpu.make_async_copy(ref.at[e], wgu.at[e, :, pl.ds(k * hid, hid)], wsem.at[2 * e + k])
            cp.start()
            weights.append(cp)
    _greet(
        [
            (z, _at(x + 1, y, c)), (z, _at(x - 1, y, c)), (z, _at(x, y + 1, c)), (z, _at(x, y - 1, c)),
            (z, _at(x, y, 1 - c)),
        ]
    )
    sends, keys = [], {}
    gx = _Gather("x", xm, xall, ssem, rsem, sends, keys)
    gc = _Gather("c", ct, call, ssem, rsem, sends, keys)
    own_x = pltpu.make_async_copy(xm, xall.at[gx.mine], lsem.at[0])
    own_c = pltpu.make_async_copy(ct, call.at[gx.mine], lsem.at[1])
    own_x.start()
    own_c.start()
    gx.start()

    def number(shape, dim):
        return lax.broadcasted_iota(jnp.int32, shape, dim)

    def rows_of(dx, dy):
        chip = gx.chip(dx, dy)
        meta = _tokens_of(xall, chip, pl.ds(width, META)).astype(F32)
        tok, lane = number((2 * TOK, META), 0), number((2 * TOK, META), 1)
        hits = []
        for e in range(2):
            match = (meta == (2 * me + e).astype(F32)) & (lane < 8)
            hits.append(jnp.max(jnp.where(match, 1.0, 0.0), axis=1, keepdims=True))
        both = jnp.where(lane == 0, hits[0], jnp.where(lane == 1, hits[1], 0.0)).astype(BF)
        t0, t1 = number((2 * TOK, 2 * TOK), 0), number((2 * TOK, 2 * TOK), 1)
        earlier = ((t1 < t0) & ((t1 < TOK) == (t0 < TOK))).astype(F32).astype(BF)
        before = jnp.dot(earlier, both, preferred_element_type=F32)
        second = lane >= ROWS
        place = lane - jnp.where(second, ROWS, 0)
        late = place >= CAP
        place = place - jnp.where(late, CAP, 0)
        hit = jnp.where(second, hits[1], hits[0])
        spot = jnp.where(second, before[:, 1:2], before[:, 0:1])
        chosen = (hit > 0.5) & (spot == place.astype(F32)) & (late == (tok >= TOK)) & (lane < 2 * ROWS)
        pick = jnp.where(chosen, 1.0, 0.0).astype(BF)
        back[chip] = pick
        rows = _pick_dot(pick, _tokens_of(xall, chip, pl.ds(0, width))).astype(BF)
        at = pl.ds(pl.multiple_of(chip * ROWS, 16), ROWS)
        xr[0, at, :] = rows[:ROWS]
        xr[1, at, :] = rows[ROWS:]
        info = _pick_dot(pick, meta.astype(BF))
        shape = (2 * ROWS, META)
        expert = (2 * me + jnp.where(number(shape, 0) >= ROWS, 1, 0)).astype(F32)
        match = jnp.where((info == expert) & (number(shape, 1) < 8), 1.0, 0.0).astype(BF)
        k0, k1 = number((META, META), 0), number((META, META), 1)
        copies = ((k1 == k0 + 8) | (k1 == k0 + 16) | (k1 == k0 + 24)) & (k0 < 8)
        spread = jnp.dot(match, jnp.where(copies, 1.0, 0.0).astype(BF), preferred_element_type=F32)
        weight = jnp.sum(spread * info, axis=1, keepdims=True)
        wr[chip] = jnp.broadcast_to(weight, shape)

    def drive(gather, work, before=None):
        done, waiting, ready = {(0, 0)}, [], [(0, 0)]
        for n, (o1, o2) in enumerate(EVENTS):
            if before is not None:
                before(n)
            gather.event(o1, o2)
            for chip in waiting:
                work(*chip)
            waiting, ready = ready, []
            done.add((o1, o2))
            if (o2, o1) in done:
                ready = [(o1, o2)] if o1 == o2 else [(o1, o2), (o2, o1)]
        for chip in waiting + ready:
            work(*chip)

    def middle(n):
        if n == 9:
            gc.start()

    own_x.wait()
    drive(gx, rows_of, middle)
    outs = []

    def put(src, dst, sem):
        cp = pltpu.make_async_copy(src, dst, sem)
        cp.start()
        outs.append(cp)

    put(xr, xr_out, osem.at[0])
    put(back, back_out, osem.at[1])
    put(wr, wr_out, osem.at[2])

    def project(e, first, last):
        @pl.loop(first, last)
        def _(j):
            cols = pl.ds(pl.multiple_of(j * 256, 256), 256)
            gu[e, :, cols] = jnp.dot(xr[e], wgu[e, :, cols], preferred_element_type=F32)

    steps = 2 * hid // 256
    units = {2: (0, 0, 2), 4: (0, 2, steps), 6: (1, 0, 2), 8: (1, 2, steps)}

    def compute(n):
        if n in units:
            e, first, last = units[n]
            if first == 0:
                weights[2 * e].wait()
                weights[2 * e + 1].wait()
            project(e, first, last)
            if last == steps:
                put(gu.at[e], gu_out.at[e], osem.at[3 + e])

    own_c.wait()
    fetched = []

    def finish():
        i, chip, cp = fetched.pop(0)
        cp.wait()
        rows = _pick_dot(back[chip], cbuf[i % 3].reshape(2 * TOK, width))
        rows = (rows * wr[chip][:, 0:1]).astype(BF)
        at = pl.ds(pl.multiple_of(chip * ROWS, 16), ROWS)
        for e in range(2):
            cr[e, at, :] = rows[e * ROWS : (e + 1) * ROWS]
            put(cr.at[e, at], cr_out.at[e, at], rowsem.at[2 * i + e])

    count = [0]

    def cot_of(dx, dy):
        chip = gc.chip(dx, dy)
        i = count[0]
        count[0] += 1
        cp = pltpu.make_async_copy(call.at[pl.ds(2 * chip, 2)], cbuf.at[i % 3], csem.at[i % 3])
        cp.start()
        fetched.append((i, chip, cp))
        if len(fetched) > 2:
            finish()

    drive(gc, cot_of, compute)
    while fetched:
        finish()
    for cp in outs:
        cp.wait()
    for cp in sends:
        cp.wait_send()


def _front(xm, ct, gate_proj, up_proj):
    width, hid = ct.shape[1], gate_proj.shape[2]
    hbm = pl.BlockSpec(memory_space=pl.ANY)
    vmem = pl.BlockSpec(memory_space=pltpu.VMEM)
    rows = 32 * CAP
    return pl.pallas_call(
        _front_kernel,
        out_shape=(
            jax.ShapeDtypeStruct((16, 2 * TOK, META), BF),
            jax.ShapeDtypeStruct((2, rows, width), BF),
            jax.ShapeDtypeStruct((2, rows, width), BF),
            jax.ShapeDtypeStruct((16, 2 * ROWS, META), F32),
            jax.ShapeDtypeStruct((2, rows, 2 * hid), F32),
            jax.ShapeDtypeStruct((32, TOK, width), BF),
        ),
        in_specs=[vmem, vmem, hbm, hbm],
        out_specs=(hbm,) * 6,
        scratch_shapes=[
            pltpu.VMEM((32, TOK, width + META), BF),
            pltpu.VMEM((3, 2, TOK, width), BF),
            pltpu.VMEM((2, rows, width), BF),
            pltpu.VMEM((2, rows, width), BF),
            pltpu.VMEM((2, width, 2 * hid), BF),
            pltpu.VMEM((2, rows, 2 * hid), F32),
            pltpu.VMEM((16, 2 * TOK, META), BF),
            pltpu.VMEM((16, 2 * ROWS, META), F32),
            pltpu.SemaphoreType.DMA((144,)),
            pltpu.SemaphoreType.DMA((144,)),
            pltpu.SemaphoreType.DMA((2,)),
            pltpu.SemaphoreType.DMA((4,)),
            pltpu.SemaphoreType.DMA((3,)),
            pltpu.SemaphoreType.DMA((5,)),
            pltpu.SemaphoreType.DMA((32,)),
        ],
        compiler_params=pltpu.CompilerParams(
            collective_id=0, has_side_effects=True, vmem_limit_bytes=63 * 1024 * 1024
        ),
        cost_estimate=pl.CostEstimate(flops=10_000_000_000, bytes_accessed=300_000_000, transcendentals=0),
        name="plane_gather",
    )(xm, ct, gate_proj, up_proj)


def _add(dst, src, n):
    @pl.loop(0, n // 16)
    def _(i):
        rows = pl.ds(pl.multiple_of(i * 16, 16), 16)
        dst[rows, :] = (dst[rows, :].astype(F32) + src[rows, :].astype(F32)).astype(BF)


def _add3(dst, own, one, two, n):
    @pl.loop(0, n // 16)
    def _(i):
        rows = pl.ds(pl.multiple_of(i * 16, 16), 16)
        total = own[rows, :].astype(F32) + one[rows, :].astype(F32) + two[rows, :].astype(F32)
        dst[rows, :] = total.astype(dst.dtype)


OBS = OAS = (2, 1, 3, 0)
LO, HI = pl.ds(0, SUB), pl.ds(SUB, SUB)


class _Reduce:
    def __init__(self, tag, bufs, aside, bsem, out, stage, ssem, rsem, sends, keys):
        self.tag, self.aside, self.bsem, self.out, self.stage = tag, aside, bsem, out, stage
        self.T, self.sb, self.ra, self.rb, self.r2a, self.r2b = bufs
        self.ssem, self.rsem, self.sends, self.keys = ssem, rsem, sends, keys
        self.z, self.x, self.y, self.c = _place()
        self.sib = (self.z, _at(self.x, self.y, 1 - self.c))
        self.width = self.T.shape[-1]
        self.order = [(h, ob, oa) for ob in OBS for oa in OAS for h in (0, 1)]
        self.loads, self.made, self.shared = {}, [], {}

    def remote(self, src, dst, to, *k):
        k = self.keys.setdefault((self.tag,) + k, len(self.keys))
        cp = pltpu.make_async_remote_copy(
            src_ref=src,
            dst_ref=dst,
            send_sem=self.ssem.at[len(self.keys) - 1],
            recv_sem=self.rsem.at[k],
            device_id=to,
            device_id_type=MESH,
        )
        cp.start()
        self.sends.append(cp)
        return cp

    def landed(self, dst, *k):
        pltpu.make_async_remote_copy(
            src_ref=dst,
            dst_ref=dst,
            send_sem=self.ssem.at[0],
            recv_sem=self.rsem.at[self.keys[(self.tag,) + k]],
            device_id=self.sib,
            device_id_type=MESH,
        ).wait_recv()

    def ax(self, h, o):
        return (self.z, _shift(1 - h, self.x, self.y, o, 0, self.c))

    def bx(self, h, o):
        return (self.z, _shift(h, self.x, self.y, o, 0, self.c))

    def chips(self, j, spread):
        for oa in OAS:
            for dx, dy in ((OBS[j], oa), (oa, OBS[j])):
                if (dx, dy) in self.made:
                    continue
                chip = _at(self.x + dx, self.y + dy, 0) // 2
                stage = self.stage.at[len(self.made), :, pl.ds(0, self.width)]
                places = ((0, dx * 4 + dy), (1, dy * 4 + dx))
                spread(chip, 1 - self.c, [(stage.at[pl.ds(h * HALF, HALF)], h) for h in (0, 1)])
                self.shared[len(self.made)] = [
                    self.remote(stage.at[pl.ds(h * HALF, HALF)], self.aside.at[h, k], self.sib, "s", h, k)
                    for h, k in places
                ]
                spread(chip, self.c, [(self.T.at[h, k], h) for h, k in places])
                self.made.append((dx, dy))

    def fetch(self, i):
        h, ob, oa = self.order[i]
        view = self.aside.at[h, ob * 4 + oa]
        self.landed(view, "s", h, ob * 4 + oa)
        cp = pltpu.make_async_copy(view, self.sb.at[i % 3], self.bsem.at[i % 3])
        cp.start()
        self.loads[i] = cp

    def one(self, i):
        h, ob, oa = self.order[i]
        if i == 0:
            self.fetch(0)
        if i + 1 < len(self.order):
            self.fetch(i + 1)
        self.loads[i].wait()
        t = self.T.at[h, ob * 4 + oa]
        _add(t, self.sb.at[i % 3], HALF)
        if oa == 2:
            self.remote(t.at[LO], self.ra.at[h, ob, 0], self.ax(h, 1), "ra", h, ob, 0)
            self.remote(t.at[HI], self.ra.at[h, ob, 1], self.ax(h, -1), "ra", h, ob, 1)
        elif oa == 1:
            self.remote(t.at[HI], self.rb.at[h, ob, 0, HI], self.ax(h, 1), "rd", h, ob, 0)
        elif oa == 3:
            self.remote(t.at[LO], self.rb.at[h, ob, 1, LO], self.ax(h, -1), "rd", h, ob, 1)

    def stage1(self, j):
        for i in range(j * 8, j * 8 + 8):
            self.one(i)

    def stage2(self, j):
        ob = OBS[j]
        for h in (0, 1):
            self.landed(self.ra.at[h, ob, 0], "ra", h, ob, 0)
            t = self.T.at[h, ob * 4 + 1]
            _add(t.at[LO], self.ra.at[h, ob, 0], SUB)
            self.remote(t.at[LO], self.rb.at[h, ob, 0, LO], self.ax(h, 1), "rs", h, ob, 0)
            self.landed(self.ra.at[h, ob, 1], "ra", h, ob, 1)
            t = self.T.at[h, ob * 4 + 3]
            _add(t.at[HI], self.ra.at[h, ob, 1], SUB)
            self.remote(t.at[HI], self.rb.at[h, ob, 1, HI], self.ax(h, -1), "rs", h, ob, 1)

    def stage3(self, j):
        ob = OBS[j]
        for h in (0, 1):
            self.landed(self.rb.at[h, ob, 0, HI], "rd", h, ob, 0)
            self.landed(self.rb.at[h, ob, 1, LO], "rd", h, ob, 1)
            self.landed(self.rb.at[h, ob, 0, LO], "rs", h, ob, 0)
            self.landed(self.rb.at[h, ob, 1, HI], "rs", h, ob, 1)
            t = self.T.at[h, ob * 4]
            _add3(t, t, self.rb.at[h, ob, 0], self.rb.at[h, ob, 1], HALF)
            if ob == 2:
                self.remote(t.at[LO], self.r2a.at[h, 0], self.bx(h, 1), "2a", h, 0)
                self.remote(t.at[HI], self.r2a.at[h, 1], self.bx(h, -1), "2a", h, 1)
            elif ob == 1:
                self.remote(t.at[HI], self.r2b.at[h, 0, HI], self.bx(h, 1), "2d", h, 0)
            elif ob == 3:
                self.remote(t.at[LO], self.r2b.at[h, 1, LO], self.bx(h, -1), "2d", h, 1)

    def stage4(self):
        for h in (0, 1):
            self.landed(self.r2a.at[h, 0], "2a", h, 0)
            t = self.T.at[h, 4]
            _add(t.at[LO], self.r2a.at[h, 0], SUB)
            self.remote(t.at[LO], self.r2b.at[h, 0, LO], self.bx(h, 1), "2s", h, 0)
            self.landed(self.r2a.at[h, 1], "2a", h, 1)
            t = self.T.at[h, 12]
            _add(t.at[HI], self.r2a.at[h, 1], SUB)
            self.remote(t.at[HI], self.r2b.at[h, 1, HI], self.bx(h, -1), "2s", h, 1)

    def stage5(self):
        for h in (0, 1):
            self.landed(self.r2b.at[h, 0, HI], "2d", h, 0)
            self.landed(self.r2b.at[h, 1, LO], "2d", h, 1)
            self.landed(self.r2b.at[h, 0, LO], "2s", h, 0)
            self.landed(self.r2b.at[h, 1, HI], "2s", h, 1)
            rows = self.out.at[pl.ds(h * HALF, HALF)]
            _add3(rows, self.T.at[h, 0], self.r2b.at[h, 0], self.r2b.at[h, 1], HALF)


def _reduce_kernel(
    back_in, y_in, r_in, dg_in, du_in, gw, uw, outy, outd, asidey, asided, *rest
):
    bufy, bufd = rest[:6], rest[6:12]
    stage, rows, back, rr, dcat, wcat, ssem, rsem, bsem, lsem, wsem = rest[12:]
    z, x, y, c = _place()
    width, hid = y_in.shape[2], dg_in.shape[2]

    def load(src, dst, sem):
        cp = pltpu.make_async_copy(src, dst, sem)
        cp.start()
        return cp

    first = [load(back_in, back, lsem.at[0]), load(y_in, rows, lsem.at[1]), load(r_in, rr, lsem.at[2])]
    later = [load(ref, dcat.at[:, :, pl.ds(k * hid, hid)], lsem.at[3 + k]) for k, ref in enumerate((dg_in, du_in))]

    def weights(e):
        return [load(ref.at[e], wcat.at[:, pl.ds(k * hid, hid)], wsem.at[k]) for k, ref in enumerate((gw, uw))]

    later += weights(0)
    _greet(
        [
            (z, _at(x + 1, y, c)), (z, _at(x - 1, y, c)), (z, _at(x, y + 1, c)), (z, _at(x, y - 1, c)),
            (z, _at(x, y, 1 - c)),
        ]
    )
    sends, keys = [], {}
    ry = _Reduce("y", bufy, asidey, bsem.at[0], outy, stage, ssem, rsem, sends, keys)
    rd = _Reduce("d", bufd, asided, bsem.at[1], outd, stage, ssem, rsem, sends, keys)

    def spread(chip, core, places, extra):
        sel = back[chip, pl.ds(pl.multiple_of(core * TOK, TOK), TOK), :][:, : 2 * ROWS]
        at = pl.ds(pl.multiple_of(chip * ROWS, 16), ROWS)

        @pl.loop(0, 4)
        def _(j):
            cols = pl.ds(pl.multiple_of(j * 512, 512), 512)
            both = jnp.concatenate([rows[0, at, cols], rows[1, at, cols]], 0)
            made = jnp.dot(sel, both, preferred_element_type=F32).astype(BF)
            for ref, h in places:
                ref[:, cols] = made[h * HALF : (h + 1) * HALF]

        if extra:
            made = jnp.dot(sel, rr[chip], preferred_element_type=F32).astype(BF)
            for ref, h in places:
                ref[:, pl.ds(width, META)] = made[h * HALF : (h + 1) * HALF]

    def spread_y(chip, core, places):
        spread(chip, core, places, True)

    def spread_d(chip, core, places):
        n = len(rd.made)
        for cp in ry.shared.pop(n, ()):
            cp.wait_send()
            sends[:] = [s for s in sends if s is not cp]
        spread(chip, core, places, False)

    def product(e, j0, j1):
        @pl.loop(j0, j1)
        def _(j):
            at = pl.ds(pl.multiple_of(j * 256, 256), 256)
            dims = (((1,), (1,)), ((), ()))
            made = lax.dot_general(dcat[e], wcat[at, :], dims, preferred_element_type=F32)
            rows[e, :, at] = made.astype(BF)

    for cp in first:
        cp.wait()
    for j in range(4):
        ry.chips(j, spread_y)
        if j >= 1:
            ry.stage1(j - 1)
        if j >= 2:
            ry.stage2(j - 2)
    for cp in later:
        cp.wait()
    n = width // 256
    product(0, 0, n // 2)
    ry.stage1(3)
    ry.stage3(0)
    ry.stage2(2)
    product(0, n // 2, n)
    second = weights(1)
    ry.stage3(1)
    ry.stage2(3)
    for cp in second:
        cp.wait()
    product(1, 0, n // 2)
    ry.stage3(2)
    ry.stage4()
    product(1, n // 2, n)
    rd.chips(0, spread_d)
    rd.chips(1, spread_d)
    rd.stage1(0)
    ry.stage3(3)
    rd.chips(2, spread_d)
    rd.stage1(1)
    ry.stage5()
    rd.stage2(0)
    rd.chips(3, spread_d)
    rd.stage1(2)
    rd.stage2(1)
    rd.stage3(0)
    rd.stage1(3)
    rd.stage2(2)
    rd.stage3(1)
    rd.stage2(3)
    rd.stage3(2)
    rd.stage4()
    rd.stage3(3)
    rd.stage5()
    for cp in sends:
        cp.wait_send()


def _reduce(back, yrows, rrows, d_gate, d_up, gate_proj, up_proj):
    width, hid = yrows.shape[2], d_gate.shape[2]
    hbm = pl.BlockSpec(memory_space=pl.ANY)
    vmem = pl.BlockSpec(memory_space=pltpu.VMEM)

    def buffers(w):
        return [
            pltpu.VMEM((2, 16, HALF, w), BF),
            pltpu.VMEM((3, HALF, w), BF),
            pltpu.VMEM((2, 4, 2, SUB, w), BF),
            pltpu.VMEM((2, 4, 2, HALF, w), BF),
            pltpu.VMEM((2, 2, SUB, w), BF),
            pltpu.VMEM((2, 2, HALF, w), BF),
        ]

    wide = width + META
    return pl.pallas_call(
        _reduce_kernel,
        out_shape=(
            jax.ShapeDtypeStruct((TOK, wide), BF),
            jax.ShapeDtypeStruct((TOK, width), BF),
            jax.ShapeDtypeStruct((2, 16, HALF, wide), BF),
            jax.ShapeDtypeStruct((2, 16, HALF, width), BF),
        ),
        in_specs=[hbm] * 7,
        out_specs=(vmem, vmem, hbm, hbm),
        scratch_shapes=buffers(wide)
        + buffers(width)
        + [
            pltpu.VMEM((16, TOK, wide), BF),
            pltpu.VMEM(yrows.shape, BF),
            pltpu.VMEM(back.shape, BF),
            pltpu.VMEM(rrows.shape, BF),
            pltpu.VMEM((2, 32 * CAP, 2 * hid), BF),
            pltpu.VMEM((width, 2 * hid), BF),
            pltpu.SemaphoreType.DMA((184,)),
            pltpu.SemaphoreType.DMA((184,)),
            pltpu.SemaphoreType.DMA((2, 3)),
            pltpu.SemaphoreType.DMA((5,)),
            pltpu.SemaphoreType.DMA((2,)),
        ],
        compiler_params=pltpu.CompilerParams(
            collective_id=1, has_side_effects=True, vmem_limit_bytes=67_000_000
        ),
        cost_estimate=pl.CostEstimate(flops=12_000_000_000, bytes_accessed=300_000_000, transcendentals=0),
        name="plane_reduce",
    )(back, yrows, rrows, d_gate, d_up, gate_proj, up_proj)


def _grads_kernel(q_ref, x_ref, c_ref, dg_ref, du_ref, h_ref, lo_ref, hi_ref):
    dims = (((0,), (0,)), ((), ()))
    n = lo_ref.shape[2]
    for k, (rows, cots) in enumerate(((x_ref, dg_ref), (x_ref, du_ref), (c_ref, h_ref))):
        g = lax.dot_general(rows[0], cots[0], dims, preferred_element_type=F32).astype(BF)
        lo_ref[k, 0] = g[:n]
        hi_ref[k, 0] = g[n:]


def _grads(quarter, xr, cr, d_gate, d_up, hidden):
    rows, width = xr.shape[1:]
    hid = hidden.shape[2]
    wide = pl.BlockSpec((1, rows, width // 4), lambda e, q: (e, 0, q[0]))
    thin = pl.BlockSpec((1, rows, hid), lambda e, q: (e, 0, 0))
    half = jax.ShapeDtypeStruct((3, 2, width // 8, hid), BF)
    spec = pl.BlockSpec((3, 1, width // 8, hid), lambda e, q: (0, e, 0, 0))
    return pl.pallas_call(
        _grads_kernel,
        grid_spec=pltpu.PrefetchScalarGridSpec(
            num_scalar_prefetch=1, grid=(2,), in_specs=[wide, wide, thin, thin, thin], out_specs=(spec, spec)
        ),
        out_shape=(half, half),
        cost_estimate=pl.CostEstimate(
            flops=12 * rows * (width // 4) * hid, bytes_accessed=14_000_000, transcendentals=0
        ),
        name="grad_quarter",
    )(quarter, xr, cr, d_gate, d_up, hidden)


def _bits(v):
    return lax.reduce_precision(v, 8, 7)


def layer(tokens, routes, route_weights, cotangent, gate_proj, up_proj, down_proj):
    width = tokens.shape[1]
    hid = gate_proj.shape[2]
    me = lax.axis_index("expert")
    w_hi = _bits(route_weights)
    w_mid = _bits(route_weights - w_hi)
    w_lo = route_weights - w_hi - w_mid
    meta = jnp.concatenate(
        [routes.astype(F32), w_hi, w_mid, w_lo, jnp.zeros((TOK, META - 32), F32)], 1
    ).astype(BF)
    mine = 2 * me + jnp.arange(2, dtype=jnp.int32)
    back, xr, cr, wr, gu, _ = _front(jnp.concatenate([tokens, meta], 1), cotangent, gate_proj, up_proj)
    we = wr[:, :, 0].reshape(16, 2, ROWS).transpose(1, 0, 2).reshape(2, 32 * CAP, 1)
    gate_pre, up_pre = gu[:, :, :hid], gu[:, :, hid:]
    sig = jax.nn.sigmoid(gate_pre)
    swish = gate_pre * sig
    d_swish = sig * (1.0 + gate_pre * (1.0 - sig))
    hidden = (swish * up_pre).astype(BF)
    d_hidden = jnp.einsum("erd,ehd->erh", cr, down_proj, preferred_element_type=F32)
    d_gate = (d_hidden * up_pre * d_swish).astype(BF)
    d_up = (d_hidden * swish).astype(BF)
    rw = jnp.sum(d_hidden * hidden.astype(F32), axis=2, keepdims=True) / jnp.where(we > 0, we, 1.0)

    z = lax.axis_index("dp")
    up = [(i, (i + 1) % 4) for i in range(4)]
    down = [(i, (i + 3) % 4) for i in range(4)]

    def quarter(o, after=None):
        which = ((z + o) % 4).reshape(1)
        if after is not None:
            which, _ = lax.optimization_barrier((which, after))
        return _grads(which, xr, cr, d_gate, d_up, hidden)

    def along(v, way):
        return lax.ppermute(v, "dp", way)

    lo2, hi2 = quarter(2)
    far_up, far_down = along(lo2, up), along(hi2, down)
    lo1, hi1 = quarter(1, lo2)
    near_up = along(hi1, up)
    lo3, hi3 = quarter(3, lo2)
    near_down = along(lo3, down)
    lo0, hi0 = quarter(0, lo3)
    yrows = (jnp.einsum("erh,ehd->erd", hidden, down_proj, preferred_element_type=F32) * we).astype(BF)
    lane = jnp.arange(META, dtype=jnp.int32)
    r_hi = _bits(rw)
    r_lo = rw - r_hi
    spot = lane[None, None, :] - mine[:, None, None]
    rrows = jnp.where(spot == 0, r_hi, 0.0) + jnp.where(spot == 64, r_lo, 0.0)
    rrows = rrows.reshape(2, 16, ROWS, META).transpose(1, 0, 2, 3).reshape(16, 2 * ROWS, META).astype(BF)

    def plus(one, two):
        return (one.astype(F32) + two.astype(F32)).astype(BF)

    lo1, hi3, lo0, hi0 = lax.optimization_barrier((lo1, hi3, lo0, hi0))
    sum_up = along(plus(lo1, far_up), up)
    sum_down = along(plus(hi3, far_down), down)
    out, dx, _, _ = _reduce(back, yrows, rrows, d_gate, d_up, gate_proj, up_proj)

    def total(one, two, three):
        return one.astype(F32) + two.astype(F32) + three.astype(F32)

    shares = jnp.concatenate([total(lo0, sum_up, near_down), total(hi0, near_up, sum_down)], 2)
    table = out[:, width : width + 64].astype(F32) + out[:, width + 64 :].astype(F32)
    onehot = routes[:, :, None] == jnp.arange(64, dtype=jnp.int32)[None, None, :]
    weight_grad = jnp.sum(jnp.where(onehot, table[:, None, :], 0.0), axis=2)

    def final(g):
        return jnp.transpose(g, (1, 0, 2))

    return (out[:, :width], dx, weight_grad, final(shares[0]), final(shares[1]), final(shares[2]))


def solution(mesh):
    rows = P(("dp", "expert"), None)
    experts = P("expert", None, None)
    grads = P("dp", "expert", None)
    return jax.shard_map(
        layer,
        mesh=mesh,
        in_specs=(rows, rows, rows, rows, experts, experts, experts),
        out_specs=(rows, rows, rows, grads, grads, grads),
        check_vma=False,
    )
```

```python
import jax
import jax.numpy as jnp
from jax import lax
from jax.experimental import pallas as pl
from jax.experimental.pallas import tpu as pltpu
from jax.sharding import PartitionSpec as P

MESH = pl.DeviceIdType.MESH
BF = jnp.bfloat16
F32 = jnp.float32
TOK = 128
HALF = 64
SUB = 32
CAP = 24
META = 128


def _place():
    me = lax.axis_index("expert")
    return lax.axis_index("dp"), me // 8, (me // 2) % 4, me % 2


def _at(x, y, c):
    return ((x + 8) % 4) * 8 + ((y + 8) % 4) * 2 + c


def _greet(peers):
    barrier = pltpu.get_barrier_semaphore()
    for peer in peers:
        pl.semaphore_signal(barrier, inc=1, device_id=peer, device_id_type=MESH)
    pl.semaphore_wait(barrier, len(peers))


def _shift(h, x, y, o1, o2, c):
    return _at(x + o1, y + o2, c) if h == 0 else _at(x + o2, y + o1, c)


class _Gather:
    def __init__(self, tag, blk, out, ssem, rsem, sends, keys):
        self.tag, self.blk, self.out, self.ssem, self.rsem = tag, blk, out, ssem, rsem
        self.sends, self.keys = sends, keys
        self.z, self.x, self.y, self.c = _place()
        self.mine = _at(self.x, self.y, self.c)
        self.sib = _at(self.x, self.y, 1 - self.c)

    def shift(self, h, o1, o2):
        return _shift(h, self.x, self.y, o1, o2, self.c)

    def send(self, slot, row, n, to, *k):
        k = self.keys.setdefault((self.tag,) + k, len(self.keys))
        src = self.blk.at[pl.ds(row, n)] if slot is None else self.out.at[slot, pl.ds(row, n)]
        cp = pltpu.make_async_remote_copy(
            src_ref=src,
            dst_ref=self.out.at[self.mine if slot is None else slot, pl.ds(row, n)],
            send_sem=self.ssem.at[len(self.sends)],
            recv_sem=self.rsem.at[k],
            device_id=(self.z, to),
            device_id_type=MESH,
        )
        cp.start()
        self.sends.append(cp)

    def landed(self, slot, row, n, *k):
        k = self.keys[(self.tag,) + k]
        view = self.out.at[slot, pl.ds(row, n)]
        pltpu.make_async_remote_copy(
            src_ref=view,
            dst_ref=view,
            send_sem=self.ssem.at[0],
            recv_sem=self.rsem.at[k],
            device_id=(self.z, self.sib),
            device_id_type=MESH,
        ).wait_recv()

    def line(self, h, o1, slot):
        self.send(slot, h * HALF, HALF, self.shift(h, 0, 1), h, "G+", o1)
        self.send(slot, h * HALF, HALF, self.shift(h, 0, -1), h, "G-", o1)

    def aside(self, h, o1, o2, slot):
        self.send(slot, h * HALF, HALF, self.sib, h, "S", o1, o2)

    def start(self):
        for h in (0, 1):
            self.send(None, h * HALF, HALF, self.shift(h, 1, 0), h, "F+")
            self.send(None, h * HALF, HALF, self.shift(h, -1, 0), h, "F-")
            self.line(h, 0, None)
            self.aside(h, 0, 0, None)

    def first(self, h, o):
        slot, sign = self.shift(h, o, 0), "+" if o < 0 else "-"
        self.landed(slot, h * HALF, HALF, h, "F" + sign)
        self.send(slot, h * HALF + (0 if o < 0 else SUB), SUB, self.shift(h, -o, 0), h, "FF" + sign)
        self.line(h, o, slot)
        self.aside(h, o, 0, slot)

    def far(self, h):
        slot = self.shift(h, 2, 0)
        self.landed(slot, h * HALF, SUB, h, "FF+")
        self.landed(slot, h * HALF + SUB, SUB, h, "FF-")
        self.line(h, 2, slot)
        self.aside(h, 2, 0, slot)

    def second(self, h, o1, o):
        slot, sign = self.shift(h, o1, o), "+" if o < 0 else "-"
        self.landed(slot, h * HALF, HALF, h, "G" + sign, o1)
        self.send(slot, h * HALF + (0 if o < 0 else SUB), SUB, self.shift(h, 0, -o), h, "GF" + sign, o1)
        self.aside(h, o1, o, slot)

    def corner(self, h, o1):
        slot = self.shift(h, o1, 2)
        self.landed(slot, h * HALF, SUB, h, "GF+", o1)
        self.landed(slot, h * HALF + SUB, SUB, h, "GF-", o1)
        self.aside(h, o1, 2, slot)

    def event(self, o1, o2):
        for h in (0, 1):
            if o2 == 0:
                self.far(h) if o1 == 2 else self.first(h, o1)
            elif o2 == 2:
                self.corner(h, o1)
            else:
                self.second(h, o1, o2)

    def chip(self, dx, dy):
        for h, o1, o2 in ((0, dx, dy), (1, dy, dx)):
            slot = _at(self.x + dx, self.y + dy, 1 - self.c)
            self.landed(slot, h * HALF, HALF, h, "S", o1, o2)
        return _at(self.x + dx, self.y + dy, 0) // 2


EVENTS = (
    (-1, 0), (1, 0), (0, -1), (0, 1), (2, 0), (-1, -1), (-1, 1), (1, -1), (1, 1),
    (0, 2), (2, -1), (2, 1), (-1, 2), (1, 2), (2, 2),
)
ROWS = 2 * CAP


def _tokens_of(ref, chip, lanes):
    return ref[pl.ds(2 * chip, 2), :, lanes].reshape(2 * TOK, -1)


def _pick_dot(back, rows):
    dims = (((0,), (0,)), ((), ()))
    return lax.dot_general(back, rows, dims, preferred_element_type=F32)[: 2 * ROWS]


def _front_kernel(
    xm, ct, gw, uw, back_out, xr_out, cr_out, wr_out, gu_out, call,
    xall, cbuf, xr, cr, wgu, gu, back, wr,
    ssem, rsem, lsem, wsem, csem, osem, rowsem,
):
    me = lax.axis_index("expert")
    z, x, y, c = _place()
    width, hid = ct.shape[1], gw.shape[2]
    weights = []
    for e in range(2):
        for k, ref in enumerate((gw, uw)):
            cp = pltpu.make_async_copy(ref.at[e], wgu.at[e, :, pl.ds(k * hid, hid)], wsem.at[2 * e + k])
            cp.start()
            weights.append(cp)
    _greet(
        [
            (z, _at(x + 1, y, c)), (z, _at(x - 1, y, c)), (z, _at(x, y + 1, c)), (z, _at(x, y - 1, c)),
            (z, _at(x, y, 1 - c)),
        ]
    )
    sends, keys = [], {}
    gx = _Gather("x", xm, xall, ssem, rsem, sends, keys)
    gc = _Gather("c", ct, call, ssem, rsem, sends, keys)
    own_x = pltpu.make_async_copy(xm, xall.at[gx.mine], lsem.at[0])
    own_c = pltpu.make_async_copy(ct, call.at[gx.mine], lsem.at[1])
    own_x.start()
    own_c.start()
    gx.start()

    def number(shape, dim):
        return lax.broadcasted_iota(jnp.int32, shape, dim)

    def rows_of(dx, dy):
        chip = gx.chip(dx, dy)
        meta = _tokens_of(xall, chip, pl.ds(width, META)).astype(F32)
        tok, lane = number((2 * TOK, META), 0), number((2 * TOK, META), 1)
        hits = []
        for e in range(2):
            match = (meta == (2 * me + e).astype(F32)) & (lane < 8)
            hits.append(jnp.max(jnp.where(match, 1.0, 0.0), axis=1, keepdims=True))
        both = jnp.where(lane == 0, hits[0], jnp.where(lane == 1, hits[1], 0.0)).astype(BF)
        t0, t1 = number((2 * TOK, 2 * TOK), 0), number((2 * TOK, 2 * TOK), 1)
        earlier = ((t1 < t0) & ((t1 < TOK) == (t0 < TOK))).astype(F32).astype(BF)
        before = jnp.dot(earlier, both, preferred_element_type=F32)
        second = lane >= ROWS
        place = lane - jnp.where(second, ROWS, 0)
        late = place >= CAP
        place = place - jnp.where(late, CAP, 0)
        hit = jnp.where(second, hits[1], hits[0])
        spot = jnp.where(second, before[:, 1:2], before[:, 0:1])
        chosen = (hit > 0.5) & (spot == place.astype(F32)) & (late == (tok >= TOK)) & (lane < 2 * ROWS)
        pick = jnp.where(chosen, 1.0, 0.0).astype(BF)
        back[chip] = pick
        rows = _pick_dot(pick, _tokens_of(xall, chip, pl.ds(0, width))).astype(BF)
        at = pl.ds(pl.multiple_of(chip * ROWS, 16), ROWS)
        xr[0, at, :] = rows[:ROWS]
        xr[1, at, :] = rows[ROWS:]
        info = _pick_dot(pick, meta.astype(BF))
        shape = (2 * ROWS, META)
        expert = (2 * me + jnp.where(number(shape, 0) >= ROWS, 1, 0)).astype(F32)
        match = jnp.where((info == expert) & (number(shape, 1) < 8), 1.0, 0.0).astype(BF)
        k0, k1 = number((META, META), 0), number((META, META), 1)
        copies = ((k1 == k0 + 8) | (k1 == k0 + 16) | (k1 == k0 + 24)) & (k0 < 8)
        spread = jnp.dot(match, jnp.where(copies, 1.0, 0.0).astype(BF), preferred_element_type=F32)
        weight = jnp.sum(spread * info, axis=1, keepdims=True)
        wr[chip] = jnp.broadcast_to(weight, shape)

    def drive(gather, work, before=None):
        done, waiting, ready = {(0, 0)}, [], [(0, 0)]
        for n, (o1, o2) in enumerate(EVENTS):
            if before is not None:
                before(n)
            gather.event(o1, o2)
            for chip in waiting:
                work(*chip)
            waiting, ready = ready, []
            done.add((o1, o2))
            if (o2, o1) in done:
                ready = [(o1, o2)] if o1 == o2 else [(o1, o2), (o2, o1)]
        for chip in waiting + ready:
            work(*chip)

    def middle(n):
        if n == 9:
            gc.start()

    own_x.wait()
    drive(gx, rows_of, middle)
    outs = []

    def put(src, dst, sem):
        cp = pltpu.make_async_copy(src, dst, sem)
        cp.start()
        outs.append(cp)

    put(xr, xr_out, osem.at[0])
    put(back, back_out, osem.at[1])
    put(wr, wr_out, osem.at[2])

    def project(e, first, last):
        @pl.loop(first, last)
        def _(j):
            cols = pl.ds(pl.multiple_of(j * 256, 256), 256)
            gu[e, :, cols] = jnp.dot(xr[e], wgu[e, :, cols], preferred_element_type=F32)

    steps = 2 * hid // 256
    units = {2: (0, 0, 2), 4: (0, 2, steps), 6: (1, 0, 2), 8: (1, 2, steps)}

    def compute(n):
        if n in units:
            e, first, last = units[n]
            if first == 0:
                weights[2 * e].wait()
                weights[2 * e + 1].wait()
            project(e, first, last)
            if last == steps:
                put(gu.at[e], gu_out.at[e], osem.at[3 + e])

    own_c.wait()
    fetched = []

    def finish():
        i, chip, cp = fetched.pop(0)
        cp.wait()
        rows = _pick_dot(back[chip], cbuf[i % 3].reshape(2 * TOK, width))
        rows = (rows * wr[chip][:, 0:1]).astype(BF)
        at = pl.ds(pl.multiple_of(chip * ROWS, 16), ROWS)
        for e in range(2):
            cr[e, at, :] = rows[e * ROWS : (e + 1) * ROWS]
            put(cr.at[e, at], cr_out.at[e, at], rowsem.at[2 * i + e])

    count = [0]

    def cot_of(dx, dy):
        chip = gc.chip(dx, dy)
        i = count[0]
        count[0] += 1
        cp = pltpu.make_async_copy(call.at[pl.ds(2 * chip, 2)], cbuf.at[i % 3], csem.at[i % 3])
        cp.start()
        fetched.append((i, chip, cp))
        if len(fetched) > 2:
            finish()

    drive(gc, cot_of, compute)
    while fetched:
        finish()
    for cp in outs:
        cp.wait()
    for cp in sends:
        cp.wait_send()


def _front(xm, ct, gate_proj, up_proj):
    width, hid = ct.shape[1], gate_proj.shape[2]
    hbm = pl.BlockSpec(memory_space=pl.ANY)
    vmem = pl.BlockSpec(memory_space=pltpu.VMEM)
    rows = 32 * CAP
    return pl.pallas_call(
        _front_kernel,
        out_shape=(
            jax.ShapeDtypeStruct((16, 2 * TOK, META), BF),
            jax.ShapeDtypeStruct((2, rows, width), BF),
            jax.ShapeDtypeStruct((2, rows, width), BF),
            jax.ShapeDtypeStruct((16, 2 * ROWS, META), F32),
            jax.ShapeDtypeStruct((2, rows, 2 * hid), F32),
            jax.ShapeDtypeStruct((32, TOK, width), BF),
        ),
        in_specs=[vmem, vmem, hbm, hbm],
        out_specs=(hbm,) * 6,
        scratch_shapes=[
            pltpu.VMEM((32, TOK, width + META), BF),
            pltpu.VMEM((3, 2, TOK, width), BF),
            pltpu.VMEM((2, rows, width), BF),
            pltpu.VMEM((2, rows, width), BF),
            pltpu.VMEM((2, width, 2 * hid), BF),
            pltpu.VMEM((2, rows, 2 * hid), F32),
            pltpu.VMEM((16, 2 * TOK, META), BF),
            pltpu.VMEM((16, 2 * ROWS, META), F32),
            pltpu.SemaphoreType.DMA((144,)),
            pltpu.SemaphoreType.DMA((144,)),
            pltpu.SemaphoreType.DMA((2,)),
            pltpu.SemaphoreType.DMA((4,)),
            pltpu.SemaphoreType.DMA((3,)),
            pltpu.SemaphoreType.DMA((5,)),
            pltpu.SemaphoreType.DMA((32,)),
        ],
        compiler_params=pltpu.CompilerParams(
            collective_id=0, has_side_effects=True, vmem_limit_bytes=63 * 1024 * 1024
        ),
        cost_estimate=pl.CostEstimate(flops=10_000_000_000, bytes_accessed=300_000_000, transcendentals=0),
        name="plane_gather",
    )(xm, ct, gate_proj, up_proj)


def _add(dst, src, n):
    @pl.loop(0, n // 16)
    def _(i):
        rows = pl.ds(pl.multiple_of(i * 16, 16), 16)
        dst[rows, :] = (dst[rows, :].astype(F32) + src[rows, :].astype(F32)).astype(BF)


def _add3(dst, own, one, two, n):
    @pl.loop(0, n // 16)
    def _(i):
        rows = pl.ds(pl.multiple_of(i * 16, 16), 16)
        total = own[rows, :].astype(F32) + one[rows, :].astype(F32) + two[rows, :].astype(F32)
        dst[rows, :] = total.astype(dst.dtype)


OBS = OAS = (2, 1, 3, 0)
LO, HI = pl.ds(0, SUB), pl.ds(SUB, SUB)


class _Reduce:
    def __init__(self, tag, bufs, aside, bsem, out, stage, ssem, rsem, sends, keys):
        self.tag, self.aside, self.bsem, self.out, self.stage = tag, aside, bsem, out, stage
        self.T, self.sb, self.ra, self.rb, self.r2a, self.r2b = bufs
        self.ssem, self.rsem, self.sends, self.keys = ssem, rsem, sends, keys
        self.z, self.x, self.y, self.c = _place()
        self.sib = (self.z, _at(self.x, self.y, 1 - self.c))
        self.width = self.T.shape[-1]
        self.order = [(h, ob, oa) for ob in OBS for oa in OAS for h in (0, 1)]
        self.loads, self.made, self.shared = {}, [], {}

    def remote(self, src, dst, to, *k):
        k = self.keys.setdefault((self.tag,) + k, len(self.keys))
        cp = pltpu.make_async_remote_copy(
            src_ref=src,
            dst_ref=dst,
            send_sem=self.ssem.at[len(self.keys) - 1],
            recv_sem=self.rsem.at[k],
            device_id=to,
            device_id_type=MESH,
        )
        cp.start()
        self.sends.append(cp)
        return cp

    def landed(self, dst, *k):
        pltpu.make_async_remote_copy(
            src_ref=dst,
            dst_ref=dst,
            send_sem=self.ssem.at[0],
            recv_sem=self.rsem.at[self.keys[(self.tag,) + k]],
            device_id=self.sib,
            device_id_type=MESH,
        ).wait_recv()

    def ax(self, h, o):
        return (self.z, _shift(1 - h, self.x, self.y, o, 0, self.c))

    def bx(self, h, o):
        return (self.z, _shift(h, self.x, self.y, o, 0, self.c))

    def make(self, dx, dy):
        if (dx, dy) in self.made:
            return
        chip = _at(self.x + dx, self.y + dy, 0) // 2
        stage = self.stage.at[len(self.made), :, pl.ds(0, self.width)]
        places = ((0, dx * 4 + dy), (1, dy * 4 + dx))
        self.spread(chip, 1 - self.c, [(stage.at[pl.ds(h * HALF, HALF)], h) for h in (0, 1)])
        self.shared[len(self.made)] = [
            self.remote(stage.at[pl.ds(h * HALF, HALF)], self.aside.at[h, k], self.sib, "s", h, k)
            for h, k in places
        ]
        self.spread(chip, self.c, [(self.T.at[h, k], h) for h, k in places])
        self.made.append((dx, dy))

    def fetch(self, i):
        h, ob, oa = self.order[i]
        view = self.aside.at[h, ob * 4 + oa]
        self.landed(view, "s", h, ob * 4 + oa)
        cp = pltpu.make_async_copy(view, self.sb.at[i % 3], self.bsem.at[i % 3])
        cp.start()
        self.loads[i] = cp

    def one(self, i):
        h, ob, oa = self.order[i]
        if i == 0:
            self.fetch(0)
        if i + 1 < len(self.order):
            self.fetch(i + 1)
        self.loads[i].wait()
        t = self.T.at[h, ob * 4 + oa]
        _add(t, self.sb.at[i % 3], HALF)
        if oa == 2:
            self.remote(t.at[LO], self.ra.at[h, ob, 0], self.ax(h, 1), "ra", h, ob, 0)
            self.remote(t.at[HI], self.ra.at[h, ob, 1], self.ax(h, -1), "ra", h, ob, 1)
        elif oa == 1:
            self.remote(t.at[HI], self.rb.at[h, ob, 0, HI], self.ax(h, 1), "rd", h, ob, 0)
        elif oa == 3:
            self.remote(t.at[LO], self.rb.at[h, ob, 1, LO], self.ax(h, -1), "rd", h, ob, 1)

    def stage1(self, j):
        for i in range(j * 8, j * 8 + 8):
            for h, ob, oa in self.order[i : i + 5]:
                self.make(*((ob, oa) if h == 0 else (oa, ob)))
            self.one(i)

    def stage2(self, j):
        ob = OBS[j]
        for h in (0, 1):
            self.landed(self.ra.at[h, ob, 0], "ra", h, ob, 0)
            t = self.T.at[h, ob * 4 + 1]
            _add(t.at[LO], self.ra.at[h, ob, 0], SUB)
            self.remote(t.at[LO], self.rb.at[h, ob, 0, LO], self.ax(h, 1), "rs", h, ob, 0)
            self.landed(self.ra.at[h, ob, 1], "ra", h, ob, 1)
            t = self.T.at[h, ob * 4 + 3]
            _add(t.at[HI], self.ra.at[h, ob, 1], SUB)
            self.remote(t.at[HI], self.rb.at[h, ob, 1, HI], self.ax(h, -1), "rs", h, ob, 1)

    def stage3(self, j):
        ob = OBS[j]
        for h in (0, 1):
            self.landed(self.rb.at[h, ob, 0, HI], "rd", h, ob, 0)
            self.landed(self.rb.at[h, ob, 1, LO], "rd", h, ob, 1)
            self.landed(self.rb.at[h, ob, 0, LO], "rs", h, ob, 0)
            self.landed(self.rb.at[h, ob, 1, HI], "rs", h, ob, 1)
            t = self.T.at[h, ob * 4]
            _add3(t, t, self.rb.at[h, ob, 0], self.rb.at[h, ob, 1], HALF)
            if ob == 2:
                self.remote(t.at[LO], self.r2a.at[h, 0], self.bx(h, 1), "2a", h, 0)
                self.remote(t.at[HI], self.r2a.at[h, 1], self.bx(h, -1), "2a", h, 1)
            elif ob == 1:
                self.remote(t.at[HI], self.r2b.at[h, 0, HI], self.bx(h, 1), "2d", h, 0)
            elif ob == 3:
                self.remote(t.at[LO], self.r2b.at[h, 1, LO], self.bx(h, -1), "2d", h, 1)

    def stage4(self):
        for h in (0, 1):
            self.landed(self.r2a.at[h, 0], "2a", h, 0)
            t = self.T.at[h, 4]
            _add(t.at[LO], self.r2a.at[h, 0], SUB)
            self.remote(t.at[LO], self.r2b.at[h, 0, LO], self.bx(h, 1), "2s", h, 0)
            self.landed(self.r2a.at[h, 1], "2a", h, 1)
            t = self.T.at[h, 12]
            _add(t.at[HI], self.r2a.at[h, 1], SUB)
            self.remote(t.at[HI], self.r2b.at[h, 1, HI], self.bx(h, -1), "2s", h, 1)

    def stage5(self):
        for h in (0, 1):
            self.landed(self.r2b.at[h, 0, HI], "2d", h, 0)
            self.landed(self.r2b.at[h, 1, LO], "2d", h, 1)
            self.landed(self.r2b.at[h, 0, LO], "2s", h, 0)
            self.landed(self.r2b.at[h, 1, HI], "2s", h, 1)
            rows = self.out.at[pl.ds(h * HALF, HALF)]
            _add3(rows, self.T.at[h, 0], self.r2b.at[h, 0], self.r2b.at[h, 1], HALF)


def _reduce_kernel(
    back_in, y_in, r_in, dg_in, du_in, gw, uw, outy, outd, asidey, asided, *rest
):
    bufy, bufd = rest[:6], rest[6:12]
    stage, rows, back, rr, dcat, wcat, ssem, rsem, bsem, lsem, wsem = rest[12:]
    z, x, y, c = _place()
    width, hid = y_in.shape[2], dg_in.shape[2]

    def load(src, dst, sem):
        cp = pltpu.make_async_copy(src, dst, sem)
        cp.start()
        return cp

    first = [load(back_in, back, lsem.at[0]), load(y_in, rows, lsem.at[1]), load(r_in, rr, lsem.at[2])]
    later = [load(ref, dcat.at[:, :, pl.ds(k * hid, hid)], lsem.at[3 + k]) for k, ref in enumerate((dg_in, du_in))]

    def weights(e):
        return [load(ref.at[e], wcat.at[:, pl.ds(k * hid, hid)], wsem.at[k]) for k, ref in enumerate((gw, uw))]

    later += weights(0)
    _greet(
        [
            (z, _at(x + 1, y, c)), (z, _at(x - 1, y, c)), (z, _at(x, y + 1, c)), (z, _at(x, y - 1, c)),
            (z, _at(x, y, 1 - c)),
        ]
    )
    sends, keys = [], {}
    ry = _Reduce("y", bufy, asidey, bsem.at[0], outy, stage, ssem, rsem, sends, keys)
    rd = _Reduce("d", bufd, asided, bsem.at[1], outd, stage, ssem, rsem, sends, keys)

    def spread(chip, core, places, extra):
        sel = back[chip, pl.ds(pl.multiple_of(core * TOK, TOK), TOK), :][:, : 2 * ROWS]
        at = pl.ds(pl.multiple_of(chip * ROWS, 16), ROWS)

        @pl.loop(0, 4)
        def _(j):
            cols = pl.ds(pl.multiple_of(j * 512, 512), 512)
            both = jnp.concatenate([rows[0, at, cols], rows[1, at, cols]], 0)
            made = jnp.dot(sel, both, preferred_element_type=F32).astype(BF)
            for ref, h in places:
                ref[:, cols] = made[h * HALF : (h + 1) * HALF]

        if extra:
            made = jnp.dot(sel, rr[chip], preferred_element_type=F32).astype(BF)
            for ref, h in places:
                ref[:, pl.ds(width, META)] = made[h * HALF : (h + 1) * HALF]

    def spread_y(chip, core, places):
        spread(chip, core, places, True)

    ry.spread = spread_y

    def spread_d(chip, core, places):
        n = len(rd.made)
        for cp in ry.shared.pop(n, ()):
            cp.wait_send()
            sends[:] = [s for s in sends if s is not cp]
        spread(chip, core, places, False)

    rd.spread = spread_d

    def product(e, j0, j1):
        @pl.loop(j0, j1)
        def _(j):
            at = pl.ds(pl.multiple_of(j * 256, 256), 256)
            dims = (((1,), (1,)), ((), ()))
            made = lax.dot_general(dcat[e], wcat[at, :], dims, preferred_element_type=F32)
            rows[e, :, at] = made.astype(BF)

    for cp in first:
        cp.wait()
    n = width // 256
    ry.stage1(0)
    ry.stage1(1)
    for h, ob, oa in ry.order:
        ry.make(*((ob, oa) if h == 0 else (oa, ob)))
    for cp in later:
        cp.wait()
    product(0, 0, n // 2)
    ry.stage1(2)
    ry.stage2(0)
    product(0, n // 2, n)
    second = weights(1)
    ry.stage1(3)
    ry.stage2(1)
    for cp in second:
        cp.wait()
    product(1, 0, n // 2)
    ry.stage2(2)
    product(1, n // 2, n)
    rd.stage1(0)
    ry.stage3(0)
    ry.stage2(3)
    rd.stage1(1)
    ry.stage3(1)
    rd.stage2(0)
    rd.stage1(2)
    ry.stage3(2)
    ry.stage4()
    rd.stage2(1)
    rd.stage1(3)
    ry.stage3(3)
    ry.stage5()
    rd.stage2(2)
    rd.stage3(0)
    rd.stage2(3)
    rd.stage3(1)
    rd.stage3(2)
    rd.stage4()
    rd.stage3(3)
    rd.stage5()
    for cp in sends:
        cp.wait_send()


def _reduce(back, yrows, rrows, d_gate, d_up, gate_proj, up_proj):
    width, hid = yrows.shape[2], d_gate.shape[2]
    hbm = pl.BlockSpec(memory_space=pl.ANY)
    vmem = pl.BlockSpec(memory_space=pltpu.VMEM)

    def buffers(w):
        return [
            pltpu.VMEM((2, 16, HALF, w), BF),
            pltpu.VMEM((3, HALF, w), BF),
            pltpu.VMEM((2, 4, 2, SUB, w), BF),
            pltpu.VMEM((2, 4, 2, HALF, w), BF),
            pltpu.VMEM((2, 2, SUB, w), BF),
            pltpu.VMEM((2, 2, HALF, w), BF),
        ]

    wide = width + META
    return pl.pallas_call(
        _reduce_kernel,
        out_shape=(
            jax.ShapeDtypeStruct((TOK, wide), BF),
            jax.ShapeDtypeStruct((TOK, width), BF),
            jax.ShapeDtypeStruct((2, 16, HALF, wide), BF),
            jax.ShapeDtypeStruct((2, 16, HALF, width), BF),
        ),
        in_specs=[hbm] * 7,
        out_specs=(vmem, vmem, hbm, hbm),
        scratch_shapes=buffers(wide)
        + buffers(width)
        + [
            pltpu.VMEM((16, TOK, wide), BF),
            pltpu.VMEM(yrows.shape, BF),
            pltpu.VMEM(back.shape, BF),
            pltpu.VMEM(rrows.shape, BF),
            pltpu.VMEM((2, 32 * CAP, 2 * hid), BF),
            pltpu.VMEM((width, 2 * hid), BF),
            pltpu.SemaphoreType.DMA((184,)),
            pltpu.SemaphoreType.DMA((184,)),
            pltpu.SemaphoreType.DMA((2, 3)),
            pltpu.SemaphoreType.DMA((5,)),
            pltpu.SemaphoreType.DMA((2,)),
        ],
        compiler_params=pltpu.CompilerParams(
            collective_id=1, has_side_effects=True, vmem_limit_bytes=67_000_000
        ),
        cost_estimate=pl.CostEstimate(flops=12_000_000_000, bytes_accessed=300_000_000, transcendentals=0),
        name="plane_reduce",
    )(back, yrows, rrows, d_gate, d_up, gate_proj, up_proj)


def _grads_kernel(q_ref, x_ref, c_ref, dg_ref, du_ref, h_ref, lo_ref, hi_ref):
    dims = (((0,), (0,)), ((), ()))
    n = lo_ref.shape[2]
    for k, (rows, cots) in enumerate(((x_ref, dg_ref), (x_ref, du_ref), (c_ref, h_ref))):
        g = lax.dot_general(rows[0], cots[0], dims, preferred_element_type=F32).astype(BF)
        lo_ref[k, 0] = g[:n]
        hi_ref[k, 0] = g[n:]


def _grads(quarter, xr, cr, d_gate, d_up, hidden):
    rows, width = xr.shape[1:]
    hid = hidden.shape[2]
    wide = pl.BlockSpec((1, rows, width // 4), lambda e, q: (e, 0, q[0]))
    thin = pl.BlockSpec((1, rows, hid), lambda e, q: (e, 0, 0))
    half = jax.ShapeDtypeStruct((3, 2, width // 8, hid), BF)
    spec = pl.BlockSpec((3, 1, width // 8, hid), lambda e, q: (0, e, 0, 0))
    return pl.pallas_call(
        _grads_kernel,
        grid_spec=pltpu.PrefetchScalarGridSpec(
            num_scalar_prefetch=1, grid=(2,), in_specs=[wide, wide, thin, thin, thin], out_specs=(spec, spec)
        ),
        out_shape=(half, half),
        cost_estimate=pl.CostEstimate(
            flops=12 * rows * (width // 4) * hid, bytes_accessed=14_000_000, transcendentals=0
        ),
        name="grad_quarter",
    )(quarter, xr, cr, d_gate, d_up, hidden)


def _bits(v):
    return lax.reduce_precision(v, 8, 7)


def layer(tokens, routes, route_weights, cotangent, gate_proj, up_proj, down_proj):
    width = tokens.shape[1]
    hid = gate_proj.shape[2]
    me = lax.axis_index("expert")
    w_hi = _bits(route_weights)
    w_mid = _bits(route_weights - w_hi)
    w_lo = route_weights - w_hi - w_mid
    meta = jnp.concatenate(
        [routes.astype(F32), w_hi, w_mid, w_lo, jnp.zeros((TOK, META - 32), F32)], 1
    ).astype(BF)
    mine = 2 * me + jnp.arange(2, dtype=jnp.int32)
    back, xr, cr, wr, gu, _ = _front(jnp.concatenate([tokens, meta], 1), cotangent, gate_proj, up_proj)
    we = wr[:, :, 0].reshape(16, 2, ROWS).transpose(1, 0, 2).reshape(2, 32 * CAP, 1)
    gate_pre, up_pre = gu[:, :, :hid], gu[:, :, hid:]
    sig = jax.nn.sigmoid(gate_pre)
    swish = gate_pre * sig
    d_swish = sig * (1.0 + gate_pre * (1.0 - sig))
    hidden = (swish * up_pre).astype(BF)
    d_hidden = jnp.einsum("erd,ehd->erh", cr, down_proj, preferred_element_type=F32)
    d_gate = (d_hidden * up_pre * d_swish).astype(BF)
    d_up = (d_hidden * swish).astype(BF)
    rw = jnp.sum(d_hidden * hidden.astype(F32), axis=2, keepdims=True) / jnp.where(we > 0, we, 1.0)

    z = lax.axis_index("dp")
    up = [(i, (i + 1) % 4) for i in range(4)]
    down = [(i, (i + 3) % 4) for i in range(4)]

    def quarter(o, after=None):
        which = ((z + o) % 4).reshape(1)
        if after is not None:
            which, _ = lax.optimization_barrier((which, after))
        return _grads(which, xr, cr, d_gate, d_up, hidden)

    def along(v, way):
        return lax.ppermute(v, "dp", way)

    lo2, hi2 = quarter(2)
    far_up, far_down = along(lo2, up), along(hi2, down)
    lo1, hi1 = quarter(1, lo2)
    near_up = along(hi1, up)
    lo3, hi3 = quarter(3, lo2)
    near_down = along(lo3, down)
    lo0, hi0 = quarter(0, lo3)
    yrows = (jnp.einsum("erh,ehd->erd", hidden, down_proj, preferred_element_type=F32) * we).astype(BF)
    lane = jnp.arange(META, dtype=jnp.int32)
    r_hi = _bits(rw)
    r_lo = rw - r_hi
    spot = lane[None, None, :] - mine[:, None, None]
    rrows = jnp.where(spot == 0, r_hi, 0.0) + jnp.where(spot == 64, r_lo, 0.0)
    rrows = rrows.reshape(2, 16, ROWS, META).transpose(1, 0, 2, 3).reshape(16, 2 * ROWS, META).astype(BF)

    def plus(one, two):
        return (one.astype(F32) + two.astype(F32)).astype(BF)

    lo1, hi3, lo0, hi0 = lax.optimization_barrier((lo1, hi3, lo0, hi0))
    sum_up = along(plus(lo1, far_up), up)
    sum_down = along(plus(hi3, far_down), down)
    out, dx, _, _ = _reduce(back, yrows, rrows, d_gate, d_up, gate_proj, up_proj)

    def total(one, two, three):
        return one.astype(F32) + two.astype(F32) + three.astype(F32)

    shares = jnp.concatenate([total(lo0, sum_up, near_down), total(hi0, near_up, sum_down)], 2)
    table = out[:, width : width + 64].astype(F32) + out[:, width + 64 :].astype(F32)
    onehot = routes[:, :, None] == jnp.arange(64, dtype=jnp.int32)[None, None, :]
    weight_grad = jnp.sum(jnp.where(onehot, table[:, None, :], 0.0), axis=2)

    def final(g):
        return jnp.transpose(g, (1, 0, 2))

    return (out[:, :width], dx, weight_grad, final(shares[0]), final(shares[1]), final(shares[2]))


def solution(mesh):
    rows = P(("dp", "expert"), None)
    experts = P("expert", None, None)
    grads = P("dp", "expert", None)
    return jax.shard_map(
        layer,
        mesh=mesh,
        in_specs=(rows, rows, rows, rows, experts, experts, experts),
        out_specs=(rows, rows, rows, grads, grads, grads),
        check_vma=False,
    )
```

```python
import jax
import jax.numpy as jnp
from jax import lax
from jax.experimental import pallas as pl
from jax.experimental.pallas import tpu as pltpu
from jax.sharding import PartitionSpec as P

MESH = pl.DeviceIdType.MESH
BF = jnp.bfloat16
F32 = jnp.float32
TOK = 128
HALF = 64
SUB = 32
CAP = 24
META = 128


def _place():
    me = lax.axis_index("expert")
    return lax.axis_index("dp"), me // 8, (me // 2) % 4, me % 2


def _at(x, y, c):
    return ((x + 8) % 4) * 8 + ((y + 8) % 4) * 2 + c


def _greet(peers):
    barrier = pltpu.get_barrier_semaphore()
    for peer in peers:
        pl.semaphore_signal(barrier, inc=1, device_id=peer, device_id_type=MESH)
    pl.semaphore_wait(barrier, len(peers))


def _shift(h, x, y, o1, o2, c):
    return _at(x + o1, y + o2, c) if h == 0 else _at(x + o2, y + o1, c)


class _Gather:
    def __init__(self, tag, blk, out, ssem, rsem, sends, keys):
        self.tag, self.blk, self.out, self.ssem, self.rsem = tag, blk, out, ssem, rsem
        self.sends, self.keys = sends, keys
        self.z, self.x, self.y, self.c = _place()
        self.mine = _at(self.x, self.y, self.c)
        self.sib = _at(self.x, self.y, 1 - self.c)

    def shift(self, h, o1, o2):
        return _shift(h, self.x, self.y, o1, o2, self.c)

    def send(self, slot, row, n, to, *k):
        k = self.keys.setdefault((self.tag,) + k, len(self.keys))
        src = self.blk.at[pl.ds(row, n)] if slot is None else self.out.at[slot, pl.ds(row, n)]
        cp = pltpu.make_async_remote_copy(
            src_ref=src,
            dst_ref=self.out.at[self.mine if slot is None else slot, pl.ds(row, n)],
            send_sem=self.ssem.at[len(self.sends)],
            recv_sem=self.rsem.at[k],
            device_id=(self.z, to),
            device_id_type=MESH,
        )
        cp.start()
        self.sends.append(cp)

    def landed(self, slot, row, n, *k):
        k = self.keys[(self.tag,) + k]
        view = self.out.at[slot, pl.ds(row, n)]
        pltpu.make_async_remote_copy(
            src_ref=view,
            dst_ref=view,
            send_sem=self.ssem.at[0],
            recv_sem=self.rsem.at[k],
            device_id=(self.z, self.sib),
            device_id_type=MESH,
        ).wait_recv()

    def line(self, h, o1, slot):
        self.send(slot, h * HALF, HALF, self.shift(h, 0, 1), h, "G+", o1)
        self.send(slot, h * HALF, HALF, self.shift(h, 0, -1), h, "G-", o1)

    def aside(self, h, o1, o2, slot):
        self.send(slot, h * HALF, HALF, self.sib, h, "S", o1, o2)

    def start(self):
        for h in (0, 1):
            self.send(None, h * HALF, HALF, self.shift(h, 1, 0), h, "F+")
            self.send(None, h * HALF, HALF, self.shift(h, -1, 0), h, "F-")
            self.line(h, 0, None)
            self.aside(h, 0, 0, None)

    def first(self, h, o):
        slot, sign = self.shift(h, o, 0), "+" if o < 0 else "-"
        self.landed(slot, h * HALF, HALF, h, "F" + sign)
        self.send(slot, h * HALF + (0 if o < 0 else SUB), SUB, self.shift(h, -o, 0), h, "FF" + sign)
        self.line(h, o, slot)
        self.aside(h, o, 0, slot)

    def far(self, h):
        slot = self.shift(h, 2, 0)
        self.landed(slot, h * HALF, SUB, h, "FF+")
        self.landed(slot, h * HALF + SUB, SUB, h, "FF-")
        self.line(h, 2, slot)
        self.aside(h, 2, 0, slot)

    def second(self, h, o1, o):
        slot, sign = self.shift(h, o1, o), "+" if o < 0 else "-"
        self.landed(slot, h * HALF, HALF, h, "G" + sign, o1)
        self.send(slot, h * HALF + (0 if o < 0 else SUB), SUB, self.shift(h, 0, -o), h, "GF" + sign, o1)
        self.aside(h, o1, o, slot)

    def corner(self, h, o1):
        slot = self.shift(h, o1, 2)
        self.landed(slot, h * HALF, SUB, h, "GF+", o1)
        self.landed(slot, h * HALF + SUB, SUB, h, "GF-", o1)
        self.aside(h, o1, 2, slot)

    def event(self, o1, o2):
        for h in (0, 1):
            if o2 == 0:
                self.far(h) if o1 == 2 else self.first(h, o1)
            elif o2 == 2:
                self.corner(h, o1)
            else:
                self.second(h, o1, o2)

    def chip(self, dx, dy):
        for h, o1, o2 in ((0, dx, dy), (1, dy, dx)):
            slot = _at(self.x + dx, self.y + dy, 1 - self.c)
            self.landed(slot, h * HALF, HALF, h, "S", o1, o2)
        return _at(self.x + dx, self.y + dy, 0) // 2


EVENTS = (
    (-1, 0), (1, 0), (0, -1), (0, 1), (2, 0), (-1, -1), (-1, 1), (1, -1), (1, 1),
    (0, 2), (2, -1), (2, 1), (-1, 2), (1, 2), (2, 2),
)
ROWS = 2 * CAP


def _tokens_of(ref, chip, lanes):
    return ref[pl.ds(2 * chip, 2), :, lanes].reshape(2 * TOK, -1)


def _pick_dot(back, rows):
    dims = (((0,), (0,)), ((), ()))
    return lax.dot_general(back, rows, dims, preferred_element_type=F32)[: 2 * ROWS]


def _front_kernel(
    xm, ct, gw, uw, back_out, xr_out, cr_out, wr_out, gu_out, call,
    xall, cbuf, xr, cr, wgu, gu, back, wr,
    ssem, rsem, lsem, wsem, csem, osem, rowsem,
):
    me = lax.axis_index("expert")
    z, x, y, c = _place()
    width, hid = ct.shape[1], gw.shape[2]
    weights = []
    for e in range(2):
        for k, ref in enumerate((gw, uw)):
            cp = pltpu.make_async_copy(ref.at[e], wgu.at[e, :, pl.ds(k * hid, hid)], wsem.at[2 * e + k])
            cp.start()
            weights.append(cp)
    _greet(
        [
            (z, _at(x + 1, y, c)), (z, _at(x - 1, y, c)), (z, _at(x, y + 1, c)), (z, _at(x, y - 1, c)),
            (z, _at(x, y, 1 - c)),
        ]
    )
    sends, keys = [], {}
    gx = _Gather("x", xm, xall, ssem, rsem, sends, keys)
    gc = _Gather("c", ct, call, ssem, rsem, sends, keys)
    own_x = pltpu.make_async_copy(xm, xall.at[gx.mine], lsem.at[0])
    own_c = pltpu.make_async_copy(ct, call.at[gx.mine], lsem.at[1])
    own_x.start()
    own_c.start()
    gx.start()

    def number(shape, dim):
        return lax.broadcasted_iota(jnp.int32, shape, dim)

    def rows_of(dx, dy):
        chip = gx.chip(dx, dy)
        meta = _tokens_of(xall, chip, pl.ds(width, META)).astype(F32)
        tok, lane = number((2 * TOK, META), 0), number((2 * TOK, META), 1)
        hits = []
        for e in range(2):
            match = (meta == (2 * me + e).astype(F32)) & (lane < 8)
            hits.append(jnp.max(jnp.where(match, 1.0, 0.0), axis=1, keepdims=True))
        both = jnp.where(lane == 0, hits[0], jnp.where(lane == 1, hits[1], 0.0)).astype(BF)
        t0, t1 = number((2 * TOK, 2 * TOK), 0), number((2 * TOK, 2 * TOK), 1)
        earlier = ((t1 < t0) & ((t1 < TOK) == (t0 < TOK))).astype(F32).astype(BF)
        before = jnp.dot(earlier, both, preferred_element_type=F32)
        second = lane >= ROWS
        place = lane - jnp.where(second, ROWS, 0)
        late = place >= CAP
        place = place - jnp.where(late, CAP, 0)
        hit = jnp.where(second, hits[1], hits[0])
        spot = jnp.where(second, before[:, 1:2], before[:, 0:1])
        chosen = (hit > 0.5) & (spot == place.astype(F32)) & (late == (tok >= TOK)) & (lane < 2 * ROWS)
        pick = jnp.where(chosen, 1.0, 0.0).astype(BF)
        back[chip] = pick
        rows = _pick_dot(pick, _tokens_of(xall, chip, pl.ds(0, width))).astype(BF)
        at = pl.ds(pl.multiple_of(chip * ROWS, 16), ROWS)
        xr[0, at, :] = rows[:ROWS]
        xr[1, at, :] = rows[ROWS:]
        info = _pick_dot(pick, meta.astype(BF))
        shape = (2 * ROWS, META)
        expert = (2 * me + jnp.where(number(shape, 0) >= ROWS, 1, 0)).astype(F32)
        match = jnp.where((info == expert) & (number(shape, 1) < 8), 1.0, 0.0).astype(BF)
        k0, k1 = number((META, META), 0), number((META, META), 1)
        copies = ((k1 == k0 + 8) | (k1 == k0 + 16) | (k1 == k0 + 24)) & (k0 < 8)
        spread = jnp.dot(match, jnp.where(copies, 1.0, 0.0).astype(BF), preferred_element_type=F32)
        weight = jnp.sum(spread * info, axis=1, keepdims=True)
        wr[chip] = jnp.broadcast_to(weight, shape)

    def drive(gather, work, before=None):
        done, waiting, ready = {(0, 0)}, [], [(0, 0)]
        for n, (o1, o2) in enumerate(EVENTS):
            if before is not None:
                before(n)
            gather.event(o1, o2)
            for chip in waiting:
                work(*chip)
            waiting, ready = ready, []
            done.add((o1, o2))
            if (o2, o1) in done:
                ready = [(o1, o2)] if o1 == o2 else [(o1, o2), (o2, o1)]
        for chip in waiting + ready:
            work(*chip)

    def middle(n):
        if n == 9:
            gc.start()

    own_x.wait()
    drive(gx, rows_of, middle)
    outs = []

    def put(src, dst, sem):
        cp = pltpu.make_async_copy(src, dst, sem)
        cp.start()
        outs.append(cp)

    put(xr, xr_out, osem.at[0])
    put(back, back_out, osem.at[1])
    put(wr, wr_out, osem.at[2])

    def project(e, first, last):
        @pl.loop(first, last)
        def _(j):
            cols = pl.ds(pl.multiple_of(j * 256, 256), 256)
            gu[e, :, cols] = jnp.dot(xr[e], wgu[e, :, cols], preferred_element_type=F32)

    steps = 2 * hid // 256
    units = {2: (0, 0, 2), 4: (0, 2, steps), 6: (1, 0, 2), 8: (1, 2, steps)}

    def compute(n):
        if n in units:
            e, first, last = units[n]
            if first == 0:
                weights[2 * e].wait()
                weights[2 * e + 1].wait()
            project(e, first, last)
            if last == steps:
                put(gu.at[e], gu_out.at[e], osem.at[3 + e])

    own_c.wait()
    fetched = []

    def finish():
        i, chip, cp = fetched.pop(0)
        cp.wait()
        rows = _pick_dot(back[chip], cbuf[i % 3].reshape(2 * TOK, width))
        rows = (rows * wr[chip][:, 0:1]).astype(BF)
        at = pl.ds(pl.multiple_of(chip * ROWS, 16), ROWS)
        for e in range(2):
            cr[e, at, :] = rows[e * ROWS : (e + 1) * ROWS]
            put(cr.at[e, at], cr_out.at[e, at], rowsem.at[2 * i + e])

    count = [0]

    def cot_of(dx, dy):
        chip = gc.chip(dx, dy)
        i = count[0]
        count[0] += 1
        cp = pltpu.make_async_copy(call.at[pl.ds(2 * chip, 2)], cbuf.at[i % 3], csem.at[i % 3])
        cp.start()
        fetched.append((i, chip, cp))
        if len(fetched) > 2:
            finish()

    drive(gc, cot_of, compute)
    while fetched:
        finish()
    for cp in outs:
        cp.wait()
    for cp in sends:
        cp.wait_send()


def _front(xm, ct, gate_proj, up_proj):
    width, hid = ct.shape[1], gate_proj.shape[2]
    hbm = pl.BlockSpec(memory_space=pl.ANY)
    vmem = pl.BlockSpec(memory_space=pltpu.VMEM)
    rows = 32 * CAP
    return pl.pallas_call(
        _front_kernel,
        out_shape=(
            jax.ShapeDtypeStruct((16, 2 * TOK, META), BF),
            jax.ShapeDtypeStruct((2, rows, width), BF),
            jax.ShapeDtypeStruct((2, rows, width), BF),
            jax.ShapeDtypeStruct((16, 2 * ROWS, META), F32),
            jax.ShapeDtypeStruct((2, rows, 2 * hid), F32),
            jax.ShapeDtypeStruct((32, TOK, width), BF),
        ),
        in_specs=[vmem, vmem, hbm, hbm],
        out_specs=(hbm,) * 6,
        scratch_shapes=[
            pltpu.VMEM((32, TOK, width + META), BF),
            pltpu.VMEM((3, 2, TOK, width), BF),
            pltpu.VMEM((2, rows, width), BF),
            pltpu.VMEM((2, rows, width), BF),
            pltpu.VMEM((2, width, 2 * hid), BF),
            pltpu.VMEM((2, rows, 2 * hid), F32),
            pltpu.VMEM((16, 2 * TOK, META), BF),
            pltpu.VMEM((16, 2 * ROWS, META), F32),
            pltpu.SemaphoreType.DMA((144,)),
            pltpu.SemaphoreType.DMA((144,)),
            pltpu.SemaphoreType.DMA((2,)),
            pltpu.SemaphoreType.DMA((4,)),
            pltpu.SemaphoreType.DMA((3,)),
            pltpu.SemaphoreType.DMA((5,)),
            pltpu.SemaphoreType.DMA((32,)),
        ],
        compiler_params=pltpu.CompilerParams(
            collective_id=0, has_side_effects=True, vmem_limit_bytes=63 * 1024 * 1024
        ),
        cost_estimate=pl.CostEstimate(flops=10_000_000_000, bytes_accessed=300_000_000, transcendentals=0),
        name="plane_gather",
    )(xm, ct, gate_proj, up_proj)


def _add(dst, src, n):
    @pl.loop(0, n // 16)
    def _(i):
        rows = pl.ds(pl.multiple_of(i * 16, 16), 16)
        dst[rows, :] = (dst[rows, :].astype(F32) + src[rows, :].astype(F32)).astype(BF)


def _add3(dst, own, one, two, n):
    @pl.loop(0, n // 16)
    def _(i):
        rows = pl.ds(pl.multiple_of(i * 16, 16), 16)
        total = own[rows, :].astype(F32) + one[rows, :].astype(F32) + two[rows, :].astype(F32)
        dst[rows, :] = total.astype(dst.dtype)


OBS = OAS = (2, 1, 3, 0)
AHEAD = 4
LO, HI = pl.ds(0, SUB), pl.ds(SUB, SUB)


class _Reduce:
    def __init__(self, tag, bufs, aside, bsem, out, stage, ssem, rsem, sends, keys):
        self.tag, self.aside, self.bsem, self.out, self.stage = tag, aside, bsem, out, stage
        self.T, self.sb, self.ra, self.rb, self.r2a, self.r2b = bufs
        self.ssem, self.rsem, self.sends, self.keys = ssem, rsem, sends, keys
        self.z, self.x, self.y, self.c = _place()
        self.sib = (self.z, _at(self.x, self.y, 1 - self.c))
        self.width = self.T.shape[-1]
        self.order = [(h, ob, oa) for ob in OBS for oa in OAS for h in (0, 1)]
        self.loads, self.made, self.shared = {}, [], {}

    def remote(self, src, dst, to, *k):
        k = self.keys.setdefault((self.tag,) + k, len(self.keys))
        cp = pltpu.make_async_remote_copy(
            src_ref=src,
            dst_ref=dst,
            send_sem=self.ssem.at[len(self.keys) - 1],
            recv_sem=self.rsem.at[k],
            device_id=to,
            device_id_type=MESH,
        )
        cp.start()
        self.sends.append(cp)
        return cp

    def landed(self, dst, *k):
        pltpu.make_async_remote_copy(
            src_ref=dst,
            dst_ref=dst,
            send_sem=self.ssem.at[0],
            recv_sem=self.rsem.at[self.keys[(self.tag,) + k]],
            device_id=self.sib,
            device_id_type=MESH,
        ).wait_recv()

    def ax(self, h, o):
        return (self.z, _shift(1 - h, self.x, self.y, o, 0, self.c))

    def bx(self, h, o):
        return (self.z, _shift(h, self.x, self.y, o, 0, self.c))

    def make(self, dx, dy):
        if (dx, dy) in self.made:
            return
        chip = _at(self.x + dx, self.y + dy, 0) // 2
        stage = self.stage.at[len(self.made), :, pl.ds(0, self.width)]
        places = ((0, dx * 4 + dy), (1, dy * 4 + dx))
        self.spread(chip, 1 - self.c, [(stage.at[pl.ds(h * HALF, HALF)], h) for h in (0, 1)])
        self.shared[len(self.made)] = [
            self.remote(stage.at[pl.ds(h * HALF, HALF)], self.aside.at[h, k], self.sib, "s", h, k)
            for h, k in places
        ]
        self.spread(chip, self.c, [(self.T.at[h, k], h) for h, k in places])
        self.made.append((dx, dy))

    def fetch(self, i):
        h, ob, oa = self.order[i]
        view = self.aside.at[h, ob * 4 + oa]
        self.landed(view, "s", h, ob * 4 + oa)
        cp = pltpu.make_async_copy(view, self.sb.at[i % (AHEAD + 1)], self.bsem.at[i % (AHEAD + 1)])
        cp.start()
        self.loads[i] = cp

    def one(self, i):
        h, ob, oa = self.order[i]
        for n in range(AHEAD) if i == 0 else ():
            self.fetch(n)
        if i + AHEAD < len(self.order):
            self.fetch(i + AHEAD)
        self.loads[i].wait()
        t = self.T.at[h, ob * 4 + oa]
        _add(t, self.sb.at[i % (AHEAD + 1)], HALF)
        if oa == 2:
            self.remote(t.at[LO], self.ra.at[h, ob, 0], self.ax(h, 1), "ra", h, ob, 0)
            self.remote(t.at[HI], self.ra.at[h, ob, 1], self.ax(h, -1), "ra", h, ob, 1)
        elif oa == 1:
            self.remote(t.at[HI], self.rb.at[h, ob, 0, HI], self.ax(h, 1), "rd", h, ob, 0)
        elif oa == 3:
            self.remote(t.at[LO], self.rb.at[h, ob, 1, LO], self.ax(h, -1), "rd", h, ob, 1)

    def stage1(self, j):
        for i in range(j * 8, j * 8 + 8):
            for h, ob, oa in self.order[i : i + AHEAD + 4]:
                self.make(*((ob, oa) if h == 0 else (oa, ob)))
            self.one(i)

    def stage2(self, j):
        ob = OBS[j]
        for h in (0, 1):
            self.landed(self.ra.at[h, ob, 0], "ra", h, ob, 0)
            t = self.T.at[h, ob * 4 + 1]
            _add(t.at[LO], self.ra.at[h, ob, 0], SUB)
            self.remote(t.at[LO], self.rb.at[h, ob, 0, LO], self.ax(h, 1), "rs", h, ob, 0)
            self.landed(self.ra.at[h, ob, 1], "ra", h, ob, 1)
            t = self.T.at[h, ob * 4 + 3]
            _add(t.at[HI], self.ra.at[h, ob, 1], SUB)
            self.remote(t.at[HI], self.rb.at[h, ob, 1, HI], self.ax(h, -1), "rs", h, ob, 1)

    def stage3(self, j):
        ob = OBS[j]
        for h in (0, 1):
            self.landed(self.rb.at[h, ob, 0, HI], "rd", h, ob, 0)
            self.landed(self.rb.at[h, ob, 1, LO], "rd", h, ob, 1)
            self.landed(self.rb.at[h, ob, 0, LO], "rs", h, ob, 0)
            self.landed(self.rb.at[h, ob, 1, HI], "rs", h, ob, 1)
            t = self.T.at[h, ob * 4]
            _add3(t, t, self.rb.at[h, ob, 0], self.rb.at[h, ob, 1], HALF)
            if ob == 2:
                self.remote(t.at[LO], self.r2a.at[h, 0], self.bx(h, 1), "2a", h, 0)
                self.remote(t.at[HI], self.r2a.at[h, 1], self.bx(h, -1), "2a", h, 1)
            elif ob == 1:
                self.remote(t.at[HI], self.r2b.at[h, 0, HI], self.bx(h, 1), "2d", h, 0)
            elif ob == 3:
                self.remote(t.at[LO], self.r2b.at[h, 1, LO], self.bx(h, -1), "2d", h, 1)

    def stage4(self):
        for h in (0, 1):
            self.landed(self.r2a.at[h, 0], "2a", h, 0)
            t = self.T.at[h, 4]
            _add(t.at[LO], self.r2a.at[h, 0], SUB)
            self.remote(t.at[LO], self.r2b.at[h, 0, LO], self.bx(h, 1), "2s", h, 0)
            self.landed(self.r2a.at[h, 1], "2a", h, 1)
            t = self.T.at[h, 12]
            _add(t.at[HI], self.r2a.at[h, 1], SUB)
            self.remote(t.at[HI], self.r2b.at[h, 1, HI], self.bx(h, -1), "2s", h, 1)

    def stage5(self):
        for h in (0, 1):
            self.landed(self.r2b.at[h, 0, HI], "2d", h, 0)
            self.landed(self.r2b.at[h, 1, LO], "2d", h, 1)
            self.landed(self.r2b.at[h, 0, LO], "2s", h, 0)
            self.landed(self.r2b.at[h, 1, HI], "2s", h, 1)
            rows = self.out.at[pl.ds(h * HALF, HALF)]
            _add3(rows, self.T.at[h, 0], self.r2b.at[h, 0], self.r2b.at[h, 1], HALF)


def _reduce_kernel(
    back_in, y_in, r_in, dg_in, du_in, gw, uw, outy, outd, asidey, asided, *rest
):
    bufy, bufd = rest[:6], rest[6:12]
    stage, rows, back, rr, dcat, wcat, ssem, rsem, bsem, lsem, wsem = rest[12:]
    z, x, y, c = _place()
    width, hid = y_in.shape[2], dg_in.shape[2]

    def load(src, dst, sem):
        cp = pltpu.make_async_copy(src, dst, sem)
        cp.start()
        return cp

    first = [load(back_in, back, lsem.at[0]), load(y_in, rows, lsem.at[1]), load(r_in, rr, lsem.at[2])]
    later = [load(ref, dcat.at[:, :, pl.ds(k * hid, hid)], lsem.at[3 + k]) for k, ref in enumerate((dg_in, du_in))]

    def weights(e):
        return [load(ref.at[e], wcat.at[:, pl.ds(k * hid, hid)], wsem.at[k]) for k, ref in enumerate((gw, uw))]

    later += weights(0)
    _greet(
        [
            (z, _at(x + 1, y, c)), (z, _at(x - 1, y, c)), (z, _at(x, y + 1, c)), (z, _at(x, y - 1, c)),
            (z, _at(x, y, 1 - c)),
        ]
    )
    sends, keys = [], {}
    ry = _Reduce("y", bufy, asidey, bsem.at[0], outy, stage, ssem, rsem, sends, keys)
    rd = _Reduce("d", bufd, asided, bsem.at[1], outd, stage, ssem, rsem, sends, keys)

    def spread(chip, core, places, extra):
        sel = back[chip, pl.ds(pl.multiple_of(core * TOK, TOK), TOK), :][:, : 2 * ROWS]
        at = pl.ds(pl.multiple_of(chip * ROWS, 16), ROWS)

        @pl.loop(0, 4)
        def _(j):
            cols = pl.ds(pl.multiple_of(j * 512, 512), 512)
            both = jnp.concatenate([rows[0, at, cols], rows[1, at, cols]], 0)
            made = jnp.dot(sel, both, preferred_element_type=F32).astype(BF)
            for ref, h in places:
                ref[:, cols] = made[h * HALF : (h + 1) * HALF]

        if extra:
            made = jnp.dot(sel, rr[chip], preferred_element_type=F32).astype(BF)
            for ref, h in places:
                ref[:, pl.ds(width, META)] = made[h * HALF : (h + 1) * HALF]

    def spread_y(chip, core, places):
        spread(chip, core, places, True)

    ry.spread = spread_y

    def spread_d(chip, core, places):
        n = len(rd.made)
        for cp in ry.shared.pop(n, ()):
            cp.wait_send()
            sends[:] = [s for s in sends if s is not cp]
        spread(chip, core, places, False)

    rd.spread = spread_d

    def product(e, j0, j1):
        @pl.loop(j0, j1)
        def _(j):
            at = pl.ds(pl.multiple_of(j * 256, 256), 256)
            dims = (((1,), (1,)), ((), ()))
            made = lax.dot_general(dcat[e], wcat[at, :], dims, preferred_element_type=F32)
            rows[e, :, at] = made.astype(BF)

    for cp in first:
        cp.wait()
    n = width // 256
    ry.stage1(0)
    ry.stage1(1)
    for h, ob, oa in ry.order:
        ry.make(*((ob, oa) if h == 0 else (oa, ob)))
    for cp in later:
        cp.wait()
    product(0, 0, n // 2)
    ry.stage1(2)
    ry.stage2(0)
    product(0, n // 2, n)
    second = weights(1)
    ry.stage1(3)
    ry.stage2(1)
    for cp in second:
        cp.wait()
    product(1, 0, n // 2)
    ry.stage2(2)
    product(1, n // 2, n)
    rd.stage1(0)
    ry.stage3(0)
    ry.stage2(3)
    rd.stage1(1)
    ry.stage3(1)
    rd.stage2(0)
    rd.stage1(2)
    ry.stage3(2)
    ry.stage4()
    rd.stage2(1)
    rd.stage1(3)
    ry.stage3(3)
    ry.stage5()
    rd.stage2(2)
    rd.stage3(0)
    rd.stage2(3)
    rd.stage3(1)
    rd.stage3(2)
    rd.stage4()
    rd.stage3(3)
    rd.stage5()
    for cp in sends:
        cp.wait_send()


def _reduce(back, yrows, rrows, d_gate, d_up, gate_proj, up_proj):
    width, hid = yrows.shape[2], d_gate.shape[2]
    hbm = pl.BlockSpec(memory_space=pl.ANY)
    vmem = pl.BlockSpec(memory_space=pltpu.VMEM)

    def buffers(w):
        return [
            pltpu.VMEM((2, 16, HALF, w), BF),
            pltpu.VMEM((AHEAD + 1, HALF, w), BF),
            pltpu.VMEM((2, 4, 2, SUB, w), BF),
            pltpu.VMEM((2, 4, 2, HALF, w), BF),
            pltpu.VMEM((2, 2, SUB, w), BF),
            pltpu.VMEM((2, 2, HALF, w), BF),
        ]

    wide = width + META
    return pl.pallas_call(
        _reduce_kernel,
        out_shape=(
            jax.ShapeDtypeStruct((TOK, wide), BF),
            jax.ShapeDtypeStruct((TOK, width), BF),
            jax.ShapeDtypeStruct((2, 16, HALF, wide), BF),
            jax.ShapeDtypeStruct((2, 16, HALF, width), BF),
        ),
        in_specs=[hbm] * 7,
        out_specs=(vmem, vmem, hbm, hbm),
        scratch_shapes=buffers(wide)
        + buffers(width)
        + [
            pltpu.VMEM((16, TOK, wide), BF),
            pltpu.VMEM(yrows.shape, BF),
            pltpu.VMEM(back.shape, BF),
            pltpu.VMEM(rrows.shape, BF),
            pltpu.VMEM((2, 32 * CAP, 2 * hid), BF),
            pltpu.VMEM((width, 2 * hid), BF),
            pltpu.SemaphoreType.DMA((184,)),
            pltpu.SemaphoreType.DMA((184,)),
            pltpu.SemaphoreType.DMA((2, AHEAD + 1)),
            pltpu.SemaphoreType.DMA((5,)),
            pltpu.SemaphoreType.DMA((2,)),
        ],
        compiler_params=pltpu.CompilerParams(
            collective_id=1, has_side_effects=True, vmem_limit_bytes=67_000_000
        ),
        cost_estimate=pl.CostEstimate(flops=12_000_000_000, bytes_accessed=300_000_000, transcendentals=0),
        name="plane_reduce",
    )(back, yrows, rrows, d_gate, d_up, gate_proj, up_proj)


def _grads_kernel(q_ref, x_ref, c_ref, dg_ref, du_ref, h_ref, lo_ref, hi_ref):
    dims = (((0,), (0,)), ((), ()))
    n = lo_ref.shape[2]
    for k, (rows, cots) in enumerate(((x_ref, dg_ref), (x_ref, du_ref), (c_ref, h_ref))):
        g = lax.dot_general(rows[0], cots[0], dims, preferred_element_type=F32).astype(BF)
        lo_ref[k, 0] = g[:n]
        hi_ref[k, 0] = g[n:]


def _grads(quarter, xr, cr, d_gate, d_up, hidden):
    rows, width = xr.shape[1:]
    hid = hidden.shape[2]
    wide = pl.BlockSpec((1, rows, width // 4), lambda e, q: (e, 0, q[0]))
    thin = pl.BlockSpec((1, rows, hid), lambda e, q: (e, 0, 0))
    half = jax.ShapeDtypeStruct((3, 2, width // 8, hid), BF)
    spec = pl.BlockSpec((3, 1, width // 8, hid), lambda e, q: (0, e, 0, 0))
    return pl.pallas_call(
        _grads_kernel,
        grid_spec=pltpu.PrefetchScalarGridSpec(
            num_scalar_prefetch=1, grid=(2,), in_specs=[wide, wide, thin, thin, thin], out_specs=(spec, spec)
        ),
        out_shape=(half, half),
        cost_estimate=pl.CostEstimate(
            flops=12 * rows * (width // 4) * hid, bytes_accessed=14_000_000, transcendentals=0
        ),
        name="grad_quarter",
    )(quarter, xr, cr, d_gate, d_up, hidden)


def _bits(v):
    return lax.reduce_precision(v, 8, 7)


def layer(tokens, routes, route_weights, cotangent, gate_proj, up_proj, down_proj):
    width = tokens.shape[1]
    hid = gate_proj.shape[2]
    me = lax.axis_index("expert")
    w_hi = _bits(route_weights)
    w_mid = _bits(route_weights - w_hi)
    w_lo = route_weights - w_hi - w_mid
    meta = jnp.concatenate(
        [routes.astype(F32), w_hi, w_mid, w_lo, jnp.zeros((TOK, META - 32), F32)], 1
    ).astype(BF)
    mine = 2 * me + jnp.arange(2, dtype=jnp.int32)
    back, xr, cr, wr, gu, _ = _front(jnp.concatenate([tokens, meta], 1), cotangent, gate_proj, up_proj)
    we = wr[:, :, 0].reshape(16, 2, ROWS).transpose(1, 0, 2).reshape(2, 32 * CAP, 1)
    gate_pre, up_pre = gu[:, :, :hid], gu[:, :, hid:]
    sig = jax.nn.sigmoid(gate_pre)
    swish = gate_pre * sig
    d_swish = sig * (1.0 + gate_pre * (1.0 - sig))
    hidden = (swish * up_pre).astype(BF)
    d_hidden = jnp.einsum("erd,ehd->erh", cr, down_proj, preferred_element_type=F32)
    d_gate = (d_hidden * up_pre * d_swish).astype(BF)
    d_up = (d_hidden * swish).astype(BF)
    rw = jnp.sum(d_hidden * hidden.astype(F32), axis=2, keepdims=True) / jnp.where(we > 0, we, 1.0)

    z = lax.axis_index("dp")
    up = [(i, (i + 1) % 4) for i in range(4)]
    down = [(i, (i + 3) % 4) for i in range(4)]

    def quarter(o, after=None):
        which = ((z + o) % 4).reshape(1)
        if after is not None:
            which, _ = lax.optimization_barrier((which, after))
        return _grads(which, xr, cr, d_gate, d_up, hidden)

    def along(v, way):
        return lax.ppermute(v, "dp", way)

    lo2, hi2 = quarter(2)
    far_up, far_down = along(lo2, up), along(hi2, down)
    lo1, hi1 = quarter(1, lo2)
    near_up = along(hi1, up)
    lo3, hi3 = quarter(3, lo2)
    near_down = along(lo3, down)
    lo0, hi0 = quarter(0, lo3)
    yrows = (jnp.einsum("erh,ehd->erd", hidden, down_proj, preferred_element_type=F32) * we).astype(BF)
    lane = jnp.arange(META, dtype=jnp.int32)
    r_hi = _bits(rw)
    r_lo = rw - r_hi
    spot = lane[None, None, :] - mine[:, None, None]
    rrows = jnp.where(spot == 0, r_hi, 0.0) + jnp.where(spot == 64, r_lo, 0.0)
    rrows = rrows.reshape(2, 16, ROWS, META).transpose(1, 0, 2, 3).reshape(16, 2 * ROWS, META).astype(BF)

    def plus(one, two):
        return (one.astype(F32) + two.astype(F32)).astype(BF)

    lo1, hi3, lo0, hi0 = lax.optimization_barrier((lo1, hi3, lo0, hi0))
    sum_up = along(plus(lo1, far_up), up)
    sum_down = along(plus(hi3, far_down), down)
    out, dx, _, _ = _reduce(back, yrows, rrows, d_gate, d_up, gate_proj, up_proj)

    def total(one, two, three):
        return one.astype(F32) + two.astype(F32) + three.astype(F32)

    shares = jnp.concatenate([total(lo0, sum_up, near_down), total(hi0, near_up, sum_down)], 2)
    table = out[:, width : width + 64].astype(F32) + out[:, width + 64 :].astype(F32)
    onehot = routes[:, :, None] == jnp.arange(64, dtype=jnp.int32)[None, None, :]
    weight_grad = jnp.sum(jnp.where(onehot, table[:, None, :], 0.0), axis=2)

    def final(g):
        return jnp.transpose(g, (1, 0, 2))

    return (out[:, :width], dx, weight_grad, final(shares[0]), final(shares[1]), final(shares[2]))


def solution(mesh):
    rows = P(("dp", "expert"), None)
    experts = P("expert", None, None)
    grads = P("dp", "expert", None)
    return jax.shard_map(
        layer,
        mesh=mesh,
        in_specs=(rows, rows, rows, rows, experts, experts, experts),
        out_specs=(rows, rows, rows, grads, grads, grads),
        check_vma=False,
    )
```

```python
import jax
import jax.numpy as jnp
from jax import lax
from jax.experimental import pallas as pl
from jax.experimental.pallas import tpu as pltpu
from jax.sharding import PartitionSpec as P

MESH = pl.DeviceIdType.MESH
BF = jnp.bfloat16
F32 = jnp.float32
TOK = 128
HALF = 64
SUB = 32
CAP = 24
META = 128


def _place():
    me = lax.axis_index("expert")
    return lax.axis_index("dp"), me // 8, (me // 2) % 4, me % 2


def _at(x, y, c):
    return ((x + 8) % 4) * 8 + ((y + 8) % 4) * 2 + c


def _greet(peers):
    barrier = pltpu.get_barrier_semaphore()
    for peer in peers:
        pl.semaphore_signal(barrier, inc=1, device_id=peer, device_id_type=MESH)
    pl.semaphore_wait(barrier, len(peers))


def _shift(h, x, y, o1, o2, c):
    return _at(x + o1, y + o2, c) if h == 0 else _at(x + o2, y + o1, c)


class _Gather:
    def __init__(self, tag, blk, out, ssem, rsem, sends, keys):
        self.tag, self.blk, self.out, self.ssem, self.rsem = tag, blk, out, ssem, rsem
        self.sends, self.keys = sends, keys
        self.z, self.x, self.y, self.c = _place()
        self.mine = _at(self.x, self.y, self.c)
        self.sib = _at(self.x, self.y, 1 - self.c)

    def shift(self, h, o1, o2):
        return _shift(h, self.x, self.y, o1, o2, self.c)

    def send(self, slot, row, n, to, *k):
        k = self.keys.setdefault((self.tag,) + k, len(self.keys))
        src = self.blk.at[pl.ds(row, n)] if slot is None else self.out.at[slot, pl.ds(row, n)]
        cp = pltpu.make_async_remote_copy(
            src_ref=src,
            dst_ref=self.out.at[self.mine if slot is None else slot, pl.ds(row, n)],
            send_sem=self.ssem.at[len(self.sends)],
            recv_sem=self.rsem.at[k],
            device_id=(self.z, to),
            device_id_type=MESH,
        )
        cp.start()
        self.sends.append(cp)

    def landed(self, slot, row, n, *k):
        k = self.keys[(self.tag,) + k]
        view = self.out.at[slot, pl.ds(row, n)]
        pltpu.make_async_remote_copy(
            src_ref=view,
            dst_ref=view,
            send_sem=self.ssem.at[0],
            recv_sem=self.rsem.at[k],
            device_id=(self.z, self.sib),
            device_id_type=MESH,
        ).wait_recv()

    def line(self, h, o1, slot):
        self.send(slot, h * HALF, HALF, self.shift(h, 0, 1), h, "G+", o1)
        self.send(slot, h * HALF, HALF, self.shift(h, 0, -1), h, "G-", o1)

    def aside(self, h, o1, o2, slot):
        self.send(slot, h * HALF, HALF, self.sib, h, "S", o1, o2)

    def start(self):
        for h in (0, 1):
            self.send(None, h * HALF, HALF, self.shift(h, 1, 0), h, "F+")
            self.send(None, h * HALF, HALF, self.shift(h, -1, 0), h, "F-")
            self.line(h, 0, None)
            self.aside(h, 0, 0, None)

    def first(self, h, o):
        slot, sign = self.shift(h, o, 0), "+" if o < 0 else "-"
        self.landed(slot, h * HALF, HALF, h, "F" + sign)
        self.send(slot, h * HALF + (0 if o < 0 else SUB), SUB, self.shift(h, -o, 0), h, "FF" + sign)
        self.line(h, o, slot)
        self.aside(h, o, 0, slot)

    def far(self, h):
        slot = self.shift(h, 2, 0)
        self.landed(slot, h * HALF, SUB, h, "FF+")
        self.landed(slot, h * HALF + SUB, SUB, h, "FF-")
        self.line(h, 2, slot)
        self.aside(h, 2, 0, slot)

    def second(self, h, o1, o):
        slot, sign = self.shift(h, o1, o), "+" if o < 0 else "-"
        self.landed(slot, h * HALF, HALF, h, "G" + sign, o1)
        self.send(slot, h * HALF + (0 if o < 0 else SUB), SUB, self.shift(h, 0, -o), h, "GF" + sign, o1)
        self.aside(h, o1, o, slot)

    def corner(self, h, o1):
        slot = self.shift(h, o1, 2)
        self.landed(slot, h * HALF, SUB, h, "GF+", o1)
        self.landed(slot, h * HALF + SUB, SUB, h, "GF-", o1)
        self.aside(h, o1, 2, slot)

    def event(self, o1, o2):
        for h in (0, 1):
            if o2 == 0:
                self.far(h) if o1 == 2 else self.first(h, o1)
            elif o2 == 2:
                self.corner(h, o1)
            else:
                self.second(h, o1, o2)

    def chip(self, dx, dy):
        for h, o1, o2 in ((0, dx, dy), (1, dy, dx)):
            slot = _at(self.x + dx, self.y + dy, 1 - self.c)
            self.landed(slot, h * HALF, HALF, h, "S", o1, o2)
        return _at(self.x + dx, self.y + dy, 0) // 2


EVENTS = (
    (-1, 0), (1, 0), (0, -1), (0, 1), (2, 0), (-1, -1), (-1, 1), (1, -1), (1, 1),
    (0, 2), (2, -1), (2, 1), (-1, 2), (1, 2), (2, 2),
)
ROWS = 2 * CAP


def _tokens_of(ref, chip, lanes):
    return ref[pl.ds(2 * chip, 2), :, lanes].reshape(2 * TOK, -1)


def _pick_dot(back, rows):
    dims = (((0,), (0,)), ((), ()))
    return lax.dot_general(back, rows, dims, preferred_element_type=F32)[: 2 * ROWS]


def _front_kernel(
    xm, ct, gw, uw, back_out, xr_out, cr_out, wr_out, gu_out, call,
    xall, cbuf, xr, cr, wgu, gu, back, wr,
    ssem, rsem, lsem, wsem, csem, osem, rowsem,
):
    me = lax.axis_index("expert")
    z, x, y, c = _place()
    width, hid = ct.shape[1], gw.shape[2]
    weights = []
    for e in range(2):
        for k, ref in enumerate((gw, uw)):
            cp = pltpu.make_async_copy(ref.at[e], wgu.at[e, :, pl.ds(k * hid, hid)], wsem.at[2 * e + k])
            cp.start()
            weights.append(cp)
    _greet(
        [
            (z, _at(x + 1, y, c)), (z, _at(x - 1, y, c)), (z, _at(x, y + 1, c)), (z, _at(x, y - 1, c)),
            (z, _at(x, y, 1 - c)),
        ]
    )
    sends, keys = [], {}
    gx = _Gather("x", xm, xall, ssem, rsem, sends, keys)
    gc = _Gather("c", ct, call, ssem, rsem, sends, keys)
    own_x = pltpu.make_async_copy(xm, xall.at[gx.mine], lsem.at[0])
    own_c = pltpu.make_async_copy(ct, call.at[gx.mine], lsem.at[1])
    own_x.start()
    own_c.start()
    gx.start()

    def number(shape, dim):
        return lax.broadcasted_iota(jnp.int32, shape, dim)

    def rows_of(dx, dy):
        chip = gx.chip(dx, dy)
        meta = _tokens_of(xall, chip, pl.ds(width, META)).astype(F32)
        tok, lane = number((2 * TOK, META), 0), number((2 * TOK, META), 1)
        hits = []
        for e in range(2):
            match = (meta == (2 * me + e).astype(F32)) & (lane < 8)
            hits.append(jnp.max(jnp.where(match, 1.0, 0.0), axis=1, keepdims=True))
        both = jnp.where(lane == 0, hits[0], jnp.where(lane == 1, hits[1], 0.0)).astype(BF)
        t0, t1 = number((2 * TOK, 2 * TOK), 0), number((2 * TOK, 2 * TOK), 1)
        earlier = ((t1 < t0) & ((t1 < TOK) == (t0 < TOK))).astype(F32).astype(BF)
        before = jnp.dot(earlier, both, preferred_element_type=F32)
        second = lane >= ROWS
        place = lane - jnp.where(second, ROWS, 0)
        late = place >= CAP
        place = place - jnp.where(late, CAP, 0)
        hit = jnp.where(second, hits[1], hits[0])
        spot = jnp.where(second, before[:, 1:2], before[:, 0:1])
        chosen = (hit > 0.5) & (spot == place.astype(F32)) & (late == (tok >= TOK)) & (lane < 2 * ROWS)
        pick = jnp.where(chosen, 1.0, 0.0).astype(BF)
        back[chip] = pick
        rows = _pick_dot(pick, _tokens_of(xall, chip, pl.ds(0, width))).astype(BF)
        at = pl.ds(pl.multiple_of(chip * ROWS, 16), ROWS)
        xr[0, at, :] = rows[:ROWS]
        xr[1, at, :] = rows[ROWS:]
        info = _pick_dot(pick, meta.astype(BF))
        shape = (2 * ROWS, META)
        expert = (2 * me + jnp.where(number(shape, 0) >= ROWS, 1, 0)).astype(F32)
        match = jnp.where((info == expert) & (number(shape, 1) < 8), 1.0, 0.0).astype(BF)
        k0, k1 = number((META, META), 0), number((META, META), 1)
        copies = ((k1 == k0 + 8) | (k1 == k0 + 16) | (k1 == k0 + 24)) & (k0 < 8)
        spread = jnp.dot(match, jnp.where(copies, 1.0, 0.0).astype(BF), preferred_element_type=F32)
        weight = jnp.sum(spread * info, axis=1, keepdims=True)
        wr[chip] = jnp.broadcast_to(weight, shape)

    def drive(gather, work, before=None):
        done, waiting, ready = {(0, 0)}, [], [(0, 0)]
        for n, (o1, o2) in enumerate(EVENTS):
            if before is not None:
                before(n)
            gather.event(o1, o2)
            for chip in waiting:
                work(*chip)
            waiting, ready = ready, []
            done.add((o1, o2))
            if (o2, o1) in done:
                ready = [(o1, o2)] if o1 == o2 else [(o1, o2), (o2, o1)]
        for chip in waiting + ready:
            work(*chip)

    def middle(n):
        if n == 9:
            gc.start()

    own_x.wait()
    drive(gx, rows_of, middle)
    outs = []

    def put(src, dst, sem):
        cp = pltpu.make_async_copy(src, dst, sem)
        cp.start()
        outs.append(cp)

    put(xr, xr_out, osem.at[0])
    put(back, back_out, osem.at[1])
    put(wr, wr_out, osem.at[2])

    def project(e, first, last):
        @pl.loop(first, last)
        def _(j):
            cols = pl.ds(pl.multiple_of(j * 256, 256), 256)
            gu[e, :, cols] = jnp.dot(xr[e], wgu[e, :, cols], preferred_element_type=F32)

    steps = 2 * hid // 256
    units = {2: (0, 0, 2), 4: (0, 2, steps), 6: (1, 0, 2), 8: (1, 2, steps)}

    def compute(n):
        if n in units:
            e, first, last = units[n]
            if first == 0:
                weights[2 * e].wait()
                weights[2 * e + 1].wait()
            project(e, first, last)
            if last == steps:
                put(gu.at[e], gu_out.at[e], osem.at[3 + e])

    own_c.wait()
    fetched = []

    def finish():
        i, chip, cp = fetched.pop(0)
        cp.wait()
        rows = _pick_dot(back[chip], cbuf[i % 3].reshape(2 * TOK, width))
        rows = (rows * wr[chip][:, 0:1]).astype(BF)
        at = pl.ds(pl.multiple_of(chip * ROWS, 16), ROWS)
        for e in range(2):
            cr[e, at, :] = rows[e * ROWS : (e + 1) * ROWS]
            put(cr.at[e, at], cr_out.at[e, at], rowsem.at[2 * i + e])

    count = [0]

    def cot_of(dx, dy):
        chip = gc.chip(dx, dy)
        i = count[0]
        count[0] += 1
        cp = pltpu.make_async_copy(call.at[pl.ds(2 * chip, 2)], cbuf.at[i % 3], csem.at[i % 3])
        cp.start()
        fetched.append((i, chip, cp))
        if len(fetched) > 2:
            finish()

    drive(gc, cot_of, compute)
    while fetched:
        finish()
    for cp in outs:
        cp.wait()
    for cp in sends:
        cp.wait_send()


def _front(xm, ct, gate_proj, up_proj):
    width, hid = ct.shape[1], gate_proj.shape[2]
    hbm = pl.BlockSpec(memory_space=pl.ANY)
    vmem = pl.BlockSpec(memory_space=pltpu.VMEM)
    rows = 32 * CAP
    return pl.pallas_call(
        _front_kernel,
        out_shape=(
            jax.ShapeDtypeStruct((16, 2 * TOK, META), BF),
            jax.ShapeDtypeStruct((2, rows, width), BF),
            jax.ShapeDtypeStruct((2, rows, width), BF),
            jax.ShapeDtypeStruct((16, 2 * ROWS, META), F32),
            jax.ShapeDtypeStruct((2, rows, 2 * hid), F32),
            jax.ShapeDtypeStruct((32, TOK, width), BF),
        ),
        in_specs=[vmem, vmem, hbm, hbm],
        out_specs=(hbm,) * 6,
        scratch_shapes=[
            pltpu.VMEM((32, TOK, width + META), BF),
            pltpu.VMEM((3, 2, TOK, width), BF),
            pltpu.VMEM((2, rows, width), BF),
            pltpu.VMEM((2, rows, width), BF),
            pltpu.VMEM((2, width, 2 * hid), BF),
            pltpu.VMEM((2, rows, 2 * hid), F32),
            pltpu.VMEM((16, 2 * TOK, META), BF),
            pltpu.VMEM((16, 2 * ROWS, META), F32),
            pltpu.SemaphoreType.DMA((144,)),
            pltpu.SemaphoreType.DMA((144,)),
            pltpu.SemaphoreType.DMA((2,)),
            pltpu.SemaphoreType.DMA((4,)),
            pltpu.SemaphoreType.DMA((3,)),
            pltpu.SemaphoreType.DMA((5,)),
            pltpu.SemaphoreType.DMA((32,)),
        ],
        compiler_params=pltpu.CompilerParams(
            collective_id=0, has_side_effects=True, vmem_limit_bytes=63 * 1024 * 1024
        ),
        cost_estimate=pl.CostEstimate(flops=10_000_000_000, bytes_accessed=300_000_000, transcendentals=0),
        name="plane_gather",
    )(xm, ct, gate_proj, up_proj)


def _add(dst, src, n):
    @pl.loop(0, n // 16)
    def _(i):
        rows = pl.ds(pl.multiple_of(i * 16, 16), 16)
        dst[rows, :] = (dst[rows, :].astype(F32) + src[rows, :].astype(F32)).astype(BF)


def _add3(dst, own, one, two, n):
    @pl.loop(0, n // 16)
    def _(i):
        rows = pl.ds(pl.multiple_of(i * 16, 16), 16)
        total = own[rows, :].astype(F32) + one[rows, :].astype(F32) + two[rows, :].astype(F32)
        dst[rows, :] = total.astype(dst.dtype)


OBS = OAS = (2, 1, 3, 0)
AHEAD = 4
LO, HI = pl.ds(0, SUB), pl.ds(SUB, SUB)


class _Reduce:
    def __init__(self, tag, bufs, aside, bsem, out, stage, ssem, rsem, sends, keys):
        self.tag, self.aside, self.bsem, self.out, self.stage = tag, aside, bsem, out, stage
        self.T, self.sb, self.ra, self.rb, self.r2a, self.r2b = bufs
        self.ssem, self.rsem, self.sends, self.keys = ssem, rsem, sends, keys
        self.z, self.x, self.y, self.c = _place()
        self.sib = (self.z, _at(self.x, self.y, 1 - self.c))
        self.width = self.T.shape[-1]
        self.order = [(h, ob, oa) for ob in OBS for oa in OAS for h in (0, 1)]
        self.loads, self.made, self.shared = {}, [], {}

    def remote(self, src, dst, to, *k):
        k = self.keys.setdefault((self.tag,) + k, len(self.keys))
        cp = pltpu.make_async_remote_copy(
            src_ref=src,
            dst_ref=dst,
            send_sem=self.ssem.at[len(self.keys) - 1],
            recv_sem=self.rsem.at[k],
            device_id=to,
            device_id_type=MESH,
        )
        cp.start()
        self.sends.append(cp)
        return cp

    def landed(self, dst, *k):
        pltpu.make_async_remote_copy(
            src_ref=dst,
            dst_ref=dst,
            send_sem=self.ssem.at[0],
            recv_sem=self.rsem.at[self.keys[(self.tag,) + k]],
            device_id=self.sib,
            device_id_type=MESH,
        ).wait_recv()

    def ax(self, h, o):
        return (self.z, _shift(1 - h, self.x, self.y, o, 0, self.c))

    def bx(self, h, o):
        return (self.z, _shift(h, self.x, self.y, o, 0, self.c))

    def make(self, dx, dy):
        if (dx, dy) in self.made:
            return
        chip = _at(self.x + dx, self.y + dy, 0) // 2
        stage = self.stage.at[len(self.made), :, pl.ds(0, self.width)]
        places = ((0, dx * 4 + dy), (1, dy * 4 + dx))
        self.spread(chip, 1 - self.c, [(stage.at[pl.ds(h * HALF, HALF)], h) for h in (0, 1)])
        self.shared[len(self.made)] = [
            self.remote(stage.at[pl.ds(h * HALF, HALF)], self.aside.at[h, k], self.sib, "s", h, k)
            for h, k in places
        ]
        self.spread(chip, self.c, [(self.T.at[h, k], h) for h, k in places])
        self.made.append((dx, dy))

    def fetch(self, i):
        h, ob, oa = self.order[i]
        view = self.aside.at[h, ob * 4 + oa]
        self.landed(view, "s", h, ob * 4 + oa)
        cp = pltpu.make_async_copy(view, self.sb.at[i % (AHEAD + 1)], self.bsem.at[i % (AHEAD + 1)])
        cp.start()
        self.loads[i] = cp

    def one(self, i):
        h, ob, oa = self.order[i]
        for n in range(AHEAD) if i == 0 else ():
            self.fetch(n)
        if i + AHEAD < len(self.order):
            self.fetch(i + AHEAD)
        self.loads[i].wait()
        t = self.T.at[h, ob * 4 + oa]
        _add(t, self.sb.at[i % (AHEAD + 1)], HALF)
        if oa == 2:
            self.remote(t.at[LO], self.ra.at[h, ob, 0], self.ax(h, 1), "ra", h, ob, 0)
            self.remote(t.at[HI], self.ra.at[h, ob, 1], self.ax(h, -1), "ra", h, ob, 1)
        elif oa == 1:
            self.remote(t.at[HI], self.rb.at[h, ob, 0, HI], self.ax(h, 1), "rd", h, ob, 0)
        elif oa == 3:
            self.remote(t.at[LO], self.rb.at[h, ob, 1, LO], self.ax(h, -1), "rd", h, ob, 1)

    def stage1(self, j):
        for i in range(j * 8, j * 8 + 8):
            for h, ob, oa in self.order[i : i + AHEAD + 4]:
                self.make(*((ob, oa) if h == 0 else (oa, ob)))
            self.one(i)

    def stage2(self, j):
        ob = OBS[j]
        for h in (0, 1):
            self.landed(self.ra.at[h, ob, 0], "ra", h, ob, 0)
            t = self.T.at[h, ob * 4 + 1]
            _add(t.at[LO], self.ra.at[h, ob, 0], SUB)
            self.remote(t.at[LO], self.rb.at[h, ob, 0, LO], self.ax(h, 1), "rs", h, ob, 0)
            self.landed(self.ra.at[h, ob, 1], "ra", h, ob, 1)
            t = self.T.at[h, ob * 4 + 3]
            _add(t.at[HI], self.ra.at[h, ob, 1], SUB)
            self.remote(t.at[HI], self.rb.at[h, ob, 1, HI], self.ax(h, -1), "rs", h, ob, 1)

    def stage3(self, j):
        ob = OBS[j]
        for h in (0, 1):
            self.landed(self.rb.at[h, ob, 0, HI], "rd", h, ob, 0)
            self.landed(self.rb.at[h, ob, 1, LO], "rd", h, ob, 1)
            self.landed(self.rb.at[h, ob, 0, LO], "rs", h, ob, 0)
            self.landed(self.rb.at[h, ob, 1, HI], "rs", h, ob, 1)
            t = self.T.at[h, ob * 4]
            _add3(t, t, self.rb.at[h, ob, 0], self.rb.at[h, ob, 1], HALF)
            if ob == 2:
                self.remote(t.at[LO], self.r2a.at[h, 0], self.bx(h, 1), "2a", h, 0)
                self.remote(t.at[HI], self.r2a.at[h, 1], self.bx(h, -1), "2a", h, 1)
            elif ob == 1:
                self.remote(t.at[HI], self.r2b.at[h, 0, HI], self.bx(h, 1), "2d", h, 0)
            elif ob == 3:
                self.remote(t.at[LO], self.r2b.at[h, 1, LO], self.bx(h, -1), "2d", h, 1)

    def stage4(self):
        for h in (0, 1):
            self.landed(self.r2a.at[h, 0], "2a", h, 0)
            t = self.T.at[h, 4]
            _add(t.at[LO], self.r2a.at[h, 0], SUB)
            self.remote(t.at[LO], self.r2b.at[h, 0, LO], self.bx(h, 1), "2s", h, 0)
            self.landed(self.r2a.at[h, 1], "2a", h, 1)
            t = self.T.at[h, 12]
            _add(t.at[HI], self.r2a.at[h, 1], SUB)
            self.remote(t.at[HI], self.r2b.at[h, 1, HI], self.bx(h, -1), "2s", h, 1)

    def stage5(self):
        for h in (0, 1):
            self.landed(self.r2b.at[h, 0, HI], "2d", h, 0)
            self.landed(self.r2b.at[h, 1, LO], "2d", h, 1)
            self.landed(self.r2b.at[h, 0, LO], "2s", h, 0)
            self.landed(self.r2b.at[h, 1, HI], "2s", h, 1)
            rows = self.out.at[pl.ds(h * HALF, HALF)]
            _add3(rows, self.T.at[h, 0], self.r2b.at[h, 0], self.r2b.at[h, 1], HALF)


def _reduce_kernel(
    back_in, y_in, r_in, dx_in, dg_in, du_in, gw, uw, outy, outd, asidey, asided, *rest
):
    bufy, bufd = rest[:6], rest[6:12]
    stage, rows, back, rr, dcat, wcat, ssem, rsem, bsem, lsem, wsem = rest[12:]
    z, x, y, c = _place()
    width, hid = y_in.shape[2], dg_in.shape[2]

    def load(src, dst, sem):
        cp = pltpu.make_async_copy(src, dst, sem)
        cp.start()
        return cp

    first = [load(back_in, back, lsem.at[0]), load(y_in, rows, lsem.at[1]), load(r_in, rr, lsem.at[2])]
    later = [load(ref.at[1], dcat.at[:, pl.ds(k * hid, hid)], lsem.at[3 + k]) for k, ref in enumerate((dg_in, du_in))]

    later += [load(ref.at[1], wcat.at[:, pl.ds(k * hid, hid)], wsem.at[k]) for k, ref in enumerate((gw, uw))]
    _greet(
        [
            (z, _at(x + 1, y, c)), (z, _at(x - 1, y, c)), (z, _at(x, y + 1, c)), (z, _at(x, y - 1, c)),
            (z, _at(x, y, 1 - c)),
        ]
    )
    sends, keys = [], {}
    ry = _Reduce("y", bufy, asidey, bsem.at[0], outy, stage, ssem, rsem, sends, keys)
    rd = _Reduce("d", bufd, asided, bsem.at[1], outd, stage, ssem, rsem, sends, keys)

    def spread(chip, core, places, extra):
        sel = back[chip, pl.ds(pl.multiple_of(core * TOK, TOK), TOK), :][:, : 2 * ROWS]
        at = pl.ds(pl.multiple_of(chip * ROWS, 16), ROWS)

        @pl.loop(0, 4)
        def _(j):
            cols = pl.ds(pl.multiple_of(j * 512, 512), 512)
            both = jnp.concatenate([rows[0, at, cols], rows[1, at, cols]], 0)
            made = jnp.dot(sel, both, preferred_element_type=F32).astype(BF)
            for ref, h in places:
                ref[:, cols] = made[h * HALF : (h + 1) * HALF]

        if extra:
            made = jnp.dot(sel, rr[chip], preferred_element_type=F32).astype(BF)
            for ref, h in places:
                ref[:, pl.ds(width, META)] = made[h * HALF : (h + 1) * HALF]

    def spread_y(chip, core, places):
        spread(chip, core, places, True)

    ry.spread = spread_y

    def spread_d(chip, core, places):
        n = len(rd.made)
        for cp in ry.shared.pop(n, ()):
            cp.wait_send()
            sends[:] = [s for s in sends if s is not cp]
        spread(chip, core, places, False)

    rd.spread = spread_d

    def product(j0, j1):
        @pl.loop(j0, j1)
        def _(j):
            at = pl.ds(pl.multiple_of(j * 256, 256), 256)
            dims = (((1,), (1,)), ((), ()))
            made = lax.dot_general(dcat[...], wcat[at, :], dims, preferred_element_type=F32)
            rows[1, :, at] = made.astype(BF)

    for cp in first:
        cp.wait()
    n = width // 256
    ry.stage1(0)
    ry.stage1(1)
    for h, ob, oa in ry.order:
        ry.make(*((ob, oa) if h == 0 else (oa, ob)))
    for cp in later:
        cp.wait()
    other = load(dx_in, rows.at[0], lsem.at[5])
    product(0, n // 2)
    ry.stage1(2)
    ry.stage2(0)
    product(n // 2, n)
    ry.stage1(3)
    ry.stage2(1)
    other.wait()
    rd.stage1(0)
    ry.stage2(2)
    ry.stage3(0)
    ry.stage2(3)
    rd.stage1(1)
    ry.stage3(1)
    rd.stage2(0)
    rd.stage1(2)
    ry.stage3(2)
    ry.stage4()
    rd.stage2(1)
    rd.stage1(3)
    ry.stage3(3)
    ry.stage5()
    rd.stage2(2)
    rd.stage3(0)
    rd.stage2(3)
    rd.stage3(1)
    rd.stage3(2)
    rd.stage4()
    rd.stage3(3)
    rd.stage5()
    for cp in sends:
        cp.wait_send()


def _reduce(back, yrows, rrows, dxrows, d_gate, d_up, gate_proj, up_proj):
    width, hid = yrows.shape[2], d_gate.shape[2]
    hbm = pl.BlockSpec(memory_space=pl.ANY)
    vmem = pl.BlockSpec(memory_space=pltpu.VMEM)

    def buffers(w):
        return [
            pltpu.VMEM((2, 16, HALF, w), BF),
            pltpu.VMEM((AHEAD + 1, HALF, w), BF),
            pltpu.VMEM((2, 4, 2, SUB, w), BF),
            pltpu.VMEM((2, 4, 2, HALF, w), BF),
            pltpu.VMEM((2, 2, SUB, w), BF),
            pltpu.VMEM((2, 2, HALF, w), BF),
        ]

    wide = width + META
    return pl.pallas_call(
        _reduce_kernel,
        out_shape=(
            jax.ShapeDtypeStruct((TOK, wide), BF),
            jax.ShapeDtypeStruct((TOK, width), BF),
            jax.ShapeDtypeStruct((2, 16, HALF, wide), BF),
            jax.ShapeDtypeStruct((2, 16, HALF, width), BF),
        ),
        in_specs=[hbm] * 8,
        out_specs=(vmem, vmem, hbm, hbm),
        scratch_shapes=buffers(wide)
        + buffers(width)
        + [
            pltpu.VMEM((16, TOK, wide), BF),
            pltpu.VMEM(yrows.shape, BF),
            pltpu.VMEM(back.shape, BF),
            pltpu.VMEM(rrows.shape, BF),
            pltpu.VMEM((32 * CAP, 2 * hid), BF),
            pltpu.VMEM((width, 2 * hid), BF),
            pltpu.SemaphoreType.DMA((184,)),
            pltpu.SemaphoreType.DMA((184,)),
            pltpu.SemaphoreType.DMA((2, AHEAD + 1)),
            pltpu.SemaphoreType.DMA((6,)),
            pltpu.SemaphoreType.DMA((2,)),
        ],
        compiler_params=pltpu.CompilerParams(
            collective_id=1, has_side_effects=True, vmem_limit_bytes=67_000_000
        ),
        cost_estimate=pl.CostEstimate(flops=12_000_000_000, bytes_accessed=300_000_000, transcendentals=0),
        name="plane_reduce",
    )(back, yrows, rrows, dxrows, d_gate, d_up, gate_proj, up_proj)


def _grads_kernel(q_ref, x_ref, c_ref, dg_ref, du_ref, h_ref, *outs):
    dims = (((0,), (0,)), ((), ()))
    n = outs[0].shape[2]
    for o in range(len(outs) // 2):

        @pl.when(pl.program_id(0) == o)
        def _():
            for k, (rows, cots) in enumerate(((x_ref, dg_ref), (x_ref, du_ref), (c_ref, h_ref))):
                g = lax.dot_general(rows[0], cots[0], dims, preferred_element_type=F32).astype(BF)
                outs[2 * o][k, 0] = g[:n]
                outs[2 * o + 1][k, 0] = g[n:]


def _grads(quarters, xr, cr, d_gate, d_up, hidden):
    rows, width = xr.shape[1:]
    hid = hidden.shape[2]
    count = quarters.shape[0]
    wide = pl.BlockSpec((1, rows, width // 4), lambda o, e, q: (e, 0, q[o]))
    thin = pl.BlockSpec((1, rows, hid), lambda o, e, q: (e, 0, 0))
    half = jax.ShapeDtypeStruct((3, 2, width // 8, hid), BF)

    def spec(n):
        return pl.BlockSpec(
            (3, 1, width // 8, hid),
            lambda o, e, q: (0, jnp.where(o == n, e, jnp.where(o < n, 0, 1)), 0, 0),
        )

    return pl.pallas_call(
        _grads_kernel,
        grid_spec=pltpu.PrefetchScalarGridSpec(
            num_scalar_prefetch=1,
            grid=(count, 2),
            in_specs=[wide, wide, thin, thin, thin],
            out_specs=tuple(spec(n) for n in range(count) for _ in range(2)),
        ),
        out_shape=(half,) * (2 * count),
        compiler_params=pltpu.CompilerParams(vmem_limit_bytes=40 * 1024 * 1024),
        cost_estimate=pl.CostEstimate(
            flops=12 * count * rows * (width // 4) * hid, bytes_accessed=14_000_000 * count, transcendentals=0
        ),
        name="grad_quarter",
    )(quarters, xr, cr, d_gate, d_up, hidden)


def _bits(v):
    return lax.reduce_precision(v, 8, 7)


def layer(tokens, routes, route_weights, cotangent, gate_proj, up_proj, down_proj):
    width = tokens.shape[1]
    hid = gate_proj.shape[2]
    me = lax.axis_index("expert")
    w_hi = _bits(route_weights)
    w_mid = _bits(route_weights - w_hi)
    w_lo = route_weights - w_hi - w_mid
    meta = jnp.concatenate(
        [routes.astype(F32), w_hi, w_mid, w_lo, jnp.zeros((TOK, META - 32), F32)], 1
    ).astype(BF)
    mine = 2 * me + jnp.arange(2, dtype=jnp.int32)
    back, xr, cr, wr, gu, _ = _front(jnp.concatenate([tokens, meta], 1), cotangent, gate_proj, up_proj)
    we = wr[:, :, 0].reshape(16, 2, ROWS).transpose(1, 0, 2).reshape(2, 32 * CAP, 1)
    gate_pre, up_pre = gu[:, :, :hid], gu[:, :, hid:]
    sig = jax.nn.sigmoid(gate_pre)
    swish = gate_pre * sig
    d_swish = sig * (1.0 + gate_pre * (1.0 - sig))
    hidden = (swish * up_pre).astype(BF)
    d_hidden = jnp.einsum("erd,ehd->erh", cr, down_proj, preferred_element_type=F32)
    d_gate = (d_hidden * up_pre * d_swish).astype(BF)
    d_up = (d_hidden * swish).astype(BF)
    rw = jnp.sum(d_hidden * hidden.astype(F32), axis=2, keepdims=True) / jnp.where(we > 0, we, 1.0)

    z = lax.axis_index("dp")
    up = [(i, (i + 1) % 4) for i in range(4)]
    down = [(i, (i + 3) % 4) for i in range(4)]

    def quarters(offsets, after=None):
        which = (z + jnp.array(offsets, jnp.int32)) % 4
        if after is not None:
            which, _ = lax.optimization_barrier((which, after))
        return _grads(which, xr, cr, d_gate, d_up, hidden)

    def along(v, way):
        return lax.ppermute(v, "dp", way)

    lo2, hi2 = quarters((2,))
    far_up, far_down = along(lo2, up), along(hi2, down)
    lo1, hi1, lo3, hi3, lo0, hi0 = quarters((1, 3, 0), lo2)
    near_up, near_down = along(hi1, up), along(lo3, down)
    yrows = (jnp.einsum("erh,ehd->erd", hidden, down_proj, preferred_element_type=F32) * we).astype(BF)
    lane = jnp.arange(META, dtype=jnp.int32)
    r_hi = _bits(rw)
    r_lo = rw - r_hi
    spot = lane[None, None, :] - mine[:, None, None]
    rrows = jnp.where(spot == 0, r_hi, 0.0) + jnp.where(spot == 64, r_lo, 0.0)
    rrows = rrows.reshape(2, 16, ROWS, META).transpose(1, 0, 2, 3).reshape(16, 2 * ROWS, META).astype(BF)

    def plus(one, two):
        return (one.astype(F32) + two.astype(F32)).astype(BF)

    dxrows = (
        jnp.einsum("rh,dh->rd", d_gate[0], gate_proj[0], preferred_element_type=F32)
        + jnp.einsum("rh,dh->rd", d_up[0], up_proj[0], preferred_element_type=F32)
    ).astype(BF)
    lo1, hi3, lo0, hi0, dxrows = lax.optimization_barrier((lo1, hi3, lo0, hi0, dxrows))
    sum_up = along(plus(lo1, far_up), up)
    sum_down = along(plus(hi3, far_down), down)
    out, dx, _, _ = _reduce(back, yrows, rrows, dxrows, d_gate, d_up, gate_proj, up_proj)

    def total(one, two, three):
        return one.astype(F32) + two.astype(F32) + three.astype(F32)

    shares = jnp.concatenate([total(lo0, sum_up, near_down), total(hi0, near_up, sum_down)], 2)
    table = out[:, width : width + 64].astype(F32) + out[:, width + 64 :].astype(F32)
    onehot = routes[:, :, None] == jnp.arange(64, dtype=jnp.int32)[None, None, :]
    weight_grad = jnp.sum(jnp.where(onehot, table[:, None, :], 0.0), axis=2)

    def final(g):
        return jnp.transpose(g, (1, 0, 2))

    return (out[:, :width], dx, weight_grad, final(shares[0]), final(shares[1]), final(shares[2]))


def solution(mesh):
    rows = P(("dp", "expert"), None)
    experts = P("expert", None, None)
    grads = P("dp", "expert", None)
    return jax.shard_map(
        layer,
        mesh=mesh,
        in_specs=(rows, rows, rows, rows, experts, experts, experts),
        out_specs=(rows, rows, rows, grads, grads, grads),
        check_vma=False,
    )
```
